32 devices in a mesh: dp: 8 (over z, y), tensor: 4 (over x, core).
Axes of the slice: x: 2, y: 2, z: 4, core: 2. Of those that a mesh axis runs over, the one named last changes fastest.
Arguments:
- tokens: bfloat16 [16384, 768], P(('dp', 'tensor'))
- first_values: bfloat16 [16384, 384], P(('dp', 'tensor')), may hold values from -6 to 6
- pieces: int32 [16384], P('dp'), may hold values from 0 to 64, as said below
- lengths: int32 [8], P('dp'), may hold values from 256 to 2048, as said below
- w_query: bfloat16 [768, 768], P('dp', 'tensor'), may hold values from -0.21875 to 0.21875
- w_key: bfloat16 [768, 768], P('dp', 'tensor'), may hold values from -0.21875 to 0.21875
- w_value: bfloat16 [768, 384], P('dp'), may hold values from -0.21875 to 0.21875
- w_out: bfloat16 [768, 768], P('tensor', 'dp'), may hold values from -2.5 to 2.5
- w_up: bfloat16 [768, 3072], P('dp', 'tensor'), may hold values from -0.21875 to 0.21875
- w_down: bfloat16 [3072, 768], P('tensor', 'dp'), may hold values from -0.15625 to 0.15625
- gain_attn: float32 [768], replicated, may hold values from 0.1 to 1.9
- gain_mlp: float32 [768], replicated, may hold values from 0.1 to 1.9
- cotangent: bfloat16 [16384, 768], P(('dp', 'tensor')), may hold values from -6 to 6
Outputs:
- output: bfloat16 [16384, 768], P(('dp', 'tensor'))
- d_tokens: float32 [16384, 768], P(('dp', 'tensor'))
- d_first_values: float32 [16384, 384], P(('dp', 'tensor'))
- d_w_query: float32 [768, 768], P('dp', 'tensor')
- d_w_key: float32 [768, 768], P('dp', 'tensor')
- d_w_value: float32 [768, 384], P('dp')
- d_w_out: float32 [768, 768], P('tensor', 'dp')
- d_w_up: float32 [768, 3072], P('dp', 'tensor')
- d_w_down: float32 [3072, 768], P('tensor', 'dp')
- d_gain_attn: float32 [768], replicated
- d_gain_mlp: float32 [768], replicated
- rms: float32 [3], replicated
The draws below stay inside these ranges and needn't reach their ends.
Inputs may be any that keep to these rules, and one draw needn't show every extreme that they name: `pieces`: each aligned block of 256 tokens carries one number: 0 for text, or a positive number that no other block carries, for a picture piece. `lengths`: 2048 is reached in every draw.
All inputs are finite; a program needn't handle non-finite values.
Results may differ from the reference program's by a relative error of at most 0.018.
Values may be sent and summed in bfloat16 or wider, within the bound.
No kernel may reach another device: no remote copies, remote signals or barrier semaphores. Data moves between devices by JAX's collectives and lax.ppermute only.
A program may use at most 256 MiB of HBM per device.

```python
import math
import jax
import jax.numpy as jnp
from jax import lax

D = 768
HEADS = 12
HD = 64
FF = 3072
PIECE = 256
SEQ = 2048
VW = 384
NSEQ = 8
TOKENS = 16384


def draw_tokens(key, part):
    row_frac = jnp.arange(TOKENS, dtype=jnp.float32) / TOKENS
    row_scale = 0.5 + 1.5 * row_frac
    base = jax.random.normal(key, (TOKENS, D), jnp.float32)
    return (base * row_scale[:, None]).astype(jnp.bfloat16)


def draw_pieces(key, part):
    block_count = TOKENS // PIECE
    coins = jax.random.randint(key, (block_count,), 0, 3)
    block_ids = jnp.arange(block_count, dtype=jnp.int32)
    chosen = (coins == 0) | (block_ids == block_count - 1)
    numbers = jnp.where(chosen, block_ids + 1, 0).astype(jnp.int32)
    return jnp.repeat(numbers, PIECE).astype(jnp.int32)


def draw_lengths(key, part):
    drawn = jax.random.randint(key, (NSEQ,), SEQ // 8, SEQ + 1)
    return drawn.at[0].set(SEQ).astype(jnp.int32)


def block_levels(own_key, extent, split, low, top_value):
    level, own = 1.0, jax.random.fold_in(own_key, 6)
    for dim, blocks in split:
        heights = jnp.exp(jax.random.uniform(jax.random.fold_in(own, dim), (blocks,), jnp.float32, low / len(split), top_value / len(split)))
        level = level * jnp.repeat(heights, extent[dim] // blocks).reshape([-1 if axis == dim else 1 for axis in range(len(extent))])
    return level


def gaussian(rng, dims, deviation, most, cuts=(), kind=jnp.bfloat16):
    result = deviation * jax.random.normal(rng, dims, jnp.float32)
    if cuts:
        result = result * block_levels(rng, dims, cuts, -0.22, 0.18)
    return jnp.clip(result, -most, most).astype(kind)


def setup_inputs(seed: int = 0) -> dict:
    arg_keys = jax.random.split(jax.random.key(seed), 14)
    tokens = draw_tokens(jax.random.fold_in(arg_keys[13], 71), 0)
    first_values = gaussian(arg_keys[1], (TOKENS, VW), 1.0, 6.0, ((0, 32),))
    pieces = draw_pieces(jax.random.fold_in(arg_keys[13], 71), 0)
    lengths = draw_lengths(jax.random.fold_in(arg_keys[13], 71), 0)
    w_query = gaussian(arg_keys[4], (D, D), D ** -0.5, 0.21875, ((0, 8), (1, 4)))
    w_key = gaussian(arg_keys[5], (D, D), D ** -0.5, 0.21875, ((0, 8), (1, 4)))
    w_value = gaussian(arg_keys[6], (D, VW), D ** -0.5, 0.21875, ((0, 8),))
    w_out = gaussian(arg_keys[7], (D, D), (D // 128) ** -0.5, 2.5, ((0, 4), (1, 8)))
    w_up = gaussian(arg_keys[8], (D, FF), D ** -0.5, 0.21875, ((0, 8), (1, 4)))
    w_down = gaussian(arg_keys[9], (FF, D), (FF // 2) ** -0.5, 0.15625, ((0, 4), (1, 8)))
    gain_attn = jnp.clip(1.0 + 0.18 * jax.random.normal(arg_keys[10], (D,), jnp.float32), 0.1, 1.9)
    gain_mlp = jnp.clip(1.0 + 0.18 * jax.random.normal(arg_keys[11], (D,), jnp.float32), 0.1, 1.9)
    cotangent = gaussian(arg_keys[12], (TOKENS, D), 1.0, 6.0, ((0, 32),))
    return dict(tokens=tokens, first_values=first_values, pieces=pieces, lengths=lengths, w_query=w_query, w_key=w_key, w_value=w_value, w_out=w_out, w_up=w_up, w_down=w_down, gain_attn=gain_attn, gain_mlp=gain_mlp, cotangent=cotangent)


@jax.custom_vjp
def low(v):
    return lax.optimization_barrier(v.astype(jnp.bfloat16)).astype(jnp.float32)

@jax.custom_vjp
def low_back(v):
    return v

def low_keep(v):
    return (low(v), None)

def low_pass(kept, grad):
    return (grad,)

def back_keep(v):
    return (v, None)

def back_low(kept, grad):
    return (low(grad),)
low.defvjp(low_keep, low_pass)
low_back.defvjp(back_keep, back_low)
EPS = 1e-05
NEG = -1e+30

def matmul(first_op, second_op):
    return jnp.dot(first_op, second_op, precision=lax.Precision.HIGHEST, preferred_element_type=jnp.float32)

def layer_norm(resid, norm_gain):
    centred = resid - lax.optimization_barrier(jnp.mean(resid, axis=-1, keepdims=True))
    return centred * lax.rsqrt(lax.optimization_barrier(jnp.mean(centred * centred, axis=-1, keepdims=True)) + EPS) * norm_gain

def make_forward(allowed):
    scale_factor = 1.0 / math.sqrt(HD)

    def attend(head_parts):
        q_head, k_head, v_head = head_parts
        raw_scores = low_back(matmul(q_head, k_head.T) * scale_factor)
        scores = jnp.where(allowed, raw_scores, NEG)
        row_max = lax.optimization_barrier(jnp.max(scores, axis=-1, keepdims=True))
        exp_scores = jnp.exp(scores - row_max)
        attn_probs = exp_scores / lax.optimization_barrier(jnp.sum(exp_scores, axis=-1, keepdims=True))
        return matmul(low(attn_probs), v_head)
    attend_saved = jax.checkpoint(attend)

    def split_heads(whole):
        return whole.reshape(SEQ, HEADS, HD).transpose(1, 0, 2)

    def forward(params, x_rows, first_rows):
        query_w, key_w, value_w, out_w, up_w, down_w, gain_one, gain_two = params
        attn_input = low(layer_norm(x_rows, gain_one))
        queries = low(low_back(matmul(attn_input, query_w)))
        key_rows = low(low_back(matmul(attn_input, key_w)))
        fresh = low(low_back(matmul(attn_input, value_w)))
        value_rows = jnp.concatenate([fresh, first_rows], axis=1)
        heads_out = lax.map(attend_saved, (split_heads(queries), split_heads(key_rows), split_heads(value_rows)))
        heads_out = heads_out.transpose(1, 0, 2).reshape(SEQ, D)
        heads_out = low(low_back(heads_out))
        attn_out = low_back(matmul(heads_out, out_w))
        resid_mid = x_rows + attn_out
        mlp_input = low(layer_norm(resid_mid, gain_two))
        up_pre = low_back(matmul(mlp_input, up_w))
        hidden = low(jax.nn.gelu(up_pre, approximate=True))
        mlp_out = low_back(matmul(hidden, down_w))
        return (resid_mid + mlp_out, (attn_out, mlp_out))
    return forward

def reference(tokens, first_values, pieces, lengths, w_query, w_key, w_value, w_out, w_up, w_down, gain_attn, gain_mlp, cotangent):
    params = tuple((weight_arr.astype(jnp.float32) for weight_arr in (w_query, w_key, w_value, w_out, w_up, w_down, gain_attn, gain_mlp)))
    x_all = tokens.astype(jnp.float32).reshape(NSEQ, SEQ, D)
    first_all = first_values.astype(jnp.float32).reshape(NSEQ, SEQ, VW)
    piece_all = pieces.reshape(NSEQ, SEQ)
    cot_all = cotangent.astype(jnp.float32).reshape(NSEQ, SEQ, D)
    positions = jnp.arange(SEQ, dtype=jnp.int32)

    def step(carry, item):
        grad_acc, square_acc = carry
        x_rows, first_rows, piece_row, seq_length, cot_rows = item
        same_piece = (piece_row[:, None] == piece_row[None, :]) & (piece_row[:, None] > 0)
        causal = positions[None, :] <= positions[:, None]
        allowed = (positions[None, :] < seq_length) & (causal | same_piece)
        valid = (positions < seq_length).astype(jnp.float32)[:, None]
        forward = make_forward(allowed)
        final, pull, aux = jax.vjp(forward, params, x_rows, first_rows, has_aux=True)
        attn_out, mlp_out = aux
        param_grads, x_grad, first_grad = pull(cot_rows)
        squares = jnp.stack([jnp.sum(valid * final * final), jnp.sum(valid * attn_out * attn_out), jnp.sum(valid * mlp_out * mlp_out)])
        new_carry = (jax.tree.map(jnp.add, grad_acc, param_grads), square_acc + squares)
        return (new_carry, (final.astype(jnp.bfloat16), x_grad, first_grad))
    init = (jax.tree.map(jnp.zeros_like, params), jnp.zeros((3,), jnp.float32))
    (grads, squares), (outs, x_grads, first_grads) = lax.scan(step, init, (x_all, first_all, piece_all, lengths, cot_all))
    count = jnp.sum(lengths.astype(jnp.float32))
    rms = jnp.sqrt(squares / (count * D))
    return (outs.reshape(TOKENS, D), x_grads.reshape(TOKENS, D), first_grads.reshape(TOKENS, VW), grads[0], grads[1], grads[2], grads[3], grads[4], grads[5], grads[6], grads[7], rms)
```

```python
import math

import jax
import jax.numpy as jnp
from jax import lax
from jax.sharding import PartitionSpec as P

HD = 64


EPS = 1e-05
NEG = -1e30


def matmul(first_op, second_op):
    return jnp.dot(first_op, second_op, preferred_element_type=jnp.float32)


def matmul_tn(first_op, second_op):
    return lax.dot_general(
        first_op, second_op, (((0,), (0,)), ((), ())), preferred_element_type=jnp.float32
    )


def matmul_nt(first_op, second_op):
    return lax.dot_general(
        first_op, second_op, (((1,), (1,)), ((), ())), preferred_element_type=jnp.float32
    )


def norm_forward(resid, norm_gain):
    centred = resid - jnp.mean(resid, axis=-1, keepdims=True)
    inv_std = lax.rsqrt(jnp.mean(centred * centred, axis=-1, keepdims=True) + EPS)
    normed = centred * inv_std
    return (normed * norm_gain, normed, inv_std)


def norm_backward(upstream, norm_gain, normed, inv_std):
    scaled = upstream * norm_gain
    inner = (
        scaled
        - jnp.mean(scaled, axis=-1, keepdims=True)
        - normed * jnp.mean(scaled * normed, axis=-1, keepdims=True)
    )
    return (inner * inv_std, jnp.sum(upstream * normed, axis=0))


def visible_mask(pieces, valid_len, q_start, q_count, k_count):
    q_pos = q_start + lax.iota(jnp.int32, q_count)
    k_pos = lax.iota(jnp.int32, k_count)
    q_piece = pieces[q_start : q_start + q_count]
    k_piece = pieces[:k_count]
    same_piece = (q_piece[:, None] == k_piece[None, :]) & (q_piece[:, None] > 0)
    causal = k_pos[None, :] <= q_pos[:, None]
    return (k_pos[None, :] < valid_len) & (causal | same_piece)


def attend_forward(queries, key_rows, value_rows, pieces, valid_len):
    seq_len, head_cols = queries.shape
    local_heads = head_cols // HD
    scale_factor = 1.0 / math.sqrt(HD)
    block_rows = min(512, seq_len // 2)
    q_split = queries.reshape(seq_len, local_heads, HD)
    k_split = key_rows.reshape(seq_len, local_heads, HD)
    v_split = value_rows.reshape(seq_len, local_heads, HD)
    outputs = []
    log_sums = []
    for block_idx in range(seq_len // block_rows):
        q_start = block_idx * block_rows
        q_stop = q_start + block_rows
        raw_scores = (
            jnp.einsum(
                "qhd,khd->hqk",
                q_split[q_start:q_stop],
                k_split[:q_stop],
                preferred_element_type=jnp.float32,
            )
            * scale_factor
        )
        scores = jnp.where(
            visible_mask(pieces, valid_len, q_start, block_rows, q_stop)[None], raw_scores, NEG
        )
        row_max = jnp.max(scores, axis=-1, keepdims=True)
        exp_scores = jnp.exp(scores - row_max)
        row_total = jnp.sum(exp_scores, axis=-1, keepdims=True)
        attn_probs = (exp_scores / row_total).astype(jnp.bfloat16)
        head_out = jnp.einsum(
            "hqk,khd->qhd", attn_probs, v_split[:q_stop], preferred_element_type=jnp.float32
        )
        outputs.append(head_out.reshape(block_rows, head_cols).astype(jnp.bfloat16))
        log_sums.append(row_max + jnp.log(row_total))
    return (jnp.concatenate(outputs, axis=0), log_sums)


def attend_backward(queries, key_rows, value_rows, grad_heads, log_sums, pieces, valid_len):
    seq_len, head_cols = queries.shape
    local_heads = head_cols // HD
    scale_factor = 1.0 / math.sqrt(HD)
    block_rows = min(512, seq_len // 2)
    q_split = queries.reshape(seq_len, local_heads, HD)
    k_split = key_rows.reshape(seq_len, local_heads, HD)
    v_split = value_rows.reshape(seq_len, local_heads, HD)
    g_split = grad_heads.reshape(seq_len, local_heads, HD)
    grad_keys = jnp.zeros((seq_len, local_heads, HD), jnp.float32)
    grad_vals = jnp.zeros((seq_len, local_heads, HD), jnp.float32)
    grad_q_blocks = []
    for block_idx in range(seq_len // block_rows):
        q_start = block_idx * block_rows
        q_stop = q_start + block_rows
        q_block = q_split[q_start:q_stop]
        g_block = g_split[q_start:q_stop]
        raw_scores = (
            jnp.einsum(
                "qhd,khd->hqk", q_block, k_split[:q_stop], preferred_element_type=jnp.float32
            )
            * scale_factor
        )
        scores = jnp.where(
            visible_mask(pieces, valid_len, q_start, block_rows, q_stop)[None], raw_scores, NEG
        )
        attn_probs = jnp.exp(scores - log_sums[block_idx])
        low_probs = attn_probs.astype(jnp.bfloat16)
        grad_vals = grad_vals.at[:q_stop].add(
            jnp.einsum("hqk,qhd->khd", low_probs, g_block, preferred_element_type=jnp.float32)
        )
        grad_probs = jnp.einsum(
            "qhd,khd->hqk", g_block, v_split[:q_stop], preferred_element_type=jnp.float32
        )
        inner_sum = jnp.sum(attn_probs * grad_probs, axis=-1, keepdims=True)
        grad_scores = (attn_probs * (grad_probs - inner_sum)).astype(jnp.bfloat16)
        grad_q_blocks.append(
            jnp.einsum(
                "hqk,khd->qhd", grad_scores, k_split[:q_stop], preferred_element_type=jnp.float32
            )
            * scale_factor
        )
        grad_keys = grad_keys.at[:q_stop].add(
            jnp.einsum("hqk,qhd->khd", grad_scores, q_block, preferred_element_type=jnp.float32)
            * scale_factor
        )
    grad_q = jnp.concatenate(grad_q_blocks, axis=0).reshape(seq_len, head_cols)
    return (grad_q, grad_keys.reshape(seq_len, head_cols), grad_vals.reshape(seq_len, head_cols))


def gelu_tanh(pre_act):
    return jax.nn.gelu(pre_act, approximate=True)


X_SWAP = [(0, 2), (1, 3), (2, 0), (3, 1)]
CORE_SWAP = [(0, 1), (1, 0), (2, 3), (3, 2)]


def swap_x(v):
    return lax.ppermute(v, "tensor", X_SWAP)


def swap_core(v):
    return lax.ppermute(v, "tensor", CORE_SWAP)


def gather_rel(own):
    from_core = swap_core(own)
    from_x = swap_x(own)
    from_diag = swap_core(from_x)
    return jnp.concatenate([own, from_x, from_core, from_diag], axis=0)


def scatter_rel(parts):
    low = parts.astype(jnp.bfloat16)
    from_core = swap_core(low[2:4]).astype(jnp.float32)
    pair = parts[0:2] + from_core
    from_x = swap_x(pair[1].astype(jnp.bfloat16)).astype(jnp.float32)
    return pair[0] + from_x


def exchange_rel(blocks):
    from_x = swap_x(blocks[jnp.array([1, 3])])
    to_core = jnp.stack([blocks[2], from_x[1]])
    from_core = swap_core(to_core)
    return jnp.stack([blocks[0], from_x[0], from_core[0], from_core[1]])


def body(
    tokens,
    first_values,
    pieces,
    lengths,
    w_query,
    w_key,
    w_value,
    w_out,
    w_up,
    w_down,
    gain_attn,
    gain_mlp,
    cotangent,
):
    dp_size = lax.axis_size("dp")
    rank = lax.axis_index("tensor")
    core = rank % 2
    rows, model_dim = tokens.shape
    seq_len = rows * 4
    cols = w_query.shape[1]
    shard = w_query.shape[0]
    hidden_cols = w_up.shape[1]
    valid_len = lengths[0]
    positions = rank * rows + lax.iota(jnp.int32, rows)
    valid = (positions < valid_len).astype(jnp.float32)[:, None]
    rel_of_abs = jnp.array([0, 2, 1, 3])[jnp.arange(4) ^ rank]
    abs_of_rel = jnp.array([0, 2, 1, 3]) ^ rank

    def to_abs(v):
        return v.reshape(4, rows, -1)[rel_of_abs].reshape(seq_len, -1)

    def to_rel(v):
        return v.reshape(4, rows, -1)[abs_of_rel]

    value_cols = lax.dynamic_slice_in_dim(w_value, core * cols, cols, 1)
    early = jnp.concatenate([w_query, w_key, value_cols], axis=1)
    late = jnp.concatenate([w_up, w_down.T, w_out.T], axis=1)
    late_all = lax.all_gather(late, "dp", axis=0, tiled=True)
    early_all = lax.all_to_all(
        jnp.broadcast_to(early[None], (dp_size,) + early.shape), "dp", 0, 0
    ).reshape(model_dim, 3 * cols)

    tokens_wide = tokens.astype(jnp.float32)
    norm_one, normed_one, inv_one = norm_forward(tokens_wide, gain_attn)
    attn_input = norm_one.astype(jnp.bfloat16)
    input_rel = gather_rel(attn_input)
    first_x = lax.ppermute(first_values, "tensor", [(0, 2), (1, 3)])
    first_two = jnp.stack([first_values, first_x])
    first_mine = lax.dynamic_slice_in_dim(first_two, core * cols, cols, 2)
    first_other = lax.dynamic_slice_in_dim(first_two, (1 - core) * cols, cols, 2)
    first_rel = jnp.concatenate([first_mine, swap_core(first_other)], axis=0)
    cot_rel = gather_rel(cotangent)

    qkv = matmul(input_rel, early_all).astype(jnp.bfloat16)
    value_rel = jnp.where(rank < 2, qkv[:, 2 * cols :], first_rel.reshape(seq_len, cols))
    queries = to_abs(qkv[:, :cols])
    key_rows = to_abs(qkv[:, cols : 2 * cols])
    value_rows = to_abs(value_rel)
    heads_abs, log_sums = attend_forward(queries, key_rows, value_rows, pieces, valid_len)
    heads_mine = exchange_rel(to_rel(heads_abs))
    heads_cat = jnp.concatenate([heads_mine[i] for i in range(4)], axis=1)

    out_own = late_all[:, 2 * hidden_cols :]
    out_x = swap_x(out_own)
    out_pair = jnp.concatenate([out_own, out_x], axis=1)
    out_all = jnp.concatenate([out_pair, swap_core(out_pair)], axis=1)
    attn_out = matmul_nt(heads_cat, out_all)
    resid_mid = tokens_wide + attn_out
    norm_two, normed_two, inv_two = norm_forward(resid_mid, gain_mlp)
    mlp_input = norm_two.astype(jnp.bfloat16)
    mlp_rel = gather_rel(mlp_input)
    up_w = late_all[:, :hidden_cols]
    down_t = late_all[:, hidden_cols : 2 * hidden_cols]
    up_pre = matmul(mlp_rel, up_w)
    hidden_act, gelu_pull = jax.vjp(gelu_tanh, up_pre)
    hidden = hidden_act.astype(jnp.bfloat16)
    grad_hidden = matmul(cot_rel, down_t)
    grad_up_pre = gelu_pull(grad_hidden)[0].astype(jnp.bfloat16)
    grad_mlp_input = scatter_rel(matmul_nt(grad_up_pre, up_w).reshape(4, rows, model_dim))
    mlp_out = scatter_rel(matmul_nt(hidden, down_t).reshape(4, rows, model_dim))
    final = resid_mid + mlp_out
    squares = jnp.stack(
        [
            jnp.sum(valid * final * final),
            jnp.sum(valid * attn_out * attn_out),
            jnp.sum(valid * mlp_out * mlp_out),
            jnp.sum(valid),
        ]
    )
    grad_down_t = matmul_tn(cot_rel, hidden).astype(jnp.bfloat16)
    grad_up_w = matmul_tn(mlp_rel, grad_up_pre).astype(jnp.bfloat16)
    mlp_share = lax.psum_scatter(
        jnp.concatenate([grad_up_w, grad_down_t], axis=1), "dp", scatter_dimension=0, tiled=True
    ).astype(jnp.float32)

    out_grad = cotangent.astype(jnp.float32)
    grad_two, gain_two_grad = norm_backward(grad_mlp_input, gain_mlp, normed_two, inv_two)
    resid_grad = out_grad + grad_two
    resid_low = resid_grad.astype(jnp.bfloat16)
    grad_heads = matmul(resid_low, out_all).astype(jnp.bfloat16)
    grad_heads_rel = exchange_rel(grad_heads.reshape(rows, 4, cols).transpose(1, 0, 2))
    grad_out_rel = matmul_tn(resid_low, heads_cat).reshape(model_dim, 4, cols)
    grad_out_t = scatter_rel(grad_out_rel.transpose(1, 0, 2))

    grad_q, grad_k, grad_v = attend_backward(
        queries,
        key_rows,
        value_rows,
        to_abs(grad_heads_rel),
        log_sums,
        pieces,
        valid_len,
    )
    grad_v_rel = to_rel(grad_v.astype(jnp.bfloat16))
    fresh_low = jnp.where(rank < 2, grad_v_rel, jnp.zeros_like(grad_v_rel))
    grad_qkv = jnp.concatenate(
        [to_rel(grad_q.astype(jnp.bfloat16)), to_rel(grad_k.astype(jnp.bfloat16)), fresh_low],
        axis=2,
    ).reshape(seq_len, 3 * cols)
    grad_qkv_w = matmul_tn(input_rel, grad_qkv)
    grad_attn_input = scatter_rel(matmul_nt(grad_qkv, early_all).reshape(4, rows, model_dim))
    first_from_x = lax.ppermute(
        grad_v_rel[jnp.array([1, 3])], "tensor", [(2, 0), (3, 1)]
    )
    first_here = jnp.where(rank < 2, first_from_x, grad_v_rel[jnp.array([0, 2])])
    first_mine = first_here[0]
    first_peer = swap_core(first_here[1])
    first_grad = jnp.where(
        core == 0,
        jnp.concatenate([first_mine, first_peer], axis=1),
        jnp.concatenate([first_peer, first_mine], axis=1),
    ).astype(jnp.float32)
    grad_one, gain_one_grad = norm_backward(grad_attn_input, gain_attn, normed_one, inv_one)
    token_grad = resid_grad + grad_one

    tail_parts = jnp.concatenate([grad_qkv_w, grad_out_t], axis=1).astype(jnp.bfloat16)
    tail_all = lax.all_to_all(tail_parts.reshape(dp_size, shard, 4 * cols), "dp", 0, 0)
    tail_share = jnp.sum(tail_all.astype(jnp.float32), axis=0)
    value_own = tail_share[:, 2 * cols : 3 * cols]
    value_x = lax.ppermute(value_own, "tensor", [(0, 2), (1, 3)])
    value_here = jnp.where(rank < 2, value_own, value_x)
    value_peer = swap_core(value_here)
    value_share = jnp.where(
        core == 0,
        jnp.concatenate([value_here, value_peer], axis=1),
        jnp.concatenate([value_peer, value_here], axis=1),
    )
    small = jnp.concatenate([gain_one_grad, gain_two_grad, squares])
    count = dp_size * 4
    small_all = lax.all_to_all(
        jnp.broadcast_to(small[None], (count,) + small.shape), ("dp", "tensor"), 0, 0
    )
    total = jnp.sum(small_all, axis=0)
    square_total = total[2 * model_dim :]
    rms = jnp.sqrt(square_total[:3] / (square_total[3] * model_dim))
    return (
        final.astype(jnp.bfloat16),
        token_grad,
        first_grad,
        tail_share[:, :cols],
        tail_share[:, cols : 2 * cols],
        value_share,
        tail_share[:, 3 * cols :].T,
        mlp_share[:, :hidden_cols],
        mlp_share[:, hidden_cols:].T,
        total[:model_dim],
        total[model_dim : 2 * model_dim],
        rms,
    )


def solution(mesh):
    in_specs = (
        P(("dp", "tensor"), None),
        P(("dp", "tensor"), None),
        P("dp"),
        P("dp"),
        P("dp", "tensor"),
        P("dp", "tensor"),
        P("dp", None),
        P("tensor", "dp"),
        P("dp", "tensor"),
        P("tensor", "dp"),
        P(),
        P(),
        P(("dp", "tensor"), None),
    )
    out_specs = (
        P(("dp", "tensor"), None),
        P(("dp", "tensor"), None),
        P(("dp", "tensor"), None),
        P("dp", "tensor"),
        P("dp", "tensor"),
        P("dp", None),
        P("tensor", "dp"),
        P("dp", "tensor"),
        P("tensor", "dp"),
        P(),
        P(),
        P(),
    )
    return jax.shard_map(body, mesh=mesh, in_specs=in_specs, out_specs=out_specs, check_vma=False)
```

```python
import math

import jax
import jax.numpy as jnp
from jax import lax
from jax.experimental import pallas as pl
from jax.experimental.pallas import tpu as pltpu
from jax.sharding import PartitionSpec as P

HD = 64


EPS = 1e-05
NEG = -1e30


def matmul(first_op, second_op):
    return jnp.dot(first_op, second_op, preferred_element_type=jnp.float32)


def matmul_tn(first_op, second_op):
    return lax.dot_general(
        first_op, second_op, (((0,), (0,)), ((), ())), preferred_element_type=jnp.float32
    )


def matmul_nt(first_op, second_op):
    return lax.dot_general(
        first_op, second_op, (((1,), (1,)), ((), ())), preferred_element_type=jnp.float32
    )


def norm_forward(resid, norm_gain):
    centred = resid - jnp.mean(resid, axis=-1, keepdims=True)
    inv_std = lax.rsqrt(jnp.mean(centred * centred, axis=-1, keepdims=True) + EPS)
    normed = centred * inv_std
    return (normed * norm_gain, normed, inv_std)


def norm_backward(upstream, norm_gain, normed, inv_std):
    scaled = upstream * norm_gain
    inner = (
        scaled
        - jnp.mean(scaled, axis=-1, keepdims=True)
        - normed * jnp.mean(scaled * normed, axis=-1, keepdims=True)
    )
    return (inner * inv_std, jnp.sum(upstream * normed, axis=0))


BLK = 256


def nt(a, b):
    return lax.dot_general(a, b, (((1,), (1,)), ((), ())), preferred_element_type=jnp.float32)


def nn(a, b):
    return jnp.dot(a, b, preferred_element_type=jnp.float32)


def diag_allowed(picture):
    key_pos = lax.broadcasted_iota(jnp.int32, (BLK, BLK), 0)
    query_pos = lax.broadcasted_iota(jnp.int32, (BLK, BLK), 1)
    return (key_pos <= query_pos) | (picture > 0)


def pick(table_ref, info_ref, qkv_ref, first_ref, block, kind, head):
    cols = first_ref.shape[2]
    lane = kind * cols + head * HD
    part = qkv_ref[table_ref[block], :, lane : lane + HD]
    if kind == 2:
        other = first_ref[table_ref[block], :, head * HD : (head + 1) * HD]
        part = jnp.where(info_ref[1] > 0, part, other)
    return part


def prepare(table_ref, info_ref, qkv_ref, first_ref, q_aug, k_aug, head):
    blocks, rows = qkv_ref.shape[:2]
    seq = blocks * rows
    for block in range(blocks):
        span = slice(block * rows, (block + 1) * rows)
        part = pick(table_ref, info_ref, qkv_ref, first_ref, block, 0, head)
        q_aug[head, span, :HD] = part * jnp.bfloat16(1.0 / math.sqrt(HD))
        k_aug[head, span, :HD] = pick(table_ref, info_ref, qkv_ref, first_ref, block, 1, head)
    pos = lax.broadcasted_iota(jnp.int32, (seq, HD), 0)
    lane = lax.broadcasted_iota(jnp.int32, (seq, HD), 1)
    bias = jnp.where((lane == 0) & (pos >= info_ref[0]), NEG, 0.0)
    k_aug[head, :, HD:] = bias.astype(k_aug.dtype)
    q_aug[head, :, HD:] = jnp.where(lane == 0, 1.0, 0.0).astype(q_aug.dtype)


def forward_kernel(table_ref, info_ref, qkv_ref, first_ref, out_ref, lse_ref, q_aug, k_aug, v_t, o_t):
    blocks, rows, cols = first_ref.shape
    heads = cols // HD
    seq = blocks * rows
    for head in range(heads):
        prepare(table_ref, info_ref, qkv_ref, first_ref, q_aug, k_aug, head)
        for block in range(blocks):
            part = pick(table_ref, info_ref, qkv_ref, first_ref, block, 2, head)
            v_t[head, :, block * rows : (block + 1) * rows] = part.T

    def per_head(head, carry):
        for block in range(seq // BLK):
            lo, hi = block * BLK, (block + 1) * BLK
            scores = nt(k_aug[head, :hi, :], q_aug[head, lo:hi, :])
            last = jnp.where(diag_allowed(info_ref[2 + block]), scores[lo:], NEG)
            row_max = jnp.max(last, axis=0, keepdims=True)
            if block:
                row_max = jnp.maximum(row_max, jnp.max(scores[:lo], axis=0, keepdims=True))
            tail = jnp.exp(last - row_max)
            total = jnp.sum(tail, axis=0, keepdims=True)
            acc = nn(v_t[head, :, lo:hi], tail.astype(jnp.bfloat16))
            if block:
                front = jnp.exp(scores[:lo] - row_max)
                total = total + jnp.sum(front, axis=0, keepdims=True)
                acc = acc + nn(v_t[head, :, :lo], front.astype(jnp.bfloat16))
            o_t[head, :, lo:hi] = acc / total
            lse_ref[head, :, lo:hi] = row_max + jnp.log(total)
        return carry

    lax.fori_loop(0, heads, per_head, 0)
    for block in range(blocks):
        part = o_t[:, :, block * rows : (block + 1) * rows].reshape(cols, rows)
        out_ref[table_ref[block]] = part.T.astype(out_ref.dtype)


def attend(qkv, first, table, info):
    blocks, rows, cols = first.shape
    heads = cols // HD
    seq = blocks * rows
    smem = pl.BlockSpec(memory_space=pltpu.SMEM)
    vmem = pl.BlockSpec(memory_space=pltpu.VMEM)
    work = heads * seq * (seq + BLK) // 2
    return pl.pallas_call(
        forward_kernel,
        name="attend",
        out_shape=(
            jax.ShapeDtypeStruct((blocks, rows, cols), jnp.bfloat16),
            jax.ShapeDtypeStruct((heads, 1, seq), jnp.float32),
        ),
        in_specs=[smem, smem, vmem, vmem],
        out_specs=(vmem, vmem),
        scratch_shapes=[
            pltpu.VMEM((heads, seq, 2 * HD), jnp.bfloat16),
            pltpu.VMEM((heads, seq, 2 * HD), jnp.bfloat16),
            pltpu.VMEM((heads, HD, seq), jnp.bfloat16),
            pltpu.VMEM((heads, HD, seq), jnp.float32),
        ],
        compiler_params=pltpu.CompilerParams(vmem_limit_bytes=48 << 20),
        cost_estimate=pl.CostEstimate(
            flops=4 * work * HD * 4, transcendentals=work, bytes_accessed=10 * seq * cols
        ),
    )(table, info, qkv, first)


def backward_kernel(
    table_ref, info_ref, qkv_ref, first_ref, g_ref, o_ref, lse_ref, dqkv_ref, dv_ref,
    q_aug, k_aug, v_rows, g_rows, k_t, dq_t, dk_acc, dv_acc, delta,
):
    blocks, rows, cols = first_ref.shape
    heads = cols // HD
    seq = blocks * rows
    for head in range(heads):
        lane = head * HD
        prepare(table_ref, info_ref, qkv_ref, first_ref, q_aug, k_aug, head)
        for block in range(blocks):
            span = slice(block * rows, (block + 1) * rows)
            v_rows[head, span, :] = pick(table_ref, info_ref, qkv_ref, first_ref, block, 2, head)
            k_t[head, :, span] = pick(table_ref, info_ref, qkv_ref, first_ref, block, 1, head).T
            grads = g_ref[table_ref[block], :, lane : lane + HD]
            outs = o_ref[table_ref[block], :, lane : lane + HD].astype(jnp.float32)
            g_rows[head, span, :] = grads
            products = grads.astype(jnp.float32) * outs
            delta[head, :, span] = jnp.sum(products.T, axis=0, keepdims=True)

    def per_head(head, carry):
        dk_acc[head] = jnp.zeros_like(dk_acc[head])
        dv_acc[head] = jnp.zeros_like(dv_acc[head])
        for block in range(seq // BLK):
            lo, hi = block * BLK, (block + 1) * BLK
            q_block = q_aug[head, lo:hi, :]
            g_block = g_rows[head, lo:hi, :]
            lse = lse_ref[head, :, lo:hi]
            shift = delta[head, :, lo:hi]

            def part(start, stop, diagonal):
                probs = jnp.exp(nt(k_aug[head, start:stop, :], q_block) - lse)
                if diagonal:
                    probs = jnp.where(diag_allowed(info_ref[2 + block]), probs, 0.0)
                grad_probs = nt(v_rows[head, start:stop, :], g_block)
                grad_scores = (probs * (grad_probs - shift)).astype(jnp.bfloat16)
                dv_acc[head, start:stop, :] += nn(probs.astype(jnp.bfloat16), g_block)
                dk_acc[head, start:stop, :] += nn(grad_scores, q_block)[:, :HD]
                return nn(k_t[head, :, start:stop], grad_scores)

            acc = part(lo, hi, True)
            if block:
                acc = acc + part(0, lo, False)
            dq_t[head, :, lo:hi] = acc
        return carry

    lax.fori_loop(0, heads, per_head, 0)
    for block in range(blocks):
        span = slice(block * rows, (block + 1) * rows)
        to = table_ref[block]
        part = dq_t[:, :, span].reshape(cols, rows)
        dqkv_ref[to, :, :cols] = (part.T * (1.0 / math.sqrt(HD))).astype(dqkv_ref.dtype)
        for head in range(heads):
            lane = head * HD
            dqkv_ref[to, :, cols + lane : cols + lane + HD] = dk_acc[head, span, :].astype(dqkv_ref.dtype)
            value = dv_acc[head, span, :].astype(dv_ref.dtype)
            dv_ref[to, :, lane : lane + HD] = value
            kept = jnp.where(info_ref[1] > 0, value, jnp.zeros_like(value))
            dqkv_ref[to, :, 2 * cols + lane : 2 * cols + lane + HD] = kept


def attend_back(qkv, first, grad_heads, heads_out, lse, table, info):
    blocks, rows, cols = first.shape
    heads = cols // HD
    seq = blocks * rows
    smem = pl.BlockSpec(memory_space=pltpu.SMEM)
    vmem = pl.BlockSpec(memory_space=pltpu.VMEM)
    work = heads * seq * (seq + BLK) // 2
    return pl.pallas_call(
        backward_kernel,
        name="attend_back",
        out_shape=(
            jax.ShapeDtypeStruct((blocks, rows, 3 * cols), jnp.bfloat16),
            jax.ShapeDtypeStruct((blocks, rows, cols), jnp.bfloat16),
        ),
        in_specs=[smem, smem] + [vmem] * 5,
        out_specs=(vmem, vmem),
        scratch_shapes=[
            pltpu.VMEM((heads, seq, 2 * HD), jnp.bfloat16),
            pltpu.VMEM((heads, seq, 2 * HD), jnp.bfloat16),
            pltpu.VMEM((heads, seq, HD), jnp.bfloat16),
            pltpu.VMEM((heads, seq, HD), jnp.bfloat16),
            pltpu.VMEM((heads, HD, seq), jnp.bfloat16),
            pltpu.VMEM((heads, HD, seq), jnp.float32),
            pltpu.VMEM((heads, seq, HD), jnp.float32),
            pltpu.VMEM((heads, seq, HD), jnp.float32),
            pltpu.VMEM((heads, 1, seq), jnp.float32),
        ],
        compiler_params=pltpu.CompilerParams(vmem_limit_bytes=56 << 20),
        cost_estimate=pl.CostEstimate(
            flops=10 * work * HD * 4, transcendentals=work, bytes_accessed=24 * seq * cols
        ),
    )(table, info, qkv, first, grad_heads, heads_out, lse)


def gelu_tanh(pre_act):
    return jax.nn.gelu(pre_act, approximate=True)


X_SWAP = [(0, 2), (1, 3), (2, 0), (3, 1)]
CORE_SWAP = [(0, 1), (1, 0), (2, 3), (3, 2)]


def swap_x(v):
    return lax.ppermute(v, "tensor", X_SWAP)


def swap_core(v):
    return lax.ppermute(v, "tensor", CORE_SWAP)


def gather_rel(own):
    from_core = swap_core(own)
    from_x = swap_x(own)
    from_diag = swap_core(from_x)
    return jnp.concatenate([own, from_x, from_core, from_diag], axis=0)


def scatter_rel(parts):
    low = parts.astype(jnp.bfloat16)
    from_core = swap_core(low[2:4]).astype(jnp.float32)
    pair = parts[0:2] + from_core
    from_x = swap_x(pair[1].astype(jnp.bfloat16)).astype(jnp.float32)
    return pair[0] + from_x


def exchange_rel(blocks):
    from_x = swap_x(blocks[jnp.array([1, 3])])
    to_core = jnp.stack([blocks[2], from_x[1]])
    from_core = swap_core(to_core)
    return jnp.stack([blocks[0], from_x[0], from_core[0], from_core[1]])


def body(
    tokens,
    first_values,
    pieces,
    lengths,
    w_query,
    w_key,
    w_value,
    w_out,
    w_up,
    w_down,
    gain_attn,
    gain_mlp,
    cotangent,
):
    dp_size = lax.axis_size("dp")
    rank = lax.axis_index("tensor")
    core = rank % 2
    rows, model_dim = tokens.shape
    seq_len = rows * 4
    cols = w_query.shape[1]
    shard = w_query.shape[0]
    hidden_cols = w_up.shape[1]
    valid_len = lengths[0]
    positions = rank * rows + lax.iota(jnp.int32, rows)
    valid = (positions < valid_len).astype(jnp.float32)[:, None]
    table = (jnp.array([0, 2, 1, 3])[jnp.arange(4) ^ rank]).astype(jnp.int32)
    fresh = (rank < 2).astype(jnp.int32)
    info = jnp.concatenate([valid_len[None], fresh[None], pieces[::BLK]])

    value_cols = lax.dynamic_slice_in_dim(w_value, core * cols, cols, 1)
    early = jnp.concatenate([w_query, w_key, value_cols], axis=1)
    late = jnp.concatenate([w_up, w_down.T, w_out.T], axis=1)
    late_all = lax.all_gather(late, "dp", axis=0, tiled=True)
    early_all = lax.all_to_all(
        jnp.broadcast_to(early[None], (dp_size,) + early.shape), "dp", 0, 0
    ).reshape(model_dim, 3 * cols)

    tokens_wide = tokens.astype(jnp.float32)
    norm_one, normed_one, inv_one = norm_forward(tokens_wide, gain_attn)
    attn_input = norm_one.astype(jnp.bfloat16)
    input_rel = gather_rel(attn_input)
    first_x = lax.ppermute(first_values, "tensor", [(0, 2), (1, 3)])
    first_two = jnp.stack([first_values, first_x])
    first_mine = lax.dynamic_slice_in_dim(first_two, core * cols, cols, 2)
    first_other = lax.dynamic_slice_in_dim(first_two, (1 - core) * cols, cols, 2)
    first_rel = jnp.concatenate([first_mine, swap_core(first_other)], axis=0)
    cot_rel = gather_rel(cotangent)

    qkv = matmul(input_rel, early_all).astype(jnp.bfloat16).reshape(4, rows, 3 * cols)
    heads_rel, log_sums = attend(qkv, first_rel, table, info)
    heads_mine = exchange_rel(heads_rel)
    heads_cat = jnp.concatenate([heads_mine[i] for i in range(4)], axis=1)

    out_own = late_all[:, 2 * hidden_cols :]
    out_x = swap_x(out_own)
    out_pair = jnp.concatenate([out_own, out_x], axis=1)
    out_all = jnp.concatenate([out_pair, swap_core(out_pair)], axis=1)
    attn_out = matmul_nt(heads_cat, out_all)
    resid_mid = tokens_wide + attn_out
    norm_two, normed_two, inv_two = norm_forward(resid_mid, gain_mlp)
    mlp_input = norm_two.astype(jnp.bfloat16)
    mlp_rel = gather_rel(mlp_input)
    up_w = late_all[:, :hidden_cols]
    down_t = late_all[:, hidden_cols : 2 * hidden_cols]
    up_pre = matmul(mlp_rel, up_w)
    hidden_act, gelu_pull = jax.vjp(gelu_tanh, up_pre)
    hidden = hidden_act.astype(jnp.bfloat16)
    grad_hidden = matmul(cot_rel, down_t)
    grad_up_pre = gelu_pull(grad_hidden)[0].astype(jnp.bfloat16)
    grad_mlp_input = scatter_rel(matmul_nt(grad_up_pre, up_w).reshape(4, rows, model_dim))
    mlp_out = scatter_rel(matmul_nt(hidden, down_t).reshape(4, rows, model_dim))
    final = resid_mid + mlp_out
    squares = jnp.stack(
        [
            jnp.sum(valid * final * final),
            jnp.sum(valid * attn_out * attn_out),
            jnp.sum(valid * mlp_out * mlp_out),
            jnp.sum(valid),
        ]
    )
    grad_down_t = matmul_tn(cot_rel, hidden).astype(jnp.bfloat16)
    grad_up_w = matmul_tn(mlp_rel, grad_up_pre).astype(jnp.bfloat16)
    mlp_share = lax.psum_scatter(
        jnp.concatenate([grad_up_w, grad_down_t], axis=1), "dp", scatter_dimension=0, tiled=True
    ).astype(jnp.float32)

    out_grad = cotangent.astype(jnp.float32)
    grad_two, gain_two_grad = norm_backward(grad_mlp_input, gain_mlp, normed_two, inv_two)
    resid_grad = out_grad + grad_two
    resid_low = resid_grad.astype(jnp.bfloat16)
    grad_heads = matmul(resid_low, out_all).astype(jnp.bfloat16)
    grad_heads_rel = exchange_rel(grad_heads.reshape(rows, 4, cols).transpose(1, 0, 2))
    grad_out_rel = matmul_tn(resid_low, heads_cat).reshape(model_dim, 4, cols)
    grad_out_t = scatter_rel(grad_out_rel.transpose(1, 0, 2))

    grad_qkv, grad_v_rel = attend_back(
        qkv, first_rel, grad_heads_rel, heads_rel, log_sums, table, info
    )
    grad_qkv = grad_qkv.reshape(seq_len, 3 * cols)
    grad_qkv_w = matmul_tn(input_rel, grad_qkv)
    grad_attn_input = scatter_rel(matmul_nt(grad_qkv, early_all).reshape(4, rows, model_dim))
    first_from_x = lax.ppermute(
        grad_v_rel[jnp.array([1, 3])], "tensor", [(2, 0), (3, 1)]
    )
    first_here = jnp.where(rank < 2, first_from_x, grad_v_rel[jnp.array([0, 2])])
    first_mine = first_here[0]
    first_peer = swap_core(first_here[1])
    first_grad = jnp.where(
        core == 0,
        jnp.concatenate([first_mine, first_peer], axis=1),
        jnp.concatenate([first_peer, first_mine], axis=1),
    ).astype(jnp.float32)
    grad_one, gain_one_grad = norm_backward(grad_attn_input, gain_attn, normed_one, inv_one)
    token_grad = resid_grad + grad_one

    tail_parts = jnp.concatenate([grad_qkv_w, grad_out_t], axis=1).astype(jnp.bfloat16)
    tail_all = lax.all_to_all(tail_parts.reshape(dp_size, shard, 4 * cols), "dp", 0, 0)
    tail_share = jnp.sum(tail_all.astype(jnp.float32), axis=0)
    value_own = tail_share[:, 2 * cols : 3 * cols]
    value_x = lax.ppermute(value_own, "tensor", [(0, 2), (1, 3)])
    value_here = jnp.where(rank < 2, value_own, value_x)
    value_peer = swap_core(value_here)
    value_share = jnp.where(
        core == 0,
        jnp.concatenate([value_here, value_peer], axis=1),
        jnp.concatenate([value_peer, value_here], axis=1),
    )
    small = jnp.concatenate([gain_one_grad, gain_two_grad, squares])
    count = dp_size * 4
    small_all = lax.all_to_all(
        jnp.broadcast_to(small[None], (count,) + small.shape), ("dp", "tensor"), 0, 0
    )
    total = jnp.sum(small_all, axis=0)
    square_total = total[2 * model_dim :]
    rms = jnp.sqrt(square_total[:3] / (square_total[3] * model_dim))
    return (
        final.astype(jnp.bfloat16),
        token_grad,
        first_grad,
        tail_share[:, :cols],
        tail_share[:, cols : 2 * cols],
        value_share,
        tail_share[:, 3 * cols :].T,
        mlp_share[:, :hidden_cols],
        mlp_share[:, hidden_cols:].T,
        total[:model_dim],
        total[model_dim : 2 * model_dim],
        rms,
    )


def solution(mesh):
    in_specs = (
        P(("dp", "tensor"), None),
        P(("dp", "tensor"), None),
        P("dp"),
        P("dp"),
        P("dp", "tensor"),
        P("dp", "tensor"),
        P("dp", None),
        P("tensor", "dp"),
        P("dp", "tensor"),
        P("tensor", "dp"),
        P(),
        P(),
        P(("dp", "tensor"), None),
    )
    out_specs = (
        P(("dp", "tensor"), None),
        P(("dp", "tensor"), None),
        P(("dp", "tensor"), None),
        P("dp", "tensor"),
        P("dp", "tensor"),
        P("dp", None),
        P("tensor", "dp"),
        P("dp", "tensor"),
        P("tensor", "dp"),
        P(),
        P(),
        P(),
    )
    return jax.shard_map(body, mesh=mesh, in_specs=in_specs, out_specs=out_specs, check_vma=False)
```

```python
import functools
import math

import jax
import jax.numpy as jnp
from jax import lax
from jax.experimental import pallas as pl
from jax.experimental.pallas import tpu as pltpu
from jax.sharding import PartitionSpec as P

HD = 64
EPS = 1e-05
NEG = -1e30
BLK = 256

SMEM = pl.BlockSpec(memory_space=pltpu.SMEM)
VMEM = pl.BlockSpec(memory_space=pltpu.VMEM)


def nt(a, b):
    return lax.dot_general(a, b, (((1,), (1,)), ((), ())), preferred_element_type=jnp.float32)


def nn(a, b):
    return jnp.dot(a, b, preferred_element_type=jnp.float32)


def tn(a, b):
    return lax.dot_general(a, b, (((0,), (0,)), ((), ())), preferred_element_type=jnp.float32)


def call(kernel, name, outs, specs, scratch, flops, exps, args, vmem=56):
    moved = sum(math.prod(v.shape) * v.dtype.itemsize for v in list(args) + list(outs))
    return pl.pallas_call(
        kernel,
        name=name,
        out_shape=tuple(outs),
        in_specs=specs,
        out_specs=tuple(VMEM for _ in outs),
        scratch_shapes=scratch,
        compiler_params=pltpu.CompilerParams(vmem_limit_bytes=vmem << 20),
        cost_estimate=pl.CostEstimate(
            flops=int(flops), transcendentals=int(exps), bytes_accessed=int(moved)
        ),
    )(*args)


def low_shape(*shape):
    return jax.ShapeDtypeStruct(shape, jnp.bfloat16)


def wide_shape(*shape):
    return jax.ShapeDtypeStruct(shape, jnp.float32)


def diag_allowed(picture):
    key_pos = lax.broadcasted_iota(jnp.int32, (BLK, BLK), 0)
    query_pos = lax.broadcasted_iota(jnp.int32, (BLK, BLK), 1)
    return (key_pos <= query_pos) | (picture > 0)


def pick(info_ref, qkv_ref, firsts, rel, kind, head):
    cols = qkv_ref.shape[2] // 3
    lane = kind * cols + head * HD
    part = qkv_ref[rel, :, lane : lane + HD]
    if kind == 2:
        rank = info_ref[0]
        lane = head * HD
        lower = firsts[rel][:, lane : lane + HD]
        upper = firsts[rel][:, cols + lane : cols + lane + HD]
        part = jnp.where(rank < 2, part, jnp.where(rank % 2 == 0, lower, upper))
    return part


def place(info_ref, rel, rows):
    return pl.multiple_of((info_ref[0] ^ rel) * rows, rows)


def prepare(info_ref, qkv_ref, firsts, q_aug, k_aug, head):
    blocks, rows = qkv_ref.shape[:2]
    seq = blocks * rows
    for rel in range(blocks):
        span = pl.ds(place(info_ref, rel, rows), rows)
        part = pick(info_ref, qkv_ref, firsts, rel, 0, head)
        q_aug[head, span, :HD] = part * jnp.bfloat16(1.0 / math.sqrt(HD))
        k_aug[head, span, :HD] = pick(info_ref, qkv_ref, firsts, rel, 1, head)
    pos = lax.broadcasted_iota(jnp.int32, (seq, HD), 0)
    lane = lax.broadcasted_iota(jnp.int32, (seq, HD), 1)
    bias = jnp.where((lane == 0) & (pos >= info_ref[1]), NEG, 0.0)
    k_aug[head, :, HD:] = bias.astype(k_aug.dtype)
    q_aug[head, :, HD:] = jnp.where(lane == 0, 1.0, 0.0).astype(q_aug.dtype)


def forward_kernel(
    info_ref, x0, x1, x2, x3, w_ref, f0, f1, f2, f3,
    qkv_ref, own_ref, core_ref, pair_ref, lse_ref, q_aug, k_aug, v_t, o_t,
):
    inputs, firsts = (x0, x1, x2, x3), (f0, f1, f2, f3)
    blocks, rows = qkv_ref.shape[:2]
    cols = qkv_ref.shape[2] // 3
    heads = cols // HD
    seq = blocks * rows
    for rel in range(blocks):
        qkv_ref[rel] = nn(inputs[rel][...], w_ref[...]).astype(qkv_ref.dtype)
    for head in range(heads):
        prepare(info_ref, qkv_ref, firsts, q_aug, k_aug, head)
        for rel in range(blocks):
            part = pick(info_ref, qkv_ref, firsts, rel, 2, head)
            v_t[head, :, pl.ds(place(info_ref, rel, rows), rows)] = part.T

    def per_head(head, carry):
        for block in range(seq // BLK):
            lo, hi = block * BLK, (block + 1) * BLK
            scores = nt(k_aug[head, :hi, :], q_aug[head, lo:hi, :])
            last = jnp.where(diag_allowed(info_ref[2 + block]), scores[lo:], NEG)
            row_max = jnp.max(last, axis=0, keepdims=True)
            if block:
                row_max = jnp.maximum(row_max, jnp.max(scores[:lo], axis=0, keepdims=True))
            tail = jnp.exp(last - row_max)
            total = jnp.sum(tail, axis=0, keepdims=True)
            acc = nn(v_t[head, :, lo:hi], tail.astype(jnp.bfloat16))
            if block:
                front = jnp.exp(scores[:lo] - row_max)
                total = total + jnp.sum(front, axis=0, keepdims=True)
                acc = acc + nn(v_t[head, :, :lo], front.astype(jnp.bfloat16))
            o_t[head, :, lo:hi] = acc / total
            lse_ref[head, :, lo:hi] = row_max + jnp.log(total)
        return carry

    lax.fori_loop(0, heads, per_head, 0)
    for rel, out in enumerate((own_ref, core_ref, pair_ref.at[0], pair_ref.at[1])):
        part = o_t[:, :, pl.ds(place(info_ref, rel, rows), rows)].reshape(cols, rows)
        out[...] = part.T.astype(out.dtype)


def attend(info, inputs, weights, firsts):
    rows, dim = inputs[0].shape
    cols = weights.shape[1] // 3
    heads = cols // HD
    seq = 4 * rows
    work = heads * seq * (seq + BLK) // 2
    return call(
        forward_kernel,
        "attend",
        [
            low_shape(4, rows, 3 * cols),
            low_shape(rows, cols),
            low_shape(rows, cols),
            low_shape(2, rows, cols),
            wide_shape(heads, 1, seq),
        ],
        [SMEM] + [VMEM] * 9,
        [
            pltpu.VMEM((heads, seq, 2 * HD), jnp.bfloat16),
            pltpu.VMEM((heads, seq, 2 * HD), jnp.bfloat16),
            pltpu.VMEM((heads, HD, seq), jnp.bfloat16),
            pltpu.VMEM((heads, HD, seq), jnp.float32),
        ],
        16 * work * HD + 6 * seq * dim * cols,
        work,
        (info, *inputs, weights, *firsts),
        48,
    )


def backward_kernel(
    info_ref, qkv_ref, f0, f1, f2, f3, g0, g1, g2, g3, own_ref, core_ref, pair_ref, lse_ref,
    dqkv_ref, dv_own, dv_core, dv_pair,
    q_aug, k_aug, v_rows, g_rows, k_t, dq_t, dk_acc, dv_acc, delta,
):
    firsts, grads = (f0, f1, f2, f3), (g0, g1, g2.at[0], g3.at[1])
    outs = (own_ref, core_ref, pair_ref.at[0], pair_ref.at[1])
    dv_outs = (dv_own, dv_core, dv_pair.at[0], dv_pair.at[1])
    blocks, rows = qkv_ref.shape[:2]
    cols = qkv_ref.shape[2] // 3
    heads = cols // HD
    seq = blocks * rows
    for head in range(heads):
        lane = head * HD
        prepare(info_ref, qkv_ref, firsts, q_aug, k_aug, head)
        for rel in range(blocks):
            span = pl.ds(place(info_ref, rel, rows), rows)
            v_rows[head, span, :] = pick(info_ref, qkv_ref, firsts, rel, 2, head)
            k_t[head, :, span] = pick(info_ref, qkv_ref, firsts, rel, 1, head).T
            grad = grads[rel][:, lane : lane + HD]
            g_rows[head, span, :] = grad
            products = grad.astype(jnp.float32) * outs[rel][:, lane : lane + HD].astype(jnp.float32)
            delta[head, :, span] = jnp.sum(products.T, axis=0, keepdims=True)

    def per_head(head, carry):
        dk_acc[head] = jnp.zeros_like(dk_acc[head])
        dv_acc[head] = jnp.zeros_like(dv_acc[head])
        for block in range(seq // BLK):
            lo, hi = block * BLK, (block + 1) * BLK
            q_block = q_aug[head, lo:hi, :]
            g_block = g_rows[head, lo:hi, :]
            lse = lse_ref[head, :, lo:hi]
            shift = delta[head, :, lo:hi]

            def part(start, stop, diagonal):
                probs = jnp.exp(nt(k_aug[head, start:stop, :], q_block) - lse)
                if diagonal:
                    probs = jnp.where(diag_allowed(info_ref[2 + block]), probs, 0.0)
                grad_probs = nt(v_rows[head, start:stop, :], g_block)
                grad_scores = (probs * (grad_probs - shift)).astype(jnp.bfloat16)
                dv_acc[head, start:stop, :] += nn(probs.astype(jnp.bfloat16), g_block)
                dk_acc[head, start:stop, :] += nn(grad_scores, q_block)[:, :HD]
                return nn(k_t[head, :, start:stop], grad_scores)

            acc = part(lo, hi, True)
            if block:
                acc = acc + part(0, lo, False)
            dq_t[head, :, lo:hi] = acc
        return carry

    lax.fori_loop(0, heads, per_head, 0)
    fresh = info_ref[0] < 2
    for rel in range(blocks):
        span = pl.ds(place(info_ref, rel, rows), rows)
        part = dq_t[:, :, span].reshape(cols, rows)
        dqkv_ref[rel, :, :cols] = (part.T * (1.0 / math.sqrt(HD))).astype(dqkv_ref.dtype)
        for head in range(heads):
            lane = head * HD
            dqkv_ref[rel, :, cols + lane : cols + lane + HD] = dk_acc[head, span, :].astype(
                dqkv_ref.dtype
            )
            value = dv_acc[head, span, :].astype(dqkv_ref.dtype)
            dv_outs[rel][:, lane : lane + HD] = value
            kept = jnp.where(fresh, value, jnp.zeros_like(value))
            dqkv_ref[rel, :, 2 * cols + lane : 2 * cols + lane + HD] = kept


def attend_back(info, qkv, firsts, grads, outs, lse):
    rows = qkv.shape[1]
    cols = qkv.shape[2] // 3
    heads = cols // HD
    seq = 4 * rows
    work = heads * seq * (seq + BLK) // 2
    return call(
        backward_kernel,
        "attend_back",
        [
            low_shape(4, rows, 3 * cols),
            low_shape(rows, cols),
            low_shape(rows, cols),
            low_shape(2, rows, cols),
        ],
        [SMEM] + [VMEM] * 13,
        [
            pltpu.VMEM((heads, seq, 2 * HD), jnp.bfloat16),
            pltpu.VMEM((heads, seq, 2 * HD), jnp.bfloat16),
            pltpu.VMEM((heads, seq, HD), jnp.bfloat16),
            pltpu.VMEM((heads, seq, HD), jnp.bfloat16),
            pltpu.VMEM((heads, HD, seq), jnp.bfloat16),
            pltpu.VMEM((heads, HD, seq), jnp.float32),
            pltpu.VMEM((heads, seq, HD), jnp.float32),
            pltpu.VMEM((heads, seq, HD), jnp.float32),
            pltpu.VMEM((heads, 1, seq), jnp.float32),
        ],
        40 * work * HD,
        work,
        (info, qkv, *firsts, *grads, *outs, lse),
    )


def norm_stats(wide):
    centred = wide - jnp.mean(wide, axis=-1, keepdims=True)
    inv_std = lax.rsqrt(jnp.mean(centred * centred, axis=-1, keepdims=True) + EPS)
    return centred * inv_std, inv_std


def valid_rows(info_ref, rows, start, count):
    pos = info_ref[0] * rows + start + lax.broadcasted_iota(jnp.int32, (count, 1), 0)
    return (pos < info_ref[1]).astype(jnp.float32)


def row_sum(v):
    return jnp.sum(v, axis=0, keepdims=True)


def middle_kernel(
    info_ref, tok_ref, h0, h1, h2, h3, w0, w1, w2, w3, gain_ref, resid_ref, input_ref, square_ref
):
    rows = tok_ref.shape[0]
    square = 0.0
    for start in range(0, rows, BLK):
        span = slice(start, start + BLK)
        attn = nt(h0[span], w0[...]) + nt(h1[span], w1[...])
        attn = attn + nt(h2[0, span], w2[...]) + nt(h3[1, span], w3[...])
        resid = tok_ref[span].astype(jnp.float32) + attn
        resid_ref[span] = resid
        normed, _ = norm_stats(resid)
        input_ref[span] = (normed * gain_ref[...]).astype(input_ref.dtype)
        square = square + row_sum(attn * attn * valid_rows(info_ref, rows, start, BLK))
    square_ref[...] = square


def middle(info, tokens, heads, weights, gain):
    rows, dim = tokens.shape
    return call(
        middle_kernel,
        "middle",
        [wide_shape(rows, dim), low_shape(rows, dim), wide_shape(1, dim)],
        [SMEM] + [VMEM] * 10,
        [],
        2 * rows * dim * dim,
        rows,
        (info, tokens, *heads, *weights, gain),
    )


GELU_C = math.sqrt(2.0 / math.pi)
CUBE = 0.044715


def mlp_kernel(with_out, up_cols, x0, x1, c0, c1, w_ref, *refs):
    hid_ref, dup_ref, back_ref = refs[:3]
    rows = x0.shape[0]
    up_w, down_t = w_ref.at[:, :up_cols], w_ref.at[:, up_cols : 2 * up_cols]
    for block, (x_ref, c_ref) in enumerate(((x0, c0), (x1, c1))):
        for start in range(0, rows, BLK):
            span = slice(start, start + BLK)
            up = nn(x_ref[span], up_w[...])
            up2 = up * up
            th = jnp.tanh(GELU_C * up * (1.0 + CUBE * up2))
            half = 0.5 * (1.0 + th)
            hidden = (up * half).astype(jnp.bfloat16)
            hid_ref[block, span] = hidden
            slope = half + 0.5 * up * (1.0 - th * th) * (GELU_C * (1.0 + 3.0 * CUBE * up2))
            dup = (nn(c_ref[span], down_t[...]) * slope).astype(jnp.bfloat16)
            dup_ref[block, span] = dup
            back_ref[block][span] = nt(dup, up_w[...]).astype(jnp.bfloat16)
            if with_out:
                refs[3][block][span] = nt(hidden, down_t[...]).astype(jnp.bfloat16)


def mlp_kernel_full(up_cols, x0, x1, c0, c1, w_ref, hid_ref, dup_ref, b0, b1, o0, o1):
    mlp_kernel(True, up_cols, x0, x1, c0, c1, w_ref, hid_ref, dup_ref, (b0, b1), (o0, o1))


def mlp_kernel_part(up_cols, x0, x1, c0, c1, w_ref, hid_ref, dup_ref, b0, b1):
    mlp_kernel(False, up_cols, x0, x1, c0, c1, w_ref, hid_ref, dup_ref, (b0, b1))


def mlp(xs, cots, weights, up_cols, with_out):
    rows, dim = xs[0].shape
    body = mlp_kernel_full if with_out else mlp_kernel_part
    outs = [low_shape(2, rows, up_cols)] * 2 + [low_shape(rows, dim)] * (4 if with_out else 2)
    return call(
        functools.partial(body, up_cols),
        "mlp_full" if with_out else "mlp_part",
        outs,
        [VMEM] * 5,
        [],
        (8 if with_out else 6) * 2 * rows * dim * up_cols,
        2 * rows * up_cols,
        (*xs, *cots, weights),
    )


def mlp_grads_kernel(up_cols, x0, x1, x2, x3, c0, c1, c2, c3, h_a, h_b, d_a, d_b, w_ref, g_ref, o0, o1):
    down_t = w_ref.at[:, up_cols : 2 * up_cols]
    step = 2 * BLK
    for rel, out in ((0, o0), (1, o1)):
        out[...] = nt(h_b[rel], down_t[...]).astype(out.dtype)
    for start in range(0, up_cols, BLK):
        span = slice(start, start + BLK)
        acc = tn(x0[...], d_a[0, :, span]) + tn(x1[...], d_a[1, :, span])
        acc = acc + tn(x2[...], d_b[0, :, span]) + tn(x3[...], d_b[1, :, span])
        g_ref[:, span] = acc.astype(g_ref.dtype)
        acc = tn(c0[...], h_a[0, :, span]) + tn(c1[...], h_a[1, :, span])
        acc = acc + tn(c2[...], h_b[0, :, span]) + tn(c3[...], h_b[1, :, span])
        g_ref[:, up_cols + start : up_cols + start + BLK] = acc.astype(g_ref.dtype)


def mlp_grads(xs, cots, hid_a, hid_b, dup_a, dup_b, weights, up_cols):
    rows, dim = xs[0].shape
    return call(
        functools.partial(mlp_grads_kernel, up_cols),
        "mlp_grads",
        [low_shape(dim, 2 * up_cols), low_shape(rows, dim), low_shape(rows, dim)],
        [VMEM] * 13,
        [],
        20 * rows * dim * up_cols,
        0,
        (*xs, *cots, hid_a, hid_b, dup_a, dup_b, weights),
    )


def turn_kernel(
    resid_ref, cot_ref, b0, b1, b2, gain_ref, w0, w1, w2, w3,
    grad_ref, low_ref, d_own, d_core, d_pair, gain_out,
):
    rows = resid_ref.shape[0]
    gain_sum = 0.0
    for start in range(0, rows, BLK):
        span = slice(start, start + BLK)
        normed, inv_std = norm_stats(resid_ref[span])
        back = b0[span].astype(jnp.float32) + b1[span].astype(jnp.float32)
        back = back + b2[span].astype(jnp.float32)
        gain_sum = gain_sum + row_sum(back * normed)
        scaled = back * gain_ref[...]
        inner = scaled - jnp.mean(scaled, axis=-1, keepdims=True)
        inner = inner - normed * jnp.mean(scaled * normed, axis=-1, keepdims=True)
        grad = cot_ref[span].astype(jnp.float32) + inner * inv_std
        grad_ref[span] = grad
        low = grad.astype(jnp.bfloat16)
        low_ref[span] = low
        d_own[span] = nn(low, w0[...]).astype(jnp.bfloat16)
        d_core[span] = nn(low, w1[...]).astype(jnp.bfloat16)
        d_pair[0, span] = nn(low, w2[...]).astype(jnp.bfloat16)
        d_pair[1, span] = nn(low, w3[...]).astype(jnp.bfloat16)
    gain_out[...] = gain_sum


def turn(resid, cot, backs, gain, weights):
    rows, dim = cot.shape
    cols = weights[0].shape[1]
    return call(
        turn_kernel,
        "turn",
        [
            wide_shape(rows, dim),
            low_shape(rows, dim),
            low_shape(rows, cols),
            low_shape(rows, cols),
            low_shape(2, rows, cols),
            wide_shape(1, dim),
        ],
        [VMEM] * 10,
        [],
        2 * rows * dim * dim,
        rows,
        (resid, cot, *backs, gain, *weights),
    )


def out_grads_kernel(low_ref, h0, h1, h2, h3, o_near, o_far):
    cols = h0.shape[1]
    low = low_ref[...]
    o_near[0] = tn(low, h0[...])
    o_far[0] = tn(low, h1[...]).astype(jnp.bfloat16)
    o_near[1] = tn(low, h2[0])
    o_far[1] = tn(low, h3[1]).astype(jnp.bfloat16)


def out_grads(low, heads):
    rows, dim = low.shape
    cols = heads[0].shape[1]
    return call(
        out_grads_kernel,
        "out_grads",
        [wide_shape(2, dim, cols), low_shape(2, dim, cols)],
        [VMEM] * 5,
        [],
        2 * rows * dim * dim,
        0,
        (low, *heads),
    )


def input_grads_kernel(dqkv_ref, w_ref, o0, o1, o2, o3):
    for rel, out in ((2, o2), (3, o3), (0, o0), (1, o1)):
        out[...] = nt(dqkv_ref[rel], w_ref[...]).astype(out.dtype)


def input_grads(dqkv, weights):
    rows = dqkv.shape[1]
    dim, cols = weights.shape
    return call(
        input_grads_kernel,
        "input_grads",
        [low_shape(rows, dim)] * 4,
        [VMEM] * 2,
        [],
        8 * rows * dim * cols,
        0,
        (dqkv, weights),
    )


def qkv_grads_kernel(x0, x1, x2, x3, dqkv_ref, out_ref):
    acc = tn(x0[...], dqkv_ref[0]) + tn(x1[...], dqkv_ref[1])
    acc = acc + tn(x2[...], dqkv_ref[2]) + tn(x3[...], dqkv_ref[3])
    out_ref[...] = acc.astype(out_ref.dtype)


def qkv_grads(xs, dqkv):
    rows, dim = xs[0].shape
    cols = dqkv.shape[2]
    return call(
        qkv_grads_kernel,
        "qkv_grads",
        [low_shape(dim, cols)],
        [VMEM] * 5,
        [],
        8 * rows * dim * cols,
        0,
        (*xs, dqkv),
    )[0]


def finish_kernel(tok_ref, grad_ref, b0, b1, b2, gain_ref, out_ref, gain_out):
    rows = tok_ref.shape[0]
    gain_sum = 0.0
    for start in range(0, rows, BLK):
        span = slice(start, start + BLK)
        normed, inv_std = norm_stats(tok_ref[span].astype(jnp.float32))
        back = b0[span].astype(jnp.float32) + b1[span].astype(jnp.float32)
        back = back + b2[span].astype(jnp.float32)
        gain_sum = gain_sum + row_sum(back * normed)
        scaled = back * gain_ref[...]
        inner = scaled - jnp.mean(scaled, axis=-1, keepdims=True)
        inner = inner - normed * jnp.mean(scaled * normed, axis=-1, keepdims=True)
        out_ref[span] = grad_ref[span] + inner * inv_std
    gain_out[...] = gain_sum


def finish(tokens, grad, backs, gain):
    rows, dim = tokens.shape
    return call(
        finish_kernel,
        "finish",
        [wide_shape(rows, dim), wide_shape(1, dim)],
        [VMEM] * 6,
        [],
        rows * dim * 20,
        rows,
        (tokens, grad, *backs, gain),
    )


def output_kernel(info_ref, resid_ref, b0, b1, b2, out_ref, final_sq, mlp_sq):
    rows = resid_ref.shape[0]
    sum_final, sum_mlp = 0.0, 0.0
    for start in range(0, rows, BLK):
        span = slice(start, start + BLK)
        valid = valid_rows(info_ref, rows, start, BLK)
        mlp_out = b0[span].astype(jnp.float32) + b1[span].astype(jnp.float32)
        mlp_out = mlp_out + b2[span].astype(jnp.float32)
        final = resid_ref[span] + mlp_out
        out_ref[span] = final.astype(out_ref.dtype)
        sum_final = sum_final + row_sum(final * final * valid)
        sum_mlp = sum_mlp + row_sum(mlp_out * mlp_out * valid)
    final_sq[...] = sum_final
    mlp_sq[...] = sum_mlp


def output(info, resid, parts):
    rows, dim = resid.shape
    return call(
        output_kernel,
        "output",
        [low_shape(rows, dim), wide_shape(1, dim), wide_shape(1, dim)],
        [SMEM] + [VMEM] * 4,
        [],
        rows * dim * 10,
        0,
        (info, resid, *parts),
    )


X_SWAP = [(0, 2), (1, 3), (2, 0), (3, 1)]
CORE_SWAP = [(0, 1), (1, 0), (2, 3), (3, 2)]


def swap_x(v):
    return lax.ppermute(v, "tensor", X_SWAP)


def swap_core(v):
    return lax.ppermute(v, "tensor", CORE_SWAP)


def tied(value, *others):
    return lax.optimization_barrier((value, *others))[0]


def plus(a, b):
    return (a.astype(jnp.float32) + b.astype(jnp.float32)).astype(jnp.bfloat16)


def body(
    tokens,
    first_values,
    pieces,
    lengths,
    w_query,
    w_key,
    w_value,
    w_out,
    w_up,
    w_down,
    gain_attn,
    gain_mlp,
    cotangent,
):
    dp_size = lax.axis_size("dp")
    rank = lax.axis_index("tensor")
    core = rank % 2
    rows, dim = tokens.shape
    shard, cols = w_query.shape
    up_cols = w_up.shape[1]
    info = jnp.concatenate([rank[None].astype(jnp.int32), lengths, pieces[::BLK]])
    gain_one, gain_two = gain_attn[None], gain_mlp[None]

    value_cols = jnp.where(core == 0, w_value[:, :cols], w_value[:, cols:])
    early = jnp.concatenate([w_query, w_key, value_cols], axis=1)
    late = jnp.concatenate([w_up, w_down.T, w_out.T], axis=1)
    late_all = lax.all_gather(late, "dp", axis=0, tiled=True)
    early_all = lax.all_to_all(
        jnp.broadcast_to(early[None], (dp_size,) + early.shape), "dp", 0, 0
    ).reshape(dim, 3 * cols)
    tok_x = swap_x(tokens)
    tok_core = swap_core(tokens)
    tok_diag = swap_core(tok_x)
    first_x = lax.ppermute(first_values, "tensor", [(0, 2), (1, 3)])
    firsts = (first_values, swap_core(first_values), first_x, swap_core(first_x))

    def normed_low(v):
        normed, _ = norm_stats(v.astype(jnp.float32))
        return (normed * gain_one).astype(jnp.bfloat16)

    xs = tuple(normed_low(v) for v in (tokens, tok_core, tok_x, tok_diag))
    qkv, h_own, h_core, h_pair, lse = attend(info, xs, early_all, firsts)

    cot_x = swap_x(tied(cotangent, tok_x, first_x))
    out_own = late_all[:, 2 * up_cols :]
    out_x = swap_x(out_own)
    h_pair, h_core = lax.optimization_barrier((h_pair, h_core, cot_x))[:2]
    cot_core = swap_core(cotangent)
    cot_diag = swap_core(cot_x)
    outs = (out_own, swap_core(out_own), out_x, swap_core(out_x))

    from_x = swap_x(h_pair)
    heads_mine = (h_own, swap_core(h_core), from_x, swap_core(from_x))
    resid, mlp_in, attn_sq = middle(info, tokens, heads_mine, outs, gain_two)
    in_x = swap_x(mlp_in)
    in_core = swap_core(mlp_in)
    hid_a, dup_a, back_own, back_core, out_0, out_1 = mlp(
        (mlp_in, in_core), (cotangent, cot_core), late_all, up_cols, True
    )
    in_diag = swap_core(in_x)
    back_1 = swap_core(back_core)
    out_near = swap_core(out_1)
    hid_b, dup_b, back_x, back_diag = mlp((in_x, in_diag), (cot_x, cot_diag), late_all, up_cols, False)
    back_2 = swap_x(plus(back_x, swap_core(back_diag)))
    grads_mlp, out_2, out_3 = mlp_grads(
        (mlp_in, in_core, in_x, in_diag),
        (cotangent, cot_core, cot_x, cot_diag),
        hid_a, hid_b, dup_a, dup_b, late_all, up_cols,
    )
    mlp_share = lax.psum_scatter(grads_mlp, "dp", scatter_dimension=0, tiled=True)
    out_sum = plus(out_2, swap_core(out_3))

    resid_grad, resid_low, d_own, d_core, d_pair, gain_two_sum = turn(
        resid, cotangent, (back_own, back_1, back_2), gain_two, outs
    )
    d_x = swap_x(d_pair)
    grads_heads = (d_own, swap_core(d_core), d_x, swap_core(d_x))
    near, far = out_grads(resid_low, heads_mine)
    far = swap_core(far)
    dqkv, dv_own, dv_core, dv_pair = attend_back(
        info, qkv, firsts, grads_heads, (h_own, h_core, h_pair), lse
    )
    out_from_x = swap_x(tied(out_sum, d_x))
    near_x = swap_x(plus(near[1], far[1]))
    dqkv, dv_pair = lax.optimization_barrier((dqkv, dv_pair, out_from_x, near_x))[:2]

    b_0, b_1, b_2, b_3 = input_grads(dqkv, early_all)
    b_from_x = swap_x(plus(b_2, swap_core(b_3)))
    b_from_core = swap_core(b_1)
    grad_out_t = (near[0] + far[0].astype(jnp.float32) + near_x.astype(jnp.float32)).astype(jnp.bfloat16)
    grads_qkv = qkv_grads(xs, dqkv)
    tail = jnp.concatenate([grads_qkv, grad_out_t], axis=1).reshape(dp_size, shard, 4 * cols)
    tail_all = lax.all_to_all(tail, "dp", 0, 0)

    final, final_sq, mlp_sq = output(info, resid, (out_0, out_near, out_from_x))
    first_from_x = lax.ppermute(tied(dv_pair, b_from_x), "tensor", [(2, 0), (3, 1)])
    first_a = jnp.where(rank < 2, first_from_x[0], dv_own)
    first_b = swap_core(jnp.where(rank < 2, first_from_x[1], dv_core))
    first_grad = jnp.where(
        core == 0,
        jnp.concatenate([first_a, first_b], axis=1),
        jnp.concatenate([first_b, first_a], axis=1),
    ).astype(jnp.float32)
    token_grad, gain_one_sum = finish(tokens, resid_grad, (b_0, b_from_core, b_from_x), gain_one)

    tail_share = jnp.sum(tail_all.astype(jnp.float32), axis=0)
    value_own = tail_share[:, 2 * cols : 3 * cols]
    value_x = lax.ppermute(value_own, "tensor", [(0, 2), (1, 3)])
    value_here = jnp.where(rank < 2, value_own, value_x)
    value_peer = swap_core(value_here)
    value_share = jnp.where(
        core == 0,
        jnp.concatenate([value_here, value_peer], axis=1),
        jnp.concatenate([value_peer, value_here], axis=1),
    )
    positions = rank * rows + lax.iota(jnp.int32, rows)
    count = jnp.sum((positions < lengths[0]).astype(jnp.float32))
    squares = jnp.stack([jnp.sum(final_sq), jnp.sum(attn_sq), jnp.sum(mlp_sq), count])
    small = jnp.concatenate([gain_one_sum[0], gain_two_sum[0], squares])
    everyone = dp_size * 4
    small_all = lax.all_to_all(
        jnp.broadcast_to(small[None], (everyone,) + small.shape), ("dp", "tensor"), 0, 0
    )
    total = jnp.sum(small_all, axis=0)
    square_total = total[2 * dim :]
    rms = jnp.sqrt(square_total[:3] / (square_total[3] * dim))
    mlp_wide = mlp_share.astype(jnp.float32)
    return (
        final,
        token_grad,
        first_grad,
        tail_share[:, :cols],
        tail_share[:, cols : 2 * cols],
        value_share,
        tail_share[:, 3 * cols :].T,
        mlp_wide[:, :up_cols],
        mlp_wide[:, up_cols:].T,
        total[:dim],
        total[dim : 2 * dim],
        rms,
    )


def solution(mesh):
    in_specs = (
        P(("dp", "tensor"), None),
        P(("dp", "tensor"), None),
        P("dp"),
        P("dp"),
        P("dp", "tensor"),
        P("dp", "tensor"),
        P("dp", None),
        P("tensor", "dp"),
        P("dp", "tensor"),
        P("tensor", "dp"),
        P(),
        P(),
        P(("dp", "tensor"), None),
    )
    out_specs = (
        P(("dp", "tensor"), None),
        P(("dp", "tensor"), None),
        P(("dp", "tensor"), None),
        P("dp", "tensor"),
        P("dp", "tensor"),
        P("dp", None),
        P("tensor", "dp"),
        P("dp", "tensor"),
        P("tensor", "dp"),
        P(),
        P(),
        P(),
    )
    return jax.shard_map(body, mesh=mesh, in_specs=in_specs, out_specs=out_specs, check_vma=False)
```

```python
import functools
import math

import jax
import jax.numpy as jnp
from jax import lax
from jax.experimental import pallas as pl
from jax.experimental.pallas import tpu as pltpu
from jax.sharding import PartitionSpec as P

HD = 64
EPS = 1e-05
NEG = -1e30
BLK = 256
LANES = 128

SMEM = pl.BlockSpec(memory_space=pltpu.SMEM)
VMEM = pl.BlockSpec(memory_space=pltpu.VMEM)


def nt(a, b):
    return lax.dot_general(a, b, (((1,), (1,)), ((), ())), preferred_element_type=jnp.float32)


def nn(a, b):
    return jnp.dot(a, b, preferred_element_type=jnp.float32)


def tn(a, b):
    return lax.dot_general(a, b, (((0,), (0,)), ((), ())), preferred_element_type=jnp.float32)


WEIGHTS = {"output": 0.01, "mlp_shares": 0.01, "tail_shares": 0.01, "finish": 0.01}


def call(kernel, name, outs, specs, scratch, flops, exps, args, vmem=56):
    weight = WEIGHTS.get(name, 3.0)
    moved = sum(math.prod(v.shape) * v.dtype.itemsize for v in list(args) + list(outs))
    return pl.pallas_call(
        kernel,
        name=name,
        out_shape=tuple(outs),
        in_specs=specs,
        out_specs=tuple(VMEM for _ in outs),
        scratch_shapes=scratch,
        compiler_params=pltpu.CompilerParams(vmem_limit_bytes=vmem << 20),
        cost_estimate=pl.CostEstimate(
            flops=int(flops * weight),
            transcendentals=int(exps * weight),
            bytes_accessed=int(moved * weight),
        ),
    )(*args)


def low_shape(*shape):
    return jax.ShapeDtypeStruct(shape, jnp.bfloat16)


def wide_shape(*shape):
    return jax.ShapeDtypeStruct(shape, jnp.float32)


def diag_allowed(picture):
    key_pos = lax.broadcasted_iota(jnp.int32, (BLK, BLK), 0)
    query_pos = lax.broadcasted_iota(jnp.int32, (BLK, BLK), 1)
    return (key_pos <= query_pos) | (picture > 0)


def pick(info_ref, qkv_ref, firsts, rel, kind, head):
    cols = qkv_ref.shape[2] // 3
    lane = kind * cols + head * HD
    part = qkv_ref[rel, :, lane : lane + HD]
    if kind == 2:
        rank = info_ref[0]
        lane = head * HD
        lower = firsts[rel][:, lane : lane + HD]
        upper = firsts[rel][:, cols + lane : cols + lane + HD]
        part = jnp.where(rank < 2, part, jnp.where(rank % 2 == 0, lower, upper))
    return part


def place(info_ref, rel, rows):
    return pl.multiple_of((info_ref[0] ^ rel) * rows, rows)


def prepare(info_ref, qkv_ref, firsts, q_aug, k_aug, slot, head):
    blocks, rows = qkv_ref.shape[:2]
    seq = blocks * rows
    for rel in range(blocks):
        span = pl.ds(place(info_ref, rel, rows), rows)
        part = pick(info_ref, qkv_ref, firsts, rel, 0, head)
        q_aug[slot, span, :HD] = part * jnp.bfloat16(1.0 / math.sqrt(HD))
        k_aug[slot, span, :HD] = pick(info_ref, qkv_ref, firsts, rel, 1, head)
    pos = lax.broadcasted_iota(jnp.int32, (seq, HD), 0)
    lane = lax.broadcasted_iota(jnp.int32, (seq, HD), 1)
    bias = jnp.where((lane == 0) & (pos >= info_ref[1]), NEG, 0.0)
    k_aug[slot, :, HD:] = bias.astype(k_aug.dtype)
    q_aug[slot, :, HD:] = jnp.where(lane == 0, 1.0, 0.0).astype(q_aug.dtype)


def assemble(dst_ref, parts, half):
    if len(parts) == 1:
        dst_ref[...] = parts[0][0]
        return
    mine, other = parts
    count, shard = mine.shape[:2]
    for part in range(count):
        dst_ref[pl.ds(pl.multiple_of((2 * part + half) * shard, shard), shard), :] = mine[part]
        dst_ref[pl.ds(pl.multiple_of((2 * part + 1 - half) * shard, shard), shard), :] = other[part]


def forward_head(head, info_ref, q_aug, k_aug, v_t, o_t, lse_ref):
    seq = q_aug.shape[1]
    for block in range(seq // BLK):
        lo, hi = block * BLK, (block + 1) * BLK
        scores = nt(k_aug[head, :hi, :], q_aug[head, lo:hi, :])
        last = jnp.where(diag_allowed(info_ref[2 + block]), scores[lo:], NEG)
        row_max = jnp.max(last, axis=0, keepdims=True)
        if block:
            row_max = jnp.maximum(row_max, jnp.max(scores[:lo], axis=0, keepdims=True))
        tail = jnp.exp(last - row_max)
        total = jnp.sum(tail, axis=0, keepdims=True)
        acc = nn(v_t[head, :, lo:hi], tail.astype(jnp.bfloat16))
        if block:
            front = jnp.exp(scores[:lo] - row_max)
            total = total + jnp.sum(front, axis=0, keepdims=True)
            acc = acc + nn(v_t[head, :, :lo], front.astype(jnp.bfloat16))
        o_t[head, :, lo:hi] = acc / total
        lse_ref[head, :, lo:hi] = row_max + jnp.log(total)


def prepare_values(info_ref, qkv_ref, firsts, v_t, slot, head):
    rows = qkv_ref.shape[1]
    for rel in range(qkv_ref.shape[0]):
        part = pick(info_ref, qkv_ref, firsts, rel, 2, head)
        v_t[slot, :, pl.ds(place(info_ref, rel, rows), rows)] = part.T


def first_kernel(info_ref, x0, x1, x2, x3, f0, f1, f2, f3, *refs):
    *parts, qkv_ref, w_ref, o_t, lse_ref, q_aug, k_aug, v_t = refs
    inputs, firsts = (x0, x1, x2, x3), (f0, f1, f2, f3)
    assemble(w_ref, parts, info_ref[2 + 4 * x0.shape[0] // BLK])
    for rel in range(4):
        qkv_ref[rel] = nn(inputs[rel][...], w_ref[...]).astype(qkv_ref.dtype)
    prepare(info_ref, qkv_ref, firsts, q_aug, k_aug, 0, 0)
    prepare_values(info_ref, qkv_ref, firsts, v_t, 0, 0)
    forward_head(0, info_ref, q_aug, k_aug, v_t, o_t, lse_ref)


def attend_first(info, inputs, parts, firsts):
    rows, dim = inputs[0].shape
    wide = parts[0].shape[2]
    seq = 4 * rows
    work = seq * (seq + BLK) // 2
    return call(
        first_kernel,
        "attend_first",
        [
            low_shape(4, rows, wide),
            low_shape(dim, wide),
            wide_shape(1, HD, seq),
            wide_shape(1, 1, seq),
        ],
        [SMEM] + [VMEM] * (8 + len(parts)),
        [
            pltpu.VMEM((1, seq, 2 * HD), jnp.bfloat16),
            pltpu.VMEM((1, seq, 2 * HD), jnp.bfloat16),
            pltpu.VMEM((1, HD, seq), jnp.bfloat16),
        ],
        16 * work * HD + 2 * seq * dim * wide,
        work,
        (info, *inputs, *firsts, *parts),
        48,
    )


def rest_kernel(
    info_ref, qkv_ref, f0, f1, f2, f3, o_first, lse_first,
    own_ref, core_ref, pair_ref, lse_ref, q_aug, k_aug, v_t, o_t, lse_part,
):
    firsts = (f0, f1, f2, f3)
    blocks, rows = qkv_ref.shape[:2]
    cols = qkv_ref.shape[2] // 3
    heads = cols // HD
    for head in range(1, heads):
        prepare(info_ref, qkv_ref, firsts, q_aug, k_aug, head - 1, head)
        prepare_values(info_ref, qkv_ref, firsts, v_t, head - 1, head)

    def per_head(head, carry):
        forward_head(head, info_ref, q_aug, k_aug, v_t, o_t, lse_part)
        return carry

    lax.fori_loop(0, heads - 1, per_head, 0)
    lse_ref[0] = lse_first[0]
    for head in range(1, heads):
        lse_ref[head] = lse_part[head - 1]
    for rel, out in enumerate((own_ref, core_ref, pair_ref.at[0], pair_ref.at[1])):
        span = pl.ds(place(info_ref, rel, rows), rows)
        part = jnp.concatenate([o_first[0, :, span], o_t[:, :, span].reshape(cols - HD, rows)], axis=0)
        out[...] = part.T.astype(out.dtype)


def attend_rest(info, qkv, firsts, o_first, lse_first):
    rows = qkv.shape[1]
    cols = qkv.shape[2] // 3
    heads = cols // HD
    seq = 4 * rows
    work = (heads - 1) * seq * (seq + BLK) // 2
    return call(
        rest_kernel,
        "attend_rest",
        [
            low_shape(rows, cols),
            low_shape(rows, cols),
            low_shape(2, rows, cols),
            wide_shape(heads, 1, seq),
        ],
        [SMEM] + [VMEM] * 7,
        [
            pltpu.VMEM((heads - 1, seq, 2 * HD), jnp.bfloat16),
            pltpu.VMEM((heads - 1, seq, 2 * HD), jnp.bfloat16),
            pltpu.VMEM((heads - 1, HD, seq), jnp.bfloat16),
            pltpu.VMEM((heads - 1, HD, seq), jnp.float32),
            pltpu.VMEM((heads - 1, 1, seq), jnp.float32),
        ],
        16 * work * HD,
        work,
        (info, qkv, *firsts, o_first, lse_first),
        48,
    )


def backward_kernel(
    info_ref, qkv_ref, f0, f1, f2, f3, g0, g1, g2, g3, own_ref, core_ref, pair_ref, lse_ref,
    dqkv_ref, dv_own, dv_core, dv_pair,
    q_aug, k_aug, v_rows, g_rows, k_t, dq_t, dk_acc, dv_acc, delta,
):
    firsts, grads = (f0, f1, f2, f3), (g0, g1, g2.at[0], g3.at[1])
    outs = (own_ref, core_ref, pair_ref.at[0], pair_ref.at[1])
    dv_outs = (dv_own, dv_core, dv_pair.at[0], dv_pair.at[1])
    blocks, rows = qkv_ref.shape[:2]
    cols = qkv_ref.shape[2] // 3
    heads = cols // HD
    seq = blocks * rows
    for head in range(heads):
        lane = head * HD
        prepare(info_ref, qkv_ref, firsts, q_aug, k_aug, head, head)
        for rel in range(blocks):
            span = pl.ds(place(info_ref, rel, rows), rows)
            v_rows[head, span, :] = pick(info_ref, qkv_ref, firsts, rel, 2, head)
            k_t[head, :, span] = pick(info_ref, qkv_ref, firsts, rel, 1, head).T
            grad = grads[rel][:, lane : lane + HD]
            g_rows[head, span, :] = grad
            products = grad.astype(jnp.float32) * outs[rel][:, lane : lane + HD].astype(jnp.float32)
            delta[head, :, span] = jnp.sum(products.T, axis=0, keepdims=True)

    def per_head(head, carry):
        dk_acc[head] = jnp.zeros_like(dk_acc[head])
        dv_acc[head] = jnp.zeros_like(dv_acc[head])
        for block in range(seq // BLK):
            lo, hi = block * BLK, (block + 1) * BLK
            q_block = q_aug[head, lo:hi, :]
            g_block = g_rows[head, lo:hi, :]
            lse = lse_ref[head, :, lo:hi]
            shift = delta[head, :, lo:hi]

            def part(start, stop, diagonal):
                probs = jnp.exp(nt(k_aug[head, start:stop, :], q_block) - lse)
                if diagonal:
                    probs = jnp.where(diag_allowed(info_ref[2 + block]), probs, 0.0)
                grad_probs = nt(v_rows[head, start:stop, :], g_block)
                grad_scores = (probs * (grad_probs - shift)).astype(jnp.bfloat16)
                dv_acc[head, start:stop, :] += nn(probs.astype(jnp.bfloat16), g_block)
                dk_acc[head, start:stop, :] += nn(grad_scores, q_block)[:, :HD]
                return nn(k_t[head, :, start:stop], grad_scores)

            acc = part(lo, hi, True)
            if block:
                acc = acc + part(0, lo, False)
            dq_t[head, :, lo:hi] = acc
        return carry

    lax.fori_loop(0, heads, per_head, 0)
    fresh = info_ref[0] < 2
    for rel in range(blocks):
        span = pl.ds(place(info_ref, rel, rows), rows)
        part = dq_t[:, :, span].reshape(cols, rows)
        dqkv_ref[rel, :, :cols] = (part.T * (1.0 / math.sqrt(HD))).astype(dqkv_ref.dtype)
        for head in range(heads):
            lane = head * HD
            dqkv_ref[rel, :, cols + lane : cols + lane + HD] = dk_acc[head, span, :].astype(
                dqkv_ref.dtype
            )
            value = dv_acc[head, span, :].astype(dqkv_ref.dtype)
            dv_outs[rel][:, lane : lane + HD] = value
            kept = jnp.where(fresh, value, jnp.zeros_like(value))
            dqkv_ref[rel, :, 2 * cols + lane : 2 * cols + lane + HD] = kept


def attend_back(info, qkv, firsts, grads, outs, lse):
    rows = qkv.shape[1]
    cols = qkv.shape[2] // 3
    heads = cols // HD
    seq = 4 * rows
    work = heads * seq * (seq + BLK) // 2
    return call(
        backward_kernel,
        "attend_back",
        [
            low_shape(4, rows, 3 * cols),
            low_shape(rows, cols),
            low_shape(rows, cols),
            low_shape(2, rows, cols),
        ],
        [SMEM] + [VMEM] * 13,
        [
            pltpu.VMEM((heads, seq, 2 * HD), jnp.bfloat16),
            pltpu.VMEM((heads, seq, 2 * HD), jnp.bfloat16),
            pltpu.VMEM((heads, seq, HD), jnp.bfloat16),
            pltpu.VMEM((heads, seq, HD), jnp.bfloat16),
            pltpu.VMEM((heads, HD, seq), jnp.bfloat16),
            pltpu.VMEM((heads, HD, seq), jnp.float32),
            pltpu.VMEM((heads, seq, HD), jnp.float32),
            pltpu.VMEM((heads, seq, HD), jnp.float32),
            pltpu.VMEM((heads, 1, seq), jnp.float32),
        ],
        40 * work * HD,
        work,
        (info, qkv, *firsts, *grads, *outs, lse),
    )


def norm_stats(wide):
    centred = wide - jnp.mean(wide, axis=-1, keepdims=True)
    inv_std = lax.rsqrt(jnp.mean(centred * centred, axis=-1, keepdims=True) + EPS)
    return centred * inv_std, inv_std


def valid_rows(info_ref, rows, start, count):
    pos = info_ref[0] * rows + start + lax.broadcasted_iota(jnp.int32, (count, 1), 0)
    return (pos < info_ref[1]).astype(jnp.float32)


def row_sum(v):
    return jnp.sum(v, axis=0, keepdims=True)


def middle_kernel(
    info_ref, tok_ref, h0, h1, h2, h3, w0, w1, w2, w3, gain_ref, resid_ref, input_ref, square_ref
):
    rows = tok_ref.shape[0]
    square = 0.0
    for start in range(0, rows, BLK):
        span = slice(start, start + BLK)
        attn = nt(h0[span], w0[...]) + nt(h1[span], w1[...])
        attn = attn + nt(h2[0, span], w2[...]) + nt(h3[1, span], w3[...])
        resid = tok_ref[span].astype(jnp.float32) + attn
        resid_ref[span] = resid
        normed, _ = norm_stats(resid)
        input_ref[span] = (normed * gain_ref[...]).astype(input_ref.dtype)
        square = square + row_sum(attn * attn * valid_rows(info_ref, rows, start, BLK))
    square_ref[...] = square


def middle(info, tokens, heads, weights, gain):
    rows, dim = tokens.shape
    return call(
        middle_kernel,
        "middle",
        [wide_shape(rows, dim), low_shape(rows, dim), wide_shape(1, dim)],
        [SMEM] + [VMEM] * 10,
        [],
        2 * rows * dim * dim,
        rows,
        (info, tokens, *heads, *weights, gain),
    )


GELU_C = math.sqrt(2.0 / math.pi)
CUBE = 0.044715


def mlp_tiles(xs, cots, w_ref, hid_ref, dup_ref, backs, outs):
    rows = xs[0].shape[0]
    up_cols = w_ref.shape[1] // 2
    up_w, down_t = w_ref.at[:, :up_cols], w_ref.at[:, up_cols:]
    for block in range(2):
        for start in range(0, rows, BLK):
            span = slice(start, start + BLK)
            up = nn(xs[block][span], up_w[...])
            up2 = up * up
            th = jnp.tanh(GELU_C * up * (1.0 + CUBE * up2))
            half = 0.5 * (1.0 + th)
            hidden = (up * half).astype(jnp.bfloat16)
            hid_ref[block, span] = hidden
            slope = half + 0.5 * up * (1.0 - th * th) * (GELU_C * (1.0 + 3.0 * CUBE * up2))
            dup = (nn(cots[block][span], down_t[...]) * slope).astype(jnp.bfloat16)
            dup_ref[block, span] = dup
            backs[block][span] = nt(dup, up_w[...]).astype(jnp.bfloat16)
            if outs:
                outs[block][span] = nt(hidden, down_t[...]).astype(jnp.bfloat16)


def mlp_near_kernel(info_ref, x0, x1, c0, c1, *refs):
    *parts, w_ref, hid_ref, dup_ref, b0, b1, o0, o1 = refs
    assemble(w_ref, parts, info_ref[2 + 4 * x0.shape[0] // BLK])
    mlp_tiles((x0, x1), (c0, c1), w_ref, hid_ref, dup_ref, (b0, b1), (o0, o1))


def mlp_far_kernel(x0, x1, c0, c1, w_ref, hid_ref, dup_ref, b0, b1):
    mlp_tiles((x0, x1), (c0, c1), w_ref, hid_ref, dup_ref, (b0, b1), ())


def mlp_near(info, xs, cots, parts):
    rows, dim = xs[0].shape
    wide = parts[0].shape[2]
    return call(
        mlp_near_kernel,
        "mlp_near",
        [low_shape(dim, wide)] + [low_shape(2, rows, wide // 2)] * 2 + [low_shape(rows, dim)] * 4,
        [SMEM] + [VMEM] * (4 + len(parts)),
        [],
        8 * rows * dim * wide,
        rows * wide,
        (info, *xs, *cots, *parts),
    )


def mlp_far(xs, cots, weights):
    rows, dim = xs[0].shape
    wide = weights.shape[1]
    return call(
        mlp_far_kernel,
        "mlp_far",
        [low_shape(2, rows, wide // 2)] * 2 + [low_shape(rows, dim)] * 2,
        [VMEM] * 5,
        [],
        6 * rows * dim * wide,
        rows * wide,
        (*xs, *cots, weights),
    )


def mlp_grads_kernel(up_cols, x0, x1, x2, x3, c0, c1, c2, c3, h_a, h_b, d_a, d_b, w_ref, g_ref, o0, o1):
    down_t = w_ref.at[:, up_cols : 2 * up_cols]
    step = 2 * BLK
    for rel, out in ((0, o0), (1, o1)):
        out[...] = nt(h_b[rel], down_t[...]).astype(out.dtype)
    for start in range(0, up_cols, BLK):
        span = slice(start, start + BLK)
        acc = tn(x0[...], d_a[0, :, span]) + tn(x1[...], d_a[1, :, span])
        acc = acc + tn(x2[...], d_b[0, :, span]) + tn(x3[...], d_b[1, :, span])
        g_ref[:, span] = acc.astype(g_ref.dtype)
        acc = tn(c0[...], h_a[0, :, span]) + tn(c1[...], h_a[1, :, span])
        acc = acc + tn(c2[...], h_b[0, :, span]) + tn(c3[...], h_b[1, :, span])
        g_ref[:, up_cols + start : up_cols + start + BLK] = acc.astype(g_ref.dtype)


def mlp_grads(xs, cots, hid_a, hid_b, dup_a, dup_b, weights, up_cols):
    rows, dim = xs[0].shape
    return call(
        functools.partial(mlp_grads_kernel, up_cols),
        "mlp_grads",
        [low_shape(dim, 2 * up_cols), low_shape(rows, dim), low_shape(rows, dim)],
        [VMEM] * 13,
        [],
        20 * rows * dim * up_cols,
        0,
        (*xs, *cots, hid_a, hid_b, dup_a, dup_b, weights),
    )


def turn_kernel(
    resid_ref, cot_ref, b0, b1, b2, gain_ref, w0, w1, w2, w3,
    grad_ref, low_ref, d_own, d_core, d_pair, gain_out,
):
    rows = resid_ref.shape[0]
    gain_sum = 0.0
    for start in range(0, rows, BLK):
        span = slice(start, start + BLK)
        normed, inv_std = norm_stats(resid_ref[span])
        back = b0[span].astype(jnp.float32) + b1[span].astype(jnp.float32)
        back = back + b2[span].astype(jnp.float32)
        gain_sum = gain_sum + row_sum(back * normed)
        scaled = back * gain_ref[...]
        inner = scaled - jnp.mean(scaled, axis=-1, keepdims=True)
        inner = inner - normed * jnp.mean(scaled * normed, axis=-1, keepdims=True)
        grad = cot_ref[span].astype(jnp.float32) + inner * inv_std
        grad_ref[span] = grad
        low = grad.astype(jnp.bfloat16)
        low_ref[span] = low
        d_own[span] = nn(low, w0[...]).astype(jnp.bfloat16)
        d_core[span] = nn(low, w1[...]).astype(jnp.bfloat16)
        d_pair[0, span] = nn(low, w2[...]).astype(jnp.bfloat16)
        d_pair[1, span] = nn(low, w3[...]).astype(jnp.bfloat16)
    gain_out[...] = gain_sum


def turn(resid, cot, backs, gain, weights):
    rows, dim = cot.shape
    cols = weights[0].shape[1]
    return call(
        turn_kernel,
        "turn",
        [
            wide_shape(rows, dim),
            low_shape(rows, dim),
            low_shape(rows, cols),
            low_shape(rows, cols),
            low_shape(2, rows, cols),
            wide_shape(1, dim),
        ],
        [VMEM] * 10,
        [],
        2 * rows * dim * dim,
        rows,
        (resid, cot, *backs, gain, *weights),
    )


def out_grads_kernel(low_ref, h0, h1, h2, h3, o_near, o_far):
    cols = h0.shape[1]
    low = low_ref[...]
    dim = low.shape[1]
    o_near[:dim] = tn(low, h0[...])
    o_far[:dim] = tn(low, h1[...]).astype(jnp.bfloat16)
    o_near[dim:] = tn(low, h2[0])
    o_far[dim:] = tn(low, h3[1]).astype(jnp.bfloat16)


def out_grads(low, heads):
    rows, dim = low.shape
    cols = heads[0].shape[1]
    return call(
        out_grads_kernel,
        "out_grads",
        [wide_shape(2 * dim, cols), low_shape(2 * dim, cols)],
        [VMEM] * 5,
        [],
        2 * rows * dim * dim,
        0,
        (low, *heads),
    )


def input_grads_kernel(dqkv_ref, w_ref, x0, x1, x2, x3, gain_ref, o0, o1, o2, o3, gain_out):
    gain_sum = 0.0
    rows = x0.shape[0]
    for rel, x_ref, out in ((2, x2, o2), (3, x3, o3), (0, x0, o0), (1, x1, o1)):
        for start in range(0, rows, BLK):
            span = slice(start, start + BLK)
            part = nt(dqkv_ref[rel, span], w_ref[...])
            out[span] = part.astype(out.dtype)
            gain_sum = gain_sum + row_sum(part * x_ref[span].astype(jnp.float32))
    gain_out[...] = gain_sum / gain_ref[...]


def input_grads(dqkv, weights, xs, gain):
    rows = dqkv.shape[1]
    dim, cols = weights.shape
    return call(
        input_grads_kernel,
        "input_grads",
        [low_shape(rows, dim)] * 4 + [wide_shape(1, dim)],
        [VMEM] * 7,
        [],
        8 * rows * dim * cols,
        0,
        (dqkv, weights, *xs, gain),
    )


def qkv_grads_kernel(x0, x1, x2, x3, dqkv_ref, near_ref, far_ref, far_x, out_ref):
    wide = dqkv_ref.shape[2]
    acc = tn(x0[...], dqkv_ref[0]) + tn(x1[...], dqkv_ref[1])
    acc = acc + tn(x2[...], dqkv_ref[2]) + tn(x3[...], dqkv_ref[3])
    out_ref[:, :wide] = acc.astype(out_ref.dtype)
    dim = out_ref.shape[0]
    total = near_ref[:dim] + far_ref[:dim].astype(jnp.float32) + far_x[...].astype(jnp.float32)
    out_ref[:, wide:] = total.astype(out_ref.dtype)


def qkv_grads(xs, dqkv, near, far, far_x):
    rows, dim = xs[0].shape
    wide = dqkv.shape[2]
    return call(
        qkv_grads_kernel,
        "qkv_grads",
        [low_shape(dim, wide + wide // 3)],
        [VMEM] * 8,
        [],
        8 * rows * dim * wide,
        0,
        (*xs, dqkv, near, far, far_x),
    )[0]


def finish_kernel(tok_ref, grad_ref, b0, b1, b2, gain_ref, out_ref):
    rows = tok_ref.shape[0]
    for start in range(0, rows, BLK):
        span = slice(start, start + BLK)
        normed, inv_std = norm_stats(tok_ref[span].astype(jnp.float32))
        back = b0[span].astype(jnp.float32) + b1[span].astype(jnp.float32)
        back = back + b2[span].astype(jnp.float32)
        scaled = back * gain_ref[...]
        inner = scaled - jnp.mean(scaled, axis=-1, keepdims=True)
        inner = inner - normed * jnp.mean(scaled * normed, axis=-1, keepdims=True)
        out_ref[span] = grad_ref[span] + inner * inv_std


def finish(tokens, grad, backs, gain):
    rows, dim = tokens.shape
    return call(
        finish_kernel,
        "finish",
        [wide_shape(rows, dim)],
        [VMEM] * 6,
        [],
        rows * dim * 20,
        rows,
        (tokens, grad, *backs, gain),
    )[0]


def norm_kernel(t0, t1, t2, t3, gain_ref, o0, o1, o2, o3):
    rows = t0.shape[0]
    for src, out in ((t0, o0), (t1, o1), (t2, o2), (t3, o3)):
        for start in range(0, rows, BLK):
            span = slice(start, start + BLK)
            normed, _ = norm_stats(src[span].astype(jnp.float32))
            out[span] = (normed * gain_ref[...]).astype(out.dtype)


def norms(blocks, gain):
    rows, dim = blocks[0].shape
    return call(
        norm_kernel,
        "norms",
        [low_shape(rows, dim)] * 4,
        [VMEM] * 5,
        [],
        rows * dim * 40,
        rows,
        (*blocks, gain),
    )


def share_kernel(tail_ref, *outs):
    cols = outs[0].shape[1]
    for at, out in enumerate(outs):
        total = tail_ref[0, :, at * cols : (at + 1) * cols].astype(jnp.float32)
        for part in range(1, tail_ref.shape[0]):
            total = total + tail_ref[part, :, at * cols : (at + 1) * cols].astype(jnp.float32)
        out[...] = total


def shares(parts, cols, name):
    count, shard, wide = parts.shape
    return call(
        share_kernel,
        name,
        [wide_shape(shard, cols)] * (wide // cols),
        [VMEM],
        [],
        count * shard * wide,
        0,
        (parts,),
    )


def output_kernel(info_ref, resid_ref, b0, b1, b2, attn_sq, gain_one, gain_two, out_ref, small_ref):
    rows, dim = resid_ref.shape
    sum_final, sum_mlp = 0.0, 0.0
    for start in range(0, rows, BLK):
        span = slice(start, start + BLK)
        valid = valid_rows(info_ref, rows, start, BLK)
        mlp_out = b0[span].astype(jnp.float32) + b1[span].astype(jnp.float32)
        mlp_out = mlp_out + b2[span].astype(jnp.float32)
        final = resid_ref[span] + mlp_out
        out_ref[span] = final.astype(out_ref.dtype)
        sum_final = sum_final + row_sum(final * final * valid)
        sum_mlp = sum_mlp + row_sum(mlp_out * mlp_out * valid)
    count = jnp.clip(info_ref[1] - info_ref[0] * rows, 0, rows).astype(jnp.float32)
    lane = lax.broadcasted_iota(jnp.int32, (1, LANES), 1)
    parts = dim // LANES
    small_ref[...] = jnp.zeros_like(small_ref)
    for part in range(parts):
        span = slice(part * LANES, (part + 1) * LANES)
        small_ref[part : part + 1, :] = gain_one[:, span]
        small_ref[parts + part : parts + part + 1, :] = gain_two[:, span]
    row = jnp.where(lane == 3, count, 0.0)
    for at, square in enumerate((sum_final, attn_sq[...], sum_mlp)):
        row = jnp.where(lane == at, jnp.sum(square, axis=-1, keepdims=True), row)
    small_ref[2 * parts : 2 * parts + 1, :] = row


def output(info, resid, parts, sums):
    rows, dim = resid.shape
    return call(
        output_kernel,
        "output",
        [low_shape(rows, dim), wide_shape(-(-(2 * dim // LANES + 1) // 8) * 8, LANES)],
        [SMEM] + [VMEM] * 7,
        [],
        rows * dim * 10,
        0,
        (info, resid, *parts, *sums),
    )


X_SWAP = [(0, 2), (1, 3), (2, 0), (3, 1)]
CORE_SWAP = [(0, 1), (1, 0), (2, 3), (3, 2)]


def swap_x(v):
    return lax.ppermute(v, "tensor", X_SWAP)


def swap_core(v):
    return lax.ppermute(v, "tensor", CORE_SWAP)


def tied(value, *others):
    return lax.optimization_barrier((value, *others))[0]


def plus(a, b):
    return (a.astype(jnp.float32) + b.astype(jnp.float32)).astype(jnp.bfloat16)


def body(
    tokens,
    first_values,
    pieces,
    lengths,
    w_query,
    w_key,
    w_value,
    w_out,
    w_up,
    w_down,
    gain_attn,
    gain_mlp,
    cotangent,
):
    dp_size = lax.axis_size("dp")
    rank = lax.axis_index("tensor")
    core = rank % 2
    rows, dim = tokens.shape
    shard, cols = w_query.shape
    up_cols = w_up.shape[1]
    parity = lax.axis_index("dp") % 2
    info = jnp.concatenate(
        [rank[None].astype(jnp.int32), lengths, pieces[::BLK], parity[None].astype(jnp.int32)]
    )
    gain_one, gain_two = gain_attn[None], gain_mlp[None]
    pairs = [(i, i ^ 1) for i in range(dp_size)]
    lines = [list(range(first, dp_size, 2)) for first in range(2)]

    def gather_line(v):
        wide = jnp.broadcast_to(v[None], (dp_size // 2,) + v.shape)
        return lax.all_to_all(wide, "dp", 0, 0, axis_index_groups=lines)

    def swap_pair(v):
        return lax.ppermute(v, "dp", pairs)

    def in_order(mine, other):
        lower = jnp.where(parity == 0, mine, other)
        upper = jnp.where(parity == 0, other, mine)
        return jnp.stack([lower, upper], axis=1).reshape(dim, -1)

    def pieces_of(mine, other):
        if shard % 16 == 0:
            return (mine, other)
        return (in_order(mine, other)[None],)

    value_cols = jnp.where(core == 0, w_value[:, :cols], w_value[:, cols:])
    early = jnp.concatenate([w_query, w_key, value_cols], axis=1)
    late = jnp.concatenate([w_up, w_down.T, w_out.T], axis=1)
    early_mine = gather_line(early)
    tok_x = swap_x(tokens)
    tok_core = swap_core(tokens)
    late_mine = gather_line(tied(late, tok_core))
    early_other = swap_pair(early_mine)
    tok_diag = swap_core(tok_x)
    first_x = lax.ppermute(first_values, "tensor", [(0, 2), (1, 3)])
    firsts = (first_values, swap_core(first_values), first_x, swap_core(first_x))

    xs = norms((tokens, tok_core, tok_x, tok_diag), gain_one)
    qkv, early_all, o_first, lse_first = attend_first(
        info, xs, pieces_of(early_mine, early_other), firsts
    )

    cot_x = swap_x(tied(cotangent, tok_x, first_x))
    qkv, late_mine = lax.optimization_barrier((qkv, late_mine))
    late_other = swap_pair(late_mine[:, :, : 2 * up_cols])
    out_other = swap_pair(late_mine[:, :, 2 * up_cols :])
    h_own, h_core, h_pair, lse = attend_rest(info, qkv, firsts, o_first, lse_first)
    out_own = in_order(late_mine[:, :, 2 * up_cols :], out_other)
    out_x = swap_x(tied(out_own, cot_x))
    h_pair, h_core = lax.optimization_barrier((h_pair, h_core, cot_x, out_own))[:2]
    cot_core = swap_core(cotangent)
    cot_diag = swap_core(cot_x)
    outs = (out_own, swap_core(out_own), out_x, swap_core(out_x))

    from_x = swap_x(h_pair)
    heads_mine = (h_own, swap_core(h_core), from_x, swap_core(from_x))
    resid, mlp_in, attn_sq = middle(
        info, tied(tokens, late_other), heads_mine, outs, gain_two
    )
    in_x = swap_x(mlp_in)
    in_core = swap_core(mlp_in)
    late_all, hid_a, dup_a, back_own, back_core, out_0, out_1 = mlp_near(
        info,
        (mlp_in, in_core),
        (cotangent, cot_core),
        pieces_of(late_mine[:, :, : 2 * up_cols], late_other),
    )
    in_diag = swap_core(in_x)
    back_1 = swap_core(back_core)
    out_near = swap_core(out_1)
    in_far = tied(in_x, back_own)
    hid_b, dup_b, back_x, back_diag = mlp_far((in_far, in_diag), (cot_x, cot_diag), late_all)
    back_far = plus(back_x, swap_core(back_diag))
    back_2 = swap_x(back_far)
    grads_mlp, out_2, out_3 = mlp_grads(
        (mlp_in, in_core, in_x, in_diag),
        (cotangent, cot_core, cot_x, cot_diag),
        hid_a, tied(hid_b, back_far), dup_a, dup_b, late_all, up_cols,
    )
    mlp_parts = lax.all_to_all(grads_mlp.reshape(dp_size, shard, 2 * up_cols), "dp", 0, 0)
    out_sum = plus(out_2, swap_core(out_3))

    resid_grad, resid_low, d_own, d_core, d_pair, gain_two_sum = turn(
        resid, cotangent, (back_own, back_1, back_2), gain_two, outs
    )
    d_x = swap_x(d_pair)
    grads_heads = (d_own, swap_core(d_core), d_x, swap_core(d_x))
    near, far = out_grads(resid_low, heads_mine)
    far = swap_core(far)
    dqkv, dv_own, dv_core, dv_pair = attend_back(
        info, qkv, firsts, grads_heads, (h_own, h_core, h_pair), lse
    )
    out_from_x = swap_x(tied(out_sum, d_x))
    near_x = swap_x(tied(plus(near[dim:], far[dim:]), d_x))
    dqkv, dv_pair = lax.optimization_barrier((dqkv, dv_pair, out_from_x, near_x, mlp_parts))[:2]

    first_from_x = lax.ppermute(dv_pair, "tensor", [(2, 0), (3, 1)])
    tail = qkv_grads(xs, dqkv, near, far, near_x)
    tail_all = lax.all_to_all(tail.reshape(dp_size, shard, 4 * cols), "dp", 0, 0)
    b_0, b_1, b_2, b_3, gain_one_sum = input_grads(
        tied(dqkv, tail, first_from_x), early_all, xs, gain_one
    )
    b_far = plus(b_2, swap_core(b_3))
    b_from_x = swap_x(b_far)
    b_from_core = swap_core(b_1)

    final, small = output(
        info, tied(resid, b_far), (out_0, out_near, out_from_x), (attn_sq, gain_one_sum, gain_two_sum)
    )
    first_a = jnp.where(rank < 2, first_from_x[0], dv_own)
    first_b = swap_core(jnp.where(rank < 2, first_from_x[1], dv_core))
    first_grad = jnp.where(
        core == 0,
        jnp.concatenate([first_a, first_b], axis=1),
        jnp.concatenate([first_b, first_a], axis=1),
    ).astype(jnp.float32)
    token_grad = finish(tokens, resid_grad, (b_0, b_from_core, b_from_x), gain_one)
    grad_up, grad_down_t = shares(mlp_parts, up_cols, "mlp_shares")
    grad_q, grad_k, value_own, grad_out_t = shares(tail_all, cols, "tail_shares")
    value_x = lax.ppermute(value_own, "tensor", [(0, 2), (1, 3)])
    value_here = jnp.where(rank < 2, value_own, value_x)
    value_peer = swap_core(value_here)
    value_share = jnp.where(
        core == 0,
        jnp.concatenate([value_here, value_peer], axis=1),
        jnp.concatenate([value_peer, value_here], axis=1),
    )
    total = small
    for axis, size in (("tensor", 4), ("dp", dp_size)):
        step = 1
        while step < size:
            if axis == "dp" and step * 2 == size:
                total = tied(total, b_from_x)
            total = total + lax.ppermute(total, axis, [(i, i ^ step) for i in range(size)])
            step *= 2
    parts = dim // LANES
    square_total = total[2 * parts]
    rms = jnp.sqrt(square_total[:3] / (square_total[3] * dim))
    return (
        final,
        token_grad,
        first_grad,
        grad_q,
        grad_k,
        value_share,
        grad_out_t.T,
        grad_up,
        grad_down_t.T,
        total[:parts].reshape(dim),
        total[parts : 2 * parts].reshape(dim),
        rms,
    )


def solution(mesh):
    in_specs = (
        P(("dp", "tensor"), None),
        P(("dp", "tensor"), None),
        P("dp"),
        P("dp"),
        P("dp", "tensor"),
        P("dp", "tensor"),
        P("dp", None),
        P("tensor", "dp"),
        P("dp", "tensor"),
        P("tensor", "dp"),
        P(),
        P(),
        P(("dp", "tensor"), None),
    )
    out_specs = (
        P(("dp", "tensor"), None),
        P(("dp", "tensor"), None),
        P(("dp", "tensor"), None),
        P("dp", "tensor"),
        P("dp", "tensor"),
        P("dp", None),
        P("tensor", "dp"),
        P("dp", "tensor"),
        P("tensor", "dp"),
        P(),
        P(),
        P(),
    )
    return jax.shard_map(body, mesh=mesh, in_specs=in_specs, out_specs=out_specs, check_vma=False)
```

```python
import functools
import math

import jax
import jax.numpy as jnp
from jax import lax
from jax.experimental import pallas as pl
from jax.experimental.pallas import tpu as pltpu
from jax.sharding import PartitionSpec as P

HD = 64
EPS = 1e-05
NEG = -1e30
BLK = 256
LANES = 128

SMEM = pl.BlockSpec(memory_space=pltpu.SMEM)
VMEM = pl.BlockSpec(memory_space=pltpu.VMEM)


def nt(a, b):
    return lax.dot_general(a, b, (((1,), (1,)), ((), ())), preferred_element_type=jnp.float32)


def nn(a, b):
    return jnp.dot(a, b, preferred_element_type=jnp.float32)


def tn(a, b):
    return lax.dot_general(a, b, (((0,), (0,)), ((), ())), preferred_element_type=jnp.float32)


WEIGHTS = {"attend_back": 1.45, "output": 0.01, "mlp_shares": 0.01, "tail_shares": 0.01, "finish": 0.01}


def call(kernel, name, outs, specs, scratch, flops, exps, args, vmem=32):
    weight = WEIGHTS.get(name, 3.0)
    moved = sum(math.prod(v.shape) * v.dtype.itemsize for v in list(args) + list(outs))
    return pl.pallas_call(
        kernel,
        name=name,
        out_shape=tuple(outs),
        in_specs=specs,
        out_specs=tuple(VMEM for _ in outs),
        scratch_shapes=scratch,
        compiler_params=pltpu.CompilerParams(vmem_limit_bytes=vmem << 20),
        cost_estimate=pl.CostEstimate(
            flops=int(flops * weight),
            transcendentals=int(exps * weight),
            bytes_accessed=int(moved * weight),
        ),
    )(*args)


def low_shape(*shape):
    return jax.ShapeDtypeStruct(shape, jnp.bfloat16)


def wide_shape(*shape):
    return jax.ShapeDtypeStruct(shape, jnp.float32)


def loop(count, body):
    def step(tile, carry):
        body(pl.ds(pl.multiple_of(tile * BLK, BLK), BLK))
        return carry

    lax.fori_loop(0, count // BLK, step, 0)


def diag_allowed(picture, query_axis):
    query_pos = lax.broadcasted_iota(jnp.int32, (BLK, BLK), query_axis)
    key_pos = lax.broadcasted_iota(jnp.int32, (BLK, BLK), 1 - query_axis)
    return (key_pos <= query_pos) | (picture > 0)


def place(info_ref, rel, rows):
    return pl.multiple_of((info_ref[0] ^ rel) * rows, rows)


def assemble(dst_ref, parts, half):
    if len(parts) == 1:
        dst_ref[...] = parts[0][0]
        return
    mine, other = parts
    count, shard = mine.shape[:2]
    for part in range(count):
        dst_ref[pl.ds(pl.multiple_of((2 * part + half) * shard, shard), shard), :] = mine[part]
        dst_ref[pl.ds(pl.multiple_of((2 * part + 1 - half) * shard, shard), shard), :] = other[part]


def forward_head(head, slot, info_ref, q_aug, k_aug, v_aug, o_rows, lse_ref):
    seq = q_aug.shape[1]
    for block in range(seq // BLK):
        lo, hi = block * BLK, (block + 1) * BLK
        scores = nt(q_aug[head, lo:hi, :], k_aug[head, :hi, :])
        last = jnp.where(diag_allowed(info_ref[2 + block], 0), scores[:, lo:], NEG)
        row_max = jnp.max(last, axis=1, keepdims=True)
        if block:
            row_max = jnp.maximum(row_max, jnp.max(scores[:, :lo], axis=1, keepdims=True))
        acc = nn(jnp.exp(last - row_max).astype(jnp.bfloat16), v_aug[head, lo:hi, :])
        if block:
            front = jnp.exp(scores[:, :lo] - row_max).astype(jnp.bfloat16)
            acc = acc + nn(front, v_aug[head, :lo, :])
        total = acc[:, HD : HD + 1]
        o_rows[slot, lo:hi, :] = (acc[:, :HD] / total).astype(o_rows.dtype)
        lse = row_max + jnp.log(total)
        lse_ref[slot, :, lo:hi] = jnp.broadcast_to(lse, (BLK, LANES)).T[:1]


def first_kernel(info_ref, x0, x1, x2, x3, f0, f1, f2, f3, *refs):
    *parts, w_ref, out_w, q_aug, k_aug, v_aug, k_t, o_rows, lse_ref = refs
    inputs, firsts = (x0, x1, x2, x3), (f0, f1, f2, f3)
    rows = x0.shape[0]
    seq = 4 * rows
    heads = q_aug.shape[0]
    cols = heads * HD
    rank = info_ref[0]
    assemble(w_ref, parts, info_ref[2 + seq // BLK])
    out_w[...] = w_ref[:, 3 * cols :]
    lane = lax.broadcasted_iota(jnp.int32, (seq, HD), 1)
    pos = lax.broadcasted_iota(jnp.int32, (seq, HD), 0)
    bias = jnp.where((lane == 0) & (pos >= info_ref[1]), NEG, 0.0).astype(jnp.bfloat16)
    one = jnp.where(lane == 0, 1.0, 0.0).astype(jnp.bfloat16)
    ones = jnp.where(lane < 3, 1.0, 0.0).astype(jnp.bfloat16)
    for head in range(heads):
        q_aug[head, :, HD:] = one
        k_aug[head, :, HD:] = bias
        v_aug[head, :, HD:] = ones
    for rel in range(4):
        span = pl.ds(place(info_ref, rel, rows), rows)
        part = nn(inputs[rel][...], w_ref[:, : 3 * cols])
        for head in range(heads):
            at = head * HD
            q_aug[head, span, :HD] = part[:, at : at + HD].astype(jnp.bfloat16) * jnp.bfloat16(
                1.0 / math.sqrt(HD)
            )
            keys = part[:, cols + at : cols + at + HD].astype(jnp.bfloat16)
            k_aug[head, span, :HD] = keys
            k_t[head, :, span] = keys.T
            reused = jnp.where(
                rank % 2 == 0, firsts[rel][:, at : at + HD], firsts[rel][:, cols + at : cols + at + HD]
            )
            fresh = part[:, 2 * cols + at : 2 * cols + at + HD].astype(jnp.bfloat16)
            v_aug[head, span, :HD] = jnp.where(rank < 2, fresh, reused)
    forward_head(0, 0, info_ref, q_aug, k_aug, v_aug, o_rows, lse_ref)


def attend_first(info, inputs, parts, firsts, cols):
    rows, dim = inputs[0].shape
    wide = parts[0].shape[2]
    heads = cols // HD
    seq = 4 * rows
    work = seq * (seq + BLK) // 2
    return call(
        first_kernel,
        "attend_first",
        [
            low_shape(dim, wide),
            low_shape(dim, cols),
            low_shape(heads, seq, 2 * HD),
            low_shape(heads, seq, 2 * HD),
            low_shape(heads, seq, 2 * HD),
            low_shape(heads, HD, seq),
            low_shape(1, seq, HD),
            wide_shape(1, 1, seq),
        ],
        [SMEM] + [VMEM] * (8 + len(parts)),
        [],
        16 * work * HD + 2 * seq * dim * wide,
        work,
        (info, *inputs, *firsts, *parts),
    )


def rest_kernel(
    info_ref, q_aug, k_aug, v_aug, o_first, lse_first, own_ref, core_ref, pair_ref, lse_ref, o_rows, lse_part
):
    rows, cols = own_ref.shape
    heads = cols // HD

    def per_head(head, carry):
        forward_head(head + 1, head, info_ref, q_aug, k_aug, v_aug, o_rows, lse_part)
        return carry

    lax.fori_loop(0, heads - 1, per_head, 0)
    lse_ref[0] = lse_first[0]
    for head in range(1, heads):
        lse_ref[head] = lse_part[head - 1]
    for rel, out in enumerate((own_ref, core_ref, pair_ref.at[0], pair_ref.at[1])):
        span = pl.ds(place(info_ref, rel, rows), rows)
        out[:, :HD] = o_first[0, span, :]
        for head in range(1, heads):
            out[:, head * HD : (head + 1) * HD] = o_rows[head - 1, span, :]


def attend_rest(info, q_aug, k_aug, v_aug, o_first, lse_first):
    heads, seq = q_aug.shape[:2]
    rows, cols = seq // 4, heads * HD
    work = (heads - 1) * seq * (seq + BLK) // 2
    return call(
        rest_kernel,
        "attend_rest",
        [
            low_shape(rows, cols),
            low_shape(rows, cols),
            low_shape(2, rows, cols),
            wide_shape(heads, 1, seq),
        ],
        [SMEM] + [VMEM] * 5,
        [pltpu.VMEM((heads - 1, seq, HD), jnp.bfloat16), pltpu.VMEM((heads - 1, 1, seq), jnp.float32)],
        16 * work * HD,
        work,
        (info, q_aug, k_aug, v_aug, o_first, lse_first),
    )


def backward_kernel(
    info_ref, q_aug, k_aug, v_aug, k_t, g0, g1, g2, g3, own_ref, core_ref, pair_ref, lse_ref,
    dqkv_ref, dv_own, dv_core, dv_pair, g_aug, dq_t, dk_acc, dv_acc,
):
    grads, outs = (g0, g1, g2.at[0], g3.at[1]), (own_ref, core_ref, pair_ref.at[0], pair_ref.at[1])
    dv_outs = (dv_own, dv_core, dv_pair.at[0], dv_pair.at[1])
    rows, cols = own_ref.shape
    heads, seq = q_aug.shape[:2]
    lane = lax.broadcasted_iota(jnp.int32, (rows, HD), 1)
    for head in range(heads):
        at = head * HD
        for rel in range(4):
            span = pl.ds(place(info_ref, rel, rows), rows)
            grad = grads[rel][:, at : at + HD]
            g_aug[head, span, :HD] = grad
            products = grad.astype(jnp.float32) * outs[rel][:, at : at + HD].astype(jnp.float32)
            left = -jnp.sum(products, axis=1, keepdims=True)
            part = jnp.zeros((rows, HD), jnp.bfloat16)
            for piece in range(3):
                low = left.astype(jnp.bfloat16)
                part = jnp.where(lane == piece, low, part)
                left = left - low.astype(jnp.float32)
            g_aug[head, span, HD:] = part

    def per_head(head, carry):
        for block in range(seq // BLK):
            lo, hi = block * BLK, (block + 1) * BLK
            probs = jnp.exp(nt(k_aug[head, lo:hi, :], q_aug[head, lo:, :]) - lse_ref[head, :, lo:])
            first = jnp.where(diag_allowed(info_ref[2 + block], 1), probs[:, :BLK], 0.0)
            probs = first if hi == seq else jnp.concatenate([first, probs[:, BLK:]], axis=1)
            grad_probs = nt(v_aug[head, lo:hi, :], g_aug[head, lo:, :])
            grad_scores = (probs * grad_probs).astype(jnp.bfloat16)
            dv_acc[head, lo:hi, :] = nn(probs.astype(jnp.bfloat16), g_aug[head, lo:, :])[:, :HD].astype(
                jnp.bfloat16
            )
            dk_acc[head, lo:hi, :] = nn(grad_scores, q_aug[head, lo:, :])[:, :HD].astype(jnp.bfloat16)
            part = nn(k_t[head, :, lo:hi], grad_scores)
            if block:
                dq_t[head, :, lo:] += part
            else:
                dq_t[head, :, :] = part
        return carry

    lax.fori_loop(0, heads, per_head, 0)
    fresh = info_ref[0] < 2
    for rel in range(4):
        span = pl.ds(place(info_ref, rel, rows), rows)
        part = dq_t[:, :, span].reshape(cols, rows)
        dqkv_ref[rel, :, :cols] = (part.T * (1.0 / math.sqrt(HD))).astype(dqkv_ref.dtype)
        for head in range(heads):
            at = head * HD
            dqkv_ref[rel, :, cols + at : cols + at + HD] = dk_acc[head, span, :]
            value = dv_acc[head, span, :]
            dv_outs[rel][:, at : at + HD] = value
            kept = jnp.where(fresh, value, jnp.zeros_like(value))
            dqkv_ref[rel, :, 2 * cols + at : 2 * cols + at + HD] = kept


def attend_back(info, prepared, grads, outs, lse):
    heads, seq = prepared[0].shape[:2]
    rows, cols = seq // 4, heads * HD
    work = heads * seq * (seq + BLK) // 2
    return call(
        backward_kernel,
        "attend_back",
        [
            low_shape(4, rows, 3 * cols),
            low_shape(rows, cols),
            low_shape(rows, cols),
            low_shape(2, rows, cols),
        ],
        [SMEM] + [VMEM] * 12,
        [
            pltpu.VMEM((heads, seq, 2 * HD), jnp.bfloat16),
            pltpu.VMEM((heads, HD, seq), jnp.float32),
            pltpu.VMEM((heads, seq, HD), jnp.bfloat16),
            pltpu.VMEM((heads, seq, HD), jnp.bfloat16),
        ],
        40 * work * HD,
        work,
        (info, *prepared, *grads, *outs, lse),
        48,
    )


def norm_stats(wide):
    centred = wide - jnp.mean(wide, axis=-1, keepdims=True)
    inv_std = lax.rsqrt(jnp.mean(centred * centred, axis=-1, keepdims=True) + EPS)
    return centred * inv_std, inv_std


def valid_rows(info_ref, rows, start, count):
    pos = info_ref[0] * rows + start + lax.broadcasted_iota(jnp.int32, (count, 1), 0)
    return (pos < info_ref[1]).astype(jnp.float32)


def row_sum(v):
    return jnp.sum(v, axis=0, keepdims=True)


def middle_kernel(
    info_ref, tok_ref, h0, h1, h2, h3, w0, w1, w2, w3, gain_ref, resid_ref, input_ref, square_ref
):
    rows = tok_ref.shape[0]
    square_ref[...] = jnp.zeros_like(square_ref)

    def tile(span):
        attn = nt(h0[span], w0[...]) + nt(h1[span], w1[...])
        attn = attn + nt(h2[0, span], w2[...]) + nt(h3[1, span], w3[...])
        resid = tok_ref[span].astype(jnp.float32) + attn
        resid_ref[span] = resid
        normed, _ = norm_stats(resid)
        input_ref[span] = (normed * gain_ref[...]).astype(input_ref.dtype)
        square_ref[...] += row_sum(attn * attn * valid_rows(info_ref, rows, span.start, BLK))

    loop(rows, tile)


def middle(info, tokens, heads, weights, gain):
    rows, dim = tokens.shape
    return call(
        middle_kernel,
        "middle",
        [wide_shape(rows, dim), low_shape(rows, dim), wide_shape(1, dim)],
        [SMEM] + [VMEM] * 10,
        [],
        2 * rows * dim * dim,
        rows,
        (info, tokens, *heads, *weights, gain),
    )


GELU_C = math.sqrt(2.0 / math.pi)
CUBE = 0.044715


def mlp_tiles(xs, cots, w_ref, hid_ref, dup_ref, backs, outs):
    rows = xs[0].shape[0]
    up_cols = w_ref.shape[1] // 2
    up_w, down_t = w_ref.at[:, :up_cols], w_ref.at[:, up_cols:]
    for block in range(2):

        def tile(span, block=block):
            up = nn(xs[block][span], up_w[...])
            up2 = up * up
            th = jnp.tanh(GELU_C * up * (1.0 + CUBE * up2))
            half = 0.5 * (1.0 + th)
            hidden = (up * half).astype(jnp.bfloat16)
            hid_ref[block, span] = hidden
            slope = half + 0.5 * up * (1.0 - th * th) * (GELU_C * (1.0 + 3.0 * CUBE * up2))
            dup = (nn(cots[block][span], down_t[...]) * slope).astype(jnp.bfloat16)
            dup_ref[block, span] = dup
            backs[block][span] = nt(dup, up_w[...]).astype(jnp.bfloat16)
            if outs:
                outs[block][span] = nt(hidden, down_t[...]).astype(jnp.bfloat16)

        loop(rows, tile)


def mlp_near_kernel(info_ref, x0, x1, c0, c1, *refs):
    *parts, w_ref, hid_ref, dup_ref, b0, b1, o0, o1 = refs
    assemble(w_ref, parts, info_ref[2 + 4 * x0.shape[0] // BLK])
    mlp_tiles((x0, x1), (c0, c1), w_ref, hid_ref, dup_ref, (b0, b1), (o0, o1))


def mlp_far_kernel(x0, x1, c0, c1, w_ref, hid_ref, dup_ref, b0, b1):
    mlp_tiles((x0, x1), (c0, c1), w_ref, hid_ref, dup_ref, (b0, b1), ())


def mlp_near(info, xs, cots, parts):
    rows, dim = xs[0].shape
    wide = parts[0].shape[2]
    return call(
        mlp_near_kernel,
        "mlp_near",
        [low_shape(dim, wide)] + [low_shape(2, rows, wide // 2)] * 2 + [low_shape(rows, dim)] * 4,
        [SMEM] + [VMEM] * (4 + len(parts)),
        [],
        8 * rows * dim * wide,
        rows * wide,
        (info, *xs, *cots, *parts),
    )


def mlp_far(xs, cots, weights):
    rows, dim = xs[0].shape
    wide = weights.shape[1]
    return call(
        mlp_far_kernel,
        "mlp_far",
        [low_shape(2, rows, wide // 2)] * 2 + [low_shape(rows, dim)] * 2,
        [VMEM] * 5,
        [],
        6 * rows * dim * wide,
        rows * wide,
        (*xs, *cots, weights),
    )


def mlp_grads_kernel(up_cols, x0, x1, x2, x3, c0, c1, c2, c3, h_a, h_b, d_a, d_b, w_ref, g_ref, o0, o1):
    down_t = w_ref.at[:, up_cols : 2 * up_cols]
    step = 2 * BLK
    for rel, out in ((0, o0), (1, o1)):
        out[...] = nt(h_b[rel], down_t[...]).astype(out.dtype)
    for start in range(0, up_cols, BLK):
        span = slice(start, start + BLK)
        acc = tn(x0[...], d_a[0, :, span]) + tn(x1[...], d_a[1, :, span])
        acc = acc + tn(x2[...], d_b[0, :, span]) + tn(x3[...], d_b[1, :, span])
        g_ref[:, span] = acc.astype(g_ref.dtype)
        acc = tn(c0[...], h_a[0, :, span]) + tn(c1[...], h_a[1, :, span])
        acc = acc + tn(c2[...], h_b[0, :, span]) + tn(c3[...], h_b[1, :, span])
        g_ref[:, up_cols + start : up_cols + start + BLK] = acc.astype(g_ref.dtype)


def mlp_grads(xs, cots, hid_a, hid_b, dup_a, dup_b, weights, up_cols):
    rows, dim = xs[0].shape
    return call(
        functools.partial(mlp_grads_kernel, up_cols),
        "mlp_grads",
        [low_shape(dim, 2 * up_cols), low_shape(rows, dim), low_shape(rows, dim)],
        [VMEM] * 13,
        [],
        20 * rows * dim * up_cols,
        0,
        (*xs, *cots, hid_a, hid_b, dup_a, dup_b, weights),
    )


def turn_kernel(
    resid_ref, cot_ref, b0, b1, b2, gain_ref, w0, w1, w2, w3,
    grad_ref, low_ref, d_own, d_core, d_pair, gain_out,
):
    rows = resid_ref.shape[0]
    gain_out[...] = jnp.zeros_like(gain_out)

    def tile(span):
        normed, inv_std = norm_stats(resid_ref[span])
        back = b0[span].astype(jnp.float32) + b1[span].astype(jnp.float32)
        back = back + b2[span].astype(jnp.float32)
        gain_out[...] += row_sum(back * normed)
        scaled = back * gain_ref[...]
        inner = scaled - jnp.mean(scaled, axis=-1, keepdims=True)
        inner = inner - normed * jnp.mean(scaled * normed, axis=-1, keepdims=True)
        grad = cot_ref[span].astype(jnp.float32) + inner * inv_std
        grad_ref[span] = grad
        low = grad.astype(jnp.bfloat16)
        low_ref[span] = low
        d_own[span] = nn(low, w0[...]).astype(jnp.bfloat16)
        d_core[span] = nn(low, w1[...]).astype(jnp.bfloat16)
        d_pair[0, span] = nn(low, w2[...]).astype(jnp.bfloat16)
        d_pair[1, span] = nn(low, w3[...]).astype(jnp.bfloat16)

    loop(rows, tile)


def turn(resid, cot, backs, gain, weights):
    rows, dim = cot.shape
    cols = weights[0].shape[1]
    return call(
        turn_kernel,
        "turn",
        [
            wide_shape(rows, dim),
            low_shape(rows, dim),
            low_shape(rows, cols),
            low_shape(rows, cols),
            low_shape(2, rows, cols),
            wide_shape(1, dim),
        ],
        [VMEM] * 10,
        [],
        2 * rows * dim * dim,
        rows,
        (resid, cot, *backs, gain, *weights),
    )


def out_grads_kernel(low_ref, h0, h1, h2, h3, o_near, o_far):
    cols = h0.shape[1]
    low = low_ref[...]
    o_near[:, :cols] = tn(low, h0[...])
    o_far[:, :cols] = tn(low, h1[...]).astype(jnp.bfloat16)
    o_near[:, cols:] = tn(low, h2[0])
    o_far[:, cols:] = tn(low, h3[1]).astype(jnp.bfloat16)


def out_grads(low, heads):
    rows, dim = low.shape
    cols = heads[0].shape[1]
    return call(
        out_grads_kernel,
        "out_grads",
        [wide_shape(dim, 2 * cols), low_shape(dim, 2 * cols)],
        [VMEM] * 5,
        [],
        2 * rows * dim * dim,
        0,
        (low, *heads),
    )


def slot_sum_kernel(near_ref, far_ref, out_ref):
    cols = out_ref.shape[1]
    out_ref[...] = (near_ref[:, cols:] + far_ref[:, cols:].astype(jnp.float32)).astype(out_ref.dtype)


def slot_sum(near, far):
    dim, wide = near.shape
    return call(
        slot_sum_kernel, "slot_sum", [low_shape(dim, wide // 2)], [VMEM] * 2, [], dim * wide, 0, (near, far)
    )[0]


def input_grads_kernel(dqkv_ref, w_ref, x0, x1, x2, x3, gain_ref, o0, o1, o2, o3, gain_out):
    rows = x0.shape[0]
    wide = dqkv_ref.shape[2]
    gain_out[...] = jnp.zeros_like(gain_out)
    for rel, x_ref, out in ((2, x2, o2), (3, x3, o3), (0, x0, o0), (1, x1, o1)):

        def tile(span, rel=rel, x_ref=x_ref, out=out):
            part = nt(dqkv_ref[rel, span], w_ref[:, :wide])
            out[span] = part.astype(out.dtype)
            gain_out[...] += row_sum(part * x_ref[span].astype(jnp.float32))

        loop(rows, tile)
    gain_out[...] = gain_out[...] / gain_ref[...]


def input_grads(dqkv, weights, xs, gain):
    rows, cols = dqkv.shape[1:]
    dim = weights.shape[0]
    return call(
        input_grads_kernel,
        "input_grads",
        [low_shape(rows, dim)] * 4 + [wide_shape(1, dim)],
        [VMEM] * 7,
        [],
        8 * rows * dim * cols,
        0,
        (dqkv, weights, *xs, gain),
    )


def qkv_grads_kernel(x0, x1, x2, x3, dqkv_ref, near_ref, far_ref, far_x, out_ref):
    wide = dqkv_ref.shape[2]
    acc = tn(x0[...], dqkv_ref[0]) + tn(x1[...], dqkv_ref[1])
    acc = acc + tn(x2[...], dqkv_ref[2]) + tn(x3[...], dqkv_ref[3])
    out_ref[:, :wide] = acc.astype(out_ref.dtype)
    cols = wide // 3
    total = near_ref[:, :cols] + far_ref[:, :cols].astype(jnp.float32)
    total = total + far_x[...].astype(jnp.float32)
    out_ref[:, wide:] = total.astype(out_ref.dtype)


def qkv_grads(xs, dqkv, near, far, far_x):
    rows, dim = xs[0].shape
    wide = dqkv.shape[2]
    return call(
        qkv_grads_kernel,
        "qkv_grads",
        [low_shape(dim, wide + wide // 3)],
        [VMEM] * 8,
        [],
        8 * rows * dim * wide,
        0,
        (*xs, dqkv, near, far, far_x),
    )[0]


def finish_kernel(tok_ref, grad_ref, b0, b1, b2, gain_ref, out_ref):

    def tile(span):
        normed, inv_std = norm_stats(tok_ref[span].astype(jnp.float32))
        back = b0[span].astype(jnp.float32) + b1[span].astype(jnp.float32)
        back = back + b2[span].astype(jnp.float32)
        scaled = back * gain_ref[...]
        inner = scaled - jnp.mean(scaled, axis=-1, keepdims=True)
        inner = inner - normed * jnp.mean(scaled * normed, axis=-1, keepdims=True)
        out_ref[span] = grad_ref[span] + inner * inv_std

    loop(tok_ref.shape[0], tile)


def finish(tokens, grad, backs, gain):
    rows, dim = tokens.shape
    return call(
        finish_kernel,
        "finish",
        [wide_shape(rows, dim)],
        [VMEM] * 6,
        [],
        rows * dim * 20,
        rows,
        (tokens, grad, *backs, gain),
    )[0]


def norm_kernel(t0, t1, gain_ref, o0, o1):
    for src, out in ((t0, o0), (t1, o1)):

        def tile(span, src=src, out=out):
            normed, _ = norm_stats(src[span].astype(jnp.float32))
            out[span] = (normed * gain_ref[...]).astype(out.dtype)

        loop(t0.shape[0], tile)


def norms(blocks, gain):
    rows, dim = blocks[0].shape
    return call(
        norm_kernel,
        "norms",
        [low_shape(rows, dim)] * 2,
        [VMEM] * 3,
        [],
        rows * dim * 20,
        rows,
        (*blocks, gain),
    )


def share_kernel(tail_ref, *outs):
    cols = outs[0].shape[1]
    for at, out in enumerate(outs):
        total = tail_ref[0, :, at * cols : (at + 1) * cols].astype(jnp.float32)
        for part in range(1, tail_ref.shape[0]):
            total = total + tail_ref[part, :, at * cols : (at + 1) * cols].astype(jnp.float32)
        out[...] = total


def shares(parts, cols, name):
    count, shard, wide = parts.shape
    return call(
        share_kernel,
        name,
        [wide_shape(shard, cols)] * (wide // cols),
        [VMEM],
        [],
        count * shard * wide,
        0,
        (parts,),
    )


def output_kernel(info_ref, resid_ref, b0, b1, b2, attn_sq, gain_one, gain_two, out_ref, small_ref, *sums):
    rows, dim = resid_ref.shape
    final_sum, mlp_sum = sums
    final_sum[...] = jnp.zeros_like(final_sum)
    mlp_sum[...] = jnp.zeros_like(mlp_sum)

    def tile(span):
        valid = valid_rows(info_ref, rows, span.start, BLK)
        mlp_out = b0[span].astype(jnp.float32) + b1[span].astype(jnp.float32)
        mlp_out = mlp_out + b2[span].astype(jnp.float32)
        final = resid_ref[span] + mlp_out
        out_ref[span] = final.astype(out_ref.dtype)
        final_sum[...] += row_sum(final * final * valid)
        mlp_sum[...] += row_sum(mlp_out * mlp_out * valid)

    loop(rows, tile)
    count = jnp.clip(info_ref[1] - info_ref[0] * rows, 0, rows).astype(jnp.float32)
    lane = lax.broadcasted_iota(jnp.int32, (1, LANES), 1)
    parts = dim // LANES
    small_ref[...] = jnp.zeros_like(small_ref)
    for part in range(parts):
        span = slice(part * LANES, (part + 1) * LANES)
        small_ref[part : part + 1, :] = gain_one[:, span]
        small_ref[parts + part : parts + part + 1, :] = gain_two[:, span]
    row = jnp.where(lane == 3, count, 0.0)
    for at, square in enumerate((final_sum[...], attn_sq[...], mlp_sum[...])):
        row = jnp.where(lane == at, jnp.sum(square, axis=-1, keepdims=True), row)
    small_ref[2 * parts : 2 * parts + 1, :] = row


def output(info, resid, parts, sums):
    rows, dim = resid.shape
    return call(
        output_kernel,
        "output",
        [low_shape(rows, dim), wide_shape(-(-(2 * dim // LANES + 1) // 8) * 8, LANES)],
        [SMEM] + [VMEM] * 7,
        [pltpu.VMEM((1, dim), jnp.float32)] * 2,
        rows * dim * 10,
        0,
        (info, resid, *parts, *sums),
    )


def pack_early_kernel(info_ref, wq, wk, wv, wo, out_ref):
    cols = wq.shape[1]
    even = info_ref[0] % 2 == 0
    fresh = jnp.where(even, wv[:, :cols], wv[:, cols : 2 * cols])
    turned = wo[...].T
    for part in range(out_ref.shape[0]):
        for at, value in enumerate((wq[...], wk[...], fresh, turned)):
            out_ref[part, :, at * cols : (at + 1) * cols] = value


def pack_late_kernel(up_ref, down_ref, out_ref):
    cols = up_ref.shape[1]
    for part in range(out_ref.shape[0]):
        out_ref[part, :, :cols] = up_ref[...]
        out_ref[part, :, cols:] = down_ref[...]


def pack_early(info, copies, wq, wk, wv, wo):
    shard, cols = wq.shape
    return call(
        pack_early_kernel, "pack_early", [low_shape(copies, shard, 4 * cols)],
        [SMEM] + [VMEM] * 4, [], shard * cols, 0, (info, wq, wk, wv, wo),
    )[0]


def pack_late(copies, up, down_t):
    shard, cols = up.shape
    return call(
        pack_late_kernel, "pack_late", [low_shape(copies, shard, 2 * cols)],
        [VMEM] * 2, [], shard * cols, 0, (up, down_t),
    )[0]


X_SWAP = [(0, 2), (1, 3), (2, 0), (3, 1)]
CORE_SWAP = [(0, 1), (1, 0), (2, 3), (3, 2)]


def swap_x(v):
    return lax.ppermute(v, "tensor", X_SWAP)


def swap_core(v):
    return lax.ppermute(v, "tensor", CORE_SWAP)


def tied(value, *others):
    return lax.optimization_barrier((value, *others))[0]


def plus(a, b):
    return (a.astype(jnp.float32) + b.astype(jnp.float32)).astype(jnp.bfloat16)


def body(
    tokens,
    first_values,
    pieces,
    lengths,
    w_query,
    w_key,
    w_value,
    w_out,
    w_up,
    w_down,
    gain_attn,
    gain_mlp,
    cotangent,
):
    dp_size = lax.axis_size("dp")
    rank = lax.axis_index("tensor")
    core = rank % 2
    rows, dim = tokens.shape
    shard, cols = w_query.shape
    up_cols = w_up.shape[1]
    parity = lax.axis_index("dp") % 2
    info = jnp.concatenate(
        [rank[None].astype(jnp.int32), lengths, pieces[::BLK], parity[None].astype(jnp.int32)]
    )
    gain_one, gain_two = gain_attn[None], gain_mlp[None]
    pairs = [(i, i ^ 1) for i in range(dp_size)]
    lines = [list(range(first, dp_size, 2)) for first in range(2)]

    def gather_line(v):
        return lax.all_to_all(v, "dp", 0, 0, axis_index_groups=lines)

    def swap_pair(v):
        return lax.ppermute(v, "dp", pairs)

    def in_order(mine, other):
        lower = jnp.where(parity == 0, mine, other)
        upper = jnp.where(parity == 0, other, mine)
        return jnp.stack([lower, upper], axis=1).reshape(dim, -1)

    def pieces_of(mine, other):
        if shard % 16 == 0:
            return (mine, other)
        return (in_order(mine, other)[None],)

    early = pack_early(info, dp_size // 2, w_query, w_key, w_value, w_out)
    late = pack_late(dp_size // 2, w_up, w_down.T)
    early_mine = gather_line(early)
    tok_x = swap_x(tokens)
    tok_core = swap_core(tokens)
    xs_near = norms((tokens, tok_core), gain_one)
    early_other = swap_pair(early_mine)
    tok_diag = swap_core(tok_x)
    late_mine = gather_line(tied(late, tok_diag))
    first_x = lax.ppermute(first_values, "tensor", [(0, 2), (1, 3)])
    firsts = (first_values, swap_core(first_values), first_x, swap_core(first_x))
    xs = (*xs_near, *norms((tok_x, tok_diag), gain_one))
    early_all, out_own, *prepared, o_first, lse_first = attend_first(
        info, xs, pieces_of(early_mine, early_other), firsts, cols
    )

    out_x = swap_x(out_own)
    cot_x = swap_x(tied(cotangent, first_x, out_own))
    o_first, late_mine = lax.optimization_barrier((o_first, late_mine))
    late_other = swap_pair(late_mine)
    h_own, h_core, h_pair, lse = attend_rest(info, *prepared[:3], o_first, lse_first)
    h_pair, h_core = lax.optimization_barrier((h_pair, h_core, cot_x, out_x))[:2]
    cot_core = swap_core(cotangent)
    cot_diag = swap_core(cot_x)
    outs = (out_own, swap_core(out_own), out_x, swap_core(out_x))

    from_x = swap_x(h_pair)
    heads_mine = (h_own, swap_core(h_core), from_x, swap_core(from_x))
    resid, mlp_in, attn_sq = middle(
        info, tied(tokens, late_other), heads_mine, outs, gain_two
    )
    in_x = swap_x(mlp_in)
    in_core = swap_core(mlp_in)
    late_all, hid_a, dup_a, back_own, back_core, out_0, out_1 = mlp_near(
        info,
        (mlp_in, in_core),
        (cotangent, cot_core),
        pieces_of(late_mine, late_other),
    )
    back_1 = swap_core(back_core)
    out_near = swap_core(out_1)
    in_far = tied(in_x, back_own)
    in_diag = swap_core(in_far)
    hid_b, dup_b, back_x, back_diag = mlp_far((in_far, in_diag), (cot_x, cot_diag), late_all)
    back_far = plus(back_x, swap_core(back_diag))
    back_2 = swap_x(back_far)
    grads_mlp, out_2, out_3 = mlp_grads(
        (mlp_in, in_core, in_x, in_diag),
        (cotangent, cot_core, cot_x, cot_diag),
        hid_a, tied(hid_b, back_far), dup_a, dup_b, late_all, up_cols,
    )
    mlp_parts = lax.all_to_all(grads_mlp.reshape(dp_size, shard, 2 * up_cols), "dp", 0, 0)
    out_sum = plus(out_2, swap_core(out_3))

    resid_grad, resid_low, d_own, d_core, d_pair, gain_two_sum = turn(
        resid, cotangent, (back_own, back_1, back_2), gain_two, outs
    )
    d_x = swap_x(d_pair)
    grads_heads = (d_own, swap_core(d_core), d_x, swap_core(d_x))
    near, far = out_grads(resid_low, heads_mine)
    far = swap_core(far)
    dqkv, dv_own, dv_core, dv_pair = attend_back(
        info, prepared, grads_heads, (h_own, h_core, h_pair), lse
    )
    out_from_x = swap_x(tied(out_sum, d_x))
    near_x = swap_x(tied(slot_sum(near, far), d_x))
    dqkv, dv_pair = lax.optimization_barrier((dqkv, dv_pair, out_from_x, near_x, mlp_parts))[:2]

    first_from_x = lax.ppermute(dv_pair, "tensor", [(2, 0), (3, 1)])
    tail = qkv_grads(xs, dqkv, near, far, near_x)
    tail_all = lax.all_to_all(tail.reshape(dp_size, shard, 4 * cols), "dp", 0, 0)
    b_0, b_1, b_2, b_3, gain_one_sum = input_grads(
        tied(dqkv, tail, first_from_x), early_all, xs, gain_one
    )
    b_far = plus(b_2, swap_core(b_3))
    b_from_x = swap_x(b_far)
    b_from_core = swap_core(b_1)

    final, small = output(
        info, tied(resid, b_far), (out_0, out_near, out_from_x), (attn_sq, gain_one_sum, gain_two_sum)
    )
    first_a = jnp.where(rank < 2, first_from_x[0], dv_own)
    first_b = swap_core(jnp.where(rank < 2, first_from_x[1], dv_core))
    first_grad = jnp.where(
        core == 0,
        jnp.concatenate([first_a, first_b], axis=1),
        jnp.concatenate([first_b, first_a], axis=1),
    ).astype(jnp.float32)
    token_grad = finish(tokens, resid_grad, (b_0, b_from_core, b_from_x), gain_one)
    total = small
    for axis, size in (("tensor", 4), ("dp", dp_size)):
        step = 1
        while step < size:
            if axis == "dp" and step * 2 == size:
                total = tied(total, token_grad)
            total = total + lax.ppermute(total, axis, [(i, i ^ step) for i in range(size)])
            step *= 2
    grad_up, grad_down_t = shares(mlp_parts, up_cols, "mlp_shares")
    grad_q, grad_k, value_own, grad_out_t = shares(tail_all, cols, "tail_shares")
    value_x = lax.ppermute(value_own, "tensor", [(0, 2), (1, 3)])
    value_here = jnp.where(rank < 2, value_own, value_x)
    value_peer = swap_core(value_here)
    value_share = jnp.where(
        core == 0,
        jnp.concatenate([value_here, value_peer], axis=1),
        jnp.concatenate([value_peer, value_here], axis=1),
    )
    parts = dim // LANES
    square_total = total[2 * parts]
    rms = jnp.sqrt(square_total[:3] / (square_total[3] * dim))
    return (
        final,
        token_grad,
        first_grad,
        grad_q,
        grad_k,
        value_share,
        grad_out_t.T,
        grad_up,
        grad_down_t.T,
        total[:parts].reshape(dim),
        total[parts : 2 * parts].reshape(dim),
        rms,
    )


def solution(mesh):
    in_specs = (
        P(("dp", "tensor"), None),
        P(("dp", "tensor"), None),
        P("dp"),
        P("dp"),
        P("dp", "tensor"),
        P("dp", "tensor"),
        P("dp", None),
        P("tensor", "dp"),
        P("dp", "tensor"),
        P("tensor", "dp"),
        P(),
        P(),
        P(("dp", "tensor"), None),
    )
    out_specs = (
        P(("dp", "tensor"), None),
        P(("dp", "tensor"), None),
        P(("dp", "tensor"), None),
        P("dp", "tensor"),
        P("dp", "tensor"),
        P("dp", None),
        P("tensor", "dp"),
        P("dp", "tensor"),
        P("tensor", "dp"),
        P(),
        P(),
        P(),
    )
    return jax.shard_map(body, mesh=mesh, in_specs=in_specs, out_specs=out_specs, check_vma=False)
```

```python
import functools
import math

import jax
import jax.numpy as jnp
from jax import lax
from jax.experimental import pallas as pl
from jax.experimental.pallas import tpu as pltpu
from jax.sharding import PartitionSpec as P

HD = 64
EPS = 1e-05
NEG = -1e30
BLK = 256
LANES = 128

SMEM = pl.BlockSpec(memory_space=pltpu.SMEM)
VMEM = pl.BlockSpec(memory_space=pltpu.VMEM)


def nt(a, b):
    return lax.dot_general(a, b, (((1,), (1,)), ((), ())), preferred_element_type=jnp.float32)


def nn(a, b):
    return jnp.dot(a, b, preferred_element_type=jnp.float32)


def tn(a, b):
    return lax.dot_general(a, b, (((0,), (0,)), ((), ())), preferred_element_type=jnp.float32)


WEIGHTS = {"attend_back": 1.45, "output": 0.01, "mlp_shares": 0.01, "tail_shares": 0.01, "finish": 0.01}


def call(kernel, name, outs, specs, scratch, flops, exps, args, vmem=12):
    weight = WEIGHTS.get(name, 3.0)
    moved = sum(math.prod(v.shape) * v.dtype.itemsize for v in list(args) + list(outs))
    return pl.pallas_call(
        kernel,
        name=name,
        out_shape=tuple(outs),
        in_specs=specs,
        out_specs=tuple(VMEM for _ in outs),
        scratch_shapes=scratch,
        compiler_params=pltpu.CompilerParams(vmem_limit_bytes=vmem << 20),
        cost_estimate=pl.CostEstimate(
            flops=int(flops * weight),
            transcendentals=int(exps * weight),
            bytes_accessed=int(moved * weight),
        ),
    )(*args)


def low_shape(*shape):
    return jax.ShapeDtypeStruct(shape, jnp.bfloat16)


def wide_shape(*shape):
    return jax.ShapeDtypeStruct(shape, jnp.float32)


def loop(count, body):
    def step(tile, carry):
        body(pl.ds(pl.multiple_of(tile * BLK, BLK), BLK))
        return carry

    lax.fori_loop(0, count // BLK, step, 0)


def diag_allowed(picture, query_axis):
    query_pos = lax.broadcasted_iota(jnp.int32, (BLK, BLK), query_axis)
    key_pos = lax.broadcasted_iota(jnp.int32, (BLK, BLK), 1 - query_axis)
    return (key_pos <= query_pos) | (picture > 0)


def place(info_ref, rel, rows):
    return pl.multiple_of((info_ref[0] ^ rel) * rows, rows)


def assemble(dst_ref, parts, half):
    if len(parts) == 1:
        dst_ref[...] = parts[0][0]
        return
    mine, other = parts
    count, shard = mine.shape[:2]
    for part in range(count):
        dst_ref[pl.ds(pl.multiple_of((2 * part + half) * shard, shard), shard), :] = mine[part]
        dst_ref[pl.ds(pl.multiple_of((2 * part + 1 - half) * shard, shard), shard), :] = other[part]


def forward_head(head, slot, info_ref, q_aug, k_aug, v_aug, o_rows, lse_ref):
    seq = q_aug.shape[1]
    for block in range(seq // BLK):
        lo, hi = block * BLK, (block + 1) * BLK
        scores = nt(q_aug[head, lo:hi, :], k_aug[head, :hi, :])
        last = jnp.where(diag_allowed(info_ref[2 + block], 0), scores[:, lo:], NEG)
        row_max = jnp.max(last, axis=1, keepdims=True)
        if block:
            row_max = jnp.maximum(row_max, jnp.max(scores[:, :lo], axis=1, keepdims=True))
        acc = nn(jnp.exp(last - row_max).astype(jnp.bfloat16), v_aug[head, lo:hi, :])
        if block:
            front = jnp.exp(scores[:, :lo] - row_max).astype(jnp.bfloat16)
            acc = acc + nn(front, v_aug[head, :lo, :])
        total = acc[:, HD : HD + 1]
        o_rows[slot, lo:hi, :] = (acc[:, :HD] / total).astype(o_rows.dtype)
        lse = row_max + jnp.log(total)
        lse_ref[slot, :, lo:hi] = jnp.broadcast_to(lse, (BLK, LANES)).T[:1]


def first_kernel(info_ref, x0, x1, x2, x3, f0, f1, f2, f3, *refs):
    *parts, w_ref, out_w, q_aug, k_aug, v_aug, k_t, o_rows, lse_ref = refs
    inputs, firsts = (x0, x1, x2, x3), (f0, f1, f2, f3)
    rows = x0.shape[0]
    seq = 4 * rows
    heads = q_aug.shape[0]
    cols = heads * HD
    rank = info_ref[0]
    assemble(w_ref, parts, info_ref[2 + seq // BLK])
    out_w[...] = w_ref[:, 3 * cols :]
    lane = lax.broadcasted_iota(jnp.int32, (seq, HD), 1)
    pos = lax.broadcasted_iota(jnp.int32, (seq, HD), 0)
    bias = jnp.where((lane == 0) & (pos >= info_ref[1]), NEG, 0.0).astype(jnp.bfloat16)
    one = jnp.where(lane == 0, 1.0, 0.0).astype(jnp.bfloat16)
    ones = jnp.where(lane < 3, 1.0, 0.0).astype(jnp.bfloat16)
    for head in range(heads):
        q_aug[head, :, HD:] = one
        k_aug[head, :, HD:] = bias
        v_aug[head, :, HD:] = ones
    for rel in range(4):
        span = pl.ds(place(info_ref, rel, rows), rows)
        part = nn(inputs[rel][...], w_ref[:, : 3 * cols])
        for head in range(heads):
            at = head * HD
            q_aug[head, span, :HD] = part[:, at : at + HD].astype(jnp.bfloat16) * jnp.bfloat16(
                1.0 / math.sqrt(HD)
            )
            keys = part[:, cols + at : cols + at + HD].astype(jnp.bfloat16)
            k_aug[head, span, :HD] = keys
            k_t[head, :, span] = keys.T
            reused = jnp.where(
                rank % 2 == 0, firsts[rel][:, at : at + HD], firsts[rel][:, cols + at : cols + at + HD]
            )
            fresh = part[:, 2 * cols + at : 2 * cols + at + HD].astype(jnp.bfloat16)
            v_aug[head, span, :HD] = jnp.where(rank < 2, fresh, reused)
    forward_head(0, 0, info_ref, q_aug, k_aug, v_aug, o_rows, lse_ref)


def attend_first(info, inputs, parts, firsts, cols):
    rows, dim = inputs[0].shape
    wide = parts[0].shape[2]
    heads = cols // HD
    seq = 4 * rows
    work = seq * (seq + BLK) // 2
    return call(
        first_kernel,
        "attend_first",
        [
            low_shape(dim, wide),
            low_shape(dim, cols),
            low_shape(heads, seq, 2 * HD),
            low_shape(heads, seq, 2 * HD),
            low_shape(heads, seq, 2 * HD),
            low_shape(heads, HD, seq),
            low_shape(1, seq, HD),
            wide_shape(1, 1, seq),
        ],
        [SMEM] + [VMEM] * (8 + len(parts)),
        [],
        16 * work * HD + 2 * seq * dim * wide,
        work,
        (info, *inputs, *firsts, *parts),
    )


def rest_kernel(
    info_ref, q_aug, k_aug, v_aug, o_first, lse_first, own_ref, core_ref, pair_ref, lse_ref, o_rows, lse_part
):
    rows, cols = own_ref.shape
    heads = cols // HD

    def per_head(head, carry):
        forward_head(head + 1, head, info_ref, q_aug, k_aug, v_aug, o_rows, lse_part)
        return carry

    lax.fori_loop(0, heads - 1, per_head, 0)
    lse_ref[0] = lse_first[0]
    for head in range(1, heads):
        lse_ref[head] = lse_part[head - 1]
    for rel, (out, first) in enumerate(((own_ref, 0), (core_ref, 0), (pair_ref, 0), (pair_ref, cols))):
        span = pl.ds(place(info_ref, rel, rows), rows)
        out[:, first : first + HD] = o_first[0, span, :]
        for head in range(1, heads):
            at = first + head * HD
            out[:, at : at + HD] = o_rows[head - 1, span, :]


def attend_rest(info, q_aug, k_aug, v_aug, o_first, lse_first):
    heads, seq = q_aug.shape[:2]
    rows, cols = seq // 4, heads * HD
    work = (heads - 1) * seq * (seq + BLK) // 2
    return call(
        rest_kernel,
        "attend_rest",
        [
            low_shape(rows, cols),
            low_shape(rows, cols),
            low_shape(rows, 2 * cols),
            wide_shape(heads, 1, seq),
        ],
        [SMEM] + [VMEM] * 5,
        [pltpu.VMEM((heads - 1, seq, HD), jnp.bfloat16), pltpu.VMEM((heads - 1, 1, seq), jnp.float32)],
        16 * work * HD,
        work,
        (info, q_aug, k_aug, v_aug, o_first, lse_first),
    )


def backward_kernel(
    info_ref, q_aug, k_aug, v_aug, k_t, g0, g1, g2, g3, own_ref, core_ref, pair_ref, lse_ref,
    dqkv_ref, dv_own, dv_core, dv_pair, g_aug, dq_t, dk_acc, dv_acc,
):
    rows, cols = own_ref.shape
    grads = ((g0, 0), (g1, 0), (g2, 0), (g3, cols))
    outs = ((own_ref, 0), (core_ref, 0), (pair_ref, 0), (pair_ref, cols))
    dv_outs = ((dv_own, 0), (dv_core, 0), (dv_pair, 0), (dv_pair, cols))
    heads, seq = q_aug.shape[:2]
    lane = lax.broadcasted_iota(jnp.int32, (rows, HD), 1)
    for head in range(heads):
        at = head * HD
        for rel in range(4):
            span = pl.ds(place(info_ref, rel, rows), rows)
            src, first = grads[rel]
            grad = src[:, first + at : first + at + HD]
            g_aug[head, span, :HD] = grad
            src, first = outs[rel]
            products = grad.astype(jnp.float32) * src[:, first + at : first + at + HD].astype(jnp.float32)
            left = -jnp.sum(products, axis=1, keepdims=True)
            part = jnp.zeros((rows, HD), jnp.bfloat16)
            for piece in range(3):
                low = left.astype(jnp.bfloat16)
                part = jnp.where(lane == piece, low, part)
                left = left - low.astype(jnp.float32)
            g_aug[head, span, HD:] = part

    def per_head(head, carry):
        for block in range(seq // BLK):
            lo, hi = block * BLK, (block + 1) * BLK
            probs = jnp.exp(nt(k_aug[head, lo:hi, :], q_aug[head, lo:, :]) - lse_ref[head, :, lo:])
            first = jnp.where(diag_allowed(info_ref[2 + block], 1), probs[:, :BLK], 0.0)
            probs = first if hi == seq else jnp.concatenate([first, probs[:, BLK:]], axis=1)
            grad_probs = nt(v_aug[head, lo:hi, :], g_aug[head, lo:, :])
            grad_scores = (probs * grad_probs).astype(jnp.bfloat16)
            dv_acc[head, lo:hi, :] = nn(probs.astype(jnp.bfloat16), g_aug[head, lo:, :])[:, :HD].astype(
                jnp.bfloat16
            )
            dk_acc[head, lo:hi, :] = nn(grad_scores, q_aug[head, lo:, :])[:, :HD].astype(jnp.bfloat16)
            part = nn(k_t[head, :, lo:hi], grad_scores)
            if block:
                dq_t[head, :, lo:] += part
            else:
                dq_t[head, :, :] = part
        return carry

    lax.fori_loop(0, heads, per_head, 0)
    fresh = info_ref[0] < 2
    for rel in range(4):
        span = pl.ds(place(info_ref, rel, rows), rows)
        part = dq_t[:, :, span].reshape(cols, rows)
        dqkv_ref[rel, :, :cols] = (part.T * (1.0 / math.sqrt(HD))).astype(dqkv_ref.dtype)
        for head in range(heads):
            at = head * HD
            dqkv_ref[rel, :, cols + at : cols + at + HD] = dk_acc[head, span, :]
            value = dv_acc[head, span, :]
            out, first = dv_outs[rel]
            out[:, first + at : first + at + HD] = value
            kept = jnp.where(fresh, value, jnp.zeros_like(value))
            dqkv_ref[rel, :, 2 * cols + at : 2 * cols + at + HD] = kept


def attend_back(info, prepared, grads, outs, lse):
    heads, seq = prepared[0].shape[:2]
    rows, cols = seq // 4, heads * HD
    work = heads * seq * (seq + BLK) // 2
    return call(
        backward_kernel,
        "attend_back",
        [
            low_shape(4, rows, 3 * cols),
            low_shape(rows, cols),
            low_shape(rows, cols),
            low_shape(rows, 2 * cols),
        ],
        [SMEM] + [VMEM] * 12,
        [
            pltpu.VMEM((heads, seq, 2 * HD), jnp.bfloat16),
            pltpu.VMEM((heads, HD, seq), jnp.float32),
            pltpu.VMEM((heads, seq, HD), jnp.bfloat16),
            pltpu.VMEM((heads, seq, HD), jnp.bfloat16),
        ],
        40 * work * HD,
        work,
        (info, *prepared, *grads, *outs, lse),
        20,
    )


def norm_stats(wide):
    centred = wide - jnp.mean(wide, axis=-1, keepdims=True)
    inv_std = lax.rsqrt(jnp.mean(centred * centred, axis=-1, keepdims=True) + EPS)
    return centred * inv_std, inv_std


def valid_rows(info_ref, rows, start, count):
    pos = info_ref[0] * rows + start + lax.broadcasted_iota(jnp.int32, (count, 1), 0)
    return (pos < info_ref[1]).astype(jnp.float32)


def row_sum(v):
    return jnp.sum(v, axis=0, keepdims=True)


def middle_kernel(
    info_ref, tok_ref, h0, h1, h2, h3, w0, w1, w2, w3, gain_ref, resid_ref, input_ref, square_ref
):
    rows = tok_ref.shape[0]
    cols = h0.shape[1]
    square_ref[...] = jnp.zeros_like(square_ref)

    def tile(span):
        attn = nt(h0[span], w0[...]) + nt(h1[span], w1[...])
        attn = attn + nt(h2[span, :cols], w2[...]) + nt(h3[span, cols:], w3[...])
        resid = tok_ref[span].astype(jnp.float32) + attn
        resid_ref[span] = resid
        normed, _ = norm_stats(resid)
        input_ref[span] = (normed * gain_ref[...]).astype(input_ref.dtype)
        square_ref[...] += row_sum(attn * attn * valid_rows(info_ref, rows, span.start, BLK))

    loop(rows, tile)


def middle(info, tokens, heads, weights, gain):
    rows, dim = tokens.shape
    return call(
        middle_kernel,
        "middle",
        [wide_shape(rows, dim), low_shape(rows, dim), wide_shape(1, dim)],
        [SMEM] + [VMEM] * 10,
        [],
        2 * rows * dim * dim,
        rows,
        (info, tokens, *heads, *weights, gain),
    )


GELU_C = math.sqrt(2.0 / math.pi)
CUBE = 0.044715


def mlp_tiles(xs, cots, w_ref, hid_ref, dup_ref, backs, outs):
    rows = xs[0].shape[0]
    up_cols = w_ref.shape[1] // 2
    up_w, down_t = w_ref.at[:, :up_cols], w_ref.at[:, up_cols:]
    for block in range(2):

        def tile(span, block=block):
            up = nn(xs[block][span], up_w[...])
            up2 = up * up
            th = jnp.tanh(GELU_C * up * (1.0 + CUBE * up2))
            half = 0.5 * (1.0 + th)
            hidden = (up * half).astype(jnp.bfloat16)
            hid_ref[block, span] = hidden
            slope = half + 0.5 * up * (1.0 - th * th) * (GELU_C * (1.0 + 3.0 * CUBE * up2))
            dup = (nn(cots[block][span], down_t[...]) * slope).astype(jnp.bfloat16)
            dup_ref[block, span] = dup
            backs[block][span] = nt(dup, up_w[...]).astype(jnp.bfloat16)
            if outs:
                outs[block][span] = nt(hidden, down_t[...]).astype(jnp.bfloat16)

        loop(rows, tile)


def mlp_near_kernel(x0, x1, c0, c1, w_ref, hid_ref, dup_ref, b0, b1, o0, o1):
    mlp_tiles((x0, x1), (c0, c1), w_ref, hid_ref, dup_ref, (b0, b1), (o0, o1))


def mlp_far_kernel(x0, x1, c0, c1, w_ref, hid_ref, dup_ref, b0, b1):
    mlp_tiles((x0, x1), (c0, c1), w_ref, hid_ref, dup_ref, (b0, b1), ())


def mlp_near(xs, cots, weights):
    rows, dim = xs[0].shape
    wide = weights.shape[1]
    return call(
        mlp_near_kernel,
        "mlp_near",
        [low_shape(2, rows, wide // 2)] * 2 + [low_shape(rows, dim)] * 4,
        [VMEM] * 5,
        [],
        8 * rows * dim * wide,
        rows * wide,
        (*xs, *cots, weights),
    )


def mlp_far(xs, cots, weights):
    rows, dim = xs[0].shape
    wide = weights.shape[1]
    return call(
        mlp_far_kernel,
        "mlp_far",
        [low_shape(2, rows, wide // 2)] * 2 + [low_shape(rows, dim)] * 2,
        [VMEM] * 5,
        [],
        6 * rows * dim * wide,
        rows * wide,
        (*xs, *cots, weights),
    )


def mlp_grads_kernel(up_cols, x0, x1, x2, x3, c0, c1, c2, c3, h_a, h_b, d_a, d_b, w_ref, g_ref, o0, o1):
    down_t = w_ref.at[:, up_cols : 2 * up_cols]
    step = 2 * BLK
    for rel, out in ((0, o0), (1, o1)):
        out[...] = nt(h_b[rel], down_t[...]).astype(out.dtype)
    for start in range(0, up_cols, BLK):
        span = slice(start, start + BLK)
        acc = tn(x0[...], d_a[0, :, span]) + tn(x1[...], d_a[1, :, span])
        acc = acc + tn(x2[...], d_b[0, :, span]) + tn(x3[...], d_b[1, :, span])
        g_ref[:, span] = acc.astype(g_ref.dtype)
        acc = tn(c0[...], h_a[0, :, span]) + tn(c1[...], h_a[1, :, span])
        acc = acc + tn(c2[...], h_b[0, :, span]) + tn(c3[...], h_b[1, :, span])
        g_ref[:, up_cols + start : up_cols + start + BLK] = acc.astype(g_ref.dtype)


def mlp_grads(xs, cots, hid_a, hid_b, dup_a, dup_b, weights, up_cols):
    rows, dim = xs[0].shape
    return call(
        functools.partial(mlp_grads_kernel, up_cols),
        "mlp_grads",
        [low_shape(dim, 2 * up_cols), low_shape(rows, dim), low_shape(rows, dim)],
        [VMEM] * 13,
        [],
        20 * rows * dim * up_cols,
        0,
        (*xs, *cots, hid_a, hid_b, dup_a, dup_b, weights),
    )


def turn_kernel(
    resid_ref, cot_ref, b0, b1, b2, gain_ref, w0, w1, w2, w3,
    grad_ref, low_ref, d_own, d_core, d_pair, gain_out,
):
    rows = resid_ref.shape[0]
    cols = d_own.shape[1]
    gain_out[...] = jnp.zeros_like(gain_out)

    def tile(span):
        normed, inv_std = norm_stats(resid_ref[span])
        back = b0[span].astype(jnp.float32) + b1[span].astype(jnp.float32)
        back = back + b2[span].astype(jnp.float32)
        gain_out[...] += row_sum(back * normed)
        scaled = back * gain_ref[...]
        inner = scaled - jnp.mean(scaled, axis=-1, keepdims=True)
        inner = inner - normed * jnp.mean(scaled * normed, axis=-1, keepdims=True)
        grad = cot_ref[span].astype(jnp.float32) + inner * inv_std
        grad_ref[span] = grad
        low = grad.astype(jnp.bfloat16)
        low_ref[span] = low
        d_own[span] = nn(low, w0[...]).astype(jnp.bfloat16)
        d_core[span] = nn(low, w1[...]).astype(jnp.bfloat16)
        d_pair[span, :cols] = nn(low, w2[...]).astype(jnp.bfloat16)
        d_pair[span, cols:] = nn(low, w3[...]).astype(jnp.bfloat16)

    loop(rows, tile)


def turn(resid, cot, backs, gain, weights):
    rows, dim = cot.shape
    cols = weights[0].shape[1]
    return call(
        turn_kernel,
        "turn",
        [
            wide_shape(rows, dim),
            low_shape(rows, dim),
            low_shape(rows, cols),
            low_shape(rows, cols),
            low_shape(rows, 2 * cols),
            wide_shape(1, dim),
        ],
        [VMEM] * 10,
        [],
        2 * rows * dim * dim,
        rows,
        (resid, cot, *backs, gain, *weights),
    )


def out_grads_kernel(low_ref, h0, h1, h2, h3, o_near, o_far):
    cols = h0.shape[1]
    low = low_ref[...]
    o_near[:, :cols] = tn(low, h0[...])
    o_far[:, :cols] = tn(low, h1[...]).astype(jnp.bfloat16)
    o_near[:, cols:] = tn(low, h2[:, :cols])
    o_far[:, cols:] = tn(low, h3[:, cols:]).astype(jnp.bfloat16)


def out_grads(low, heads):
    rows, dim = low.shape
    cols = heads[0].shape[1]
    return call(
        out_grads_kernel,
        "out_grads",
        [wide_shape(dim, 2 * cols), low_shape(dim, 2 * cols)],
        [VMEM] * 5,
        [],
        2 * rows * dim * dim,
        0,
        (low, *heads),
    )


def slot_sum_kernel(near_ref, far_ref, out_ref):
    cols = out_ref.shape[1]
    out_ref[...] = (near_ref[:, cols:] + far_ref[:, cols:].astype(jnp.float32)).astype(out_ref.dtype)


def slot_sum(near, far):
    dim, wide = near.shape
    return call(
        slot_sum_kernel, "slot_sum", [low_shape(dim, wide // 2)], [VMEM] * 2, [], dim * wide, 0, (near, far)
    )[0]


def input_grads_kernel(dqkv_ref, w_ref, o0, o1, o2, o3):
    rows, wide = dqkv_ref.shape[1:]
    for rel, out in ((2, o2), (3, o3), (0, o0), (1, o1)):

        def tile(span, rel=rel, out=out):
            out[span] = nt(dqkv_ref[rel, span], w_ref[:, :wide]).astype(out.dtype)

        loop(rows, tile)


def input_grads(dqkv, weights):
    rows, cols = dqkv.shape[1:]
    dim = weights.shape[0]
    return call(
        input_grads_kernel,
        "input_grads",
        [low_shape(rows, dim)] * 4,
        [VMEM] * 2,
        [],
        8 * rows * dim * cols,
        0,
        (dqkv, weights),
    )


def qkv_grads_kernel(
    x0, x1, x2, x3, dqkv_ref, near_ref, far_ref, far_x, small_ref, w_ref, gain_ref, out_ref, all_ref
):
    wide = dqkv_ref.shape[2]
    cols = wide // 3
    acc = tn(x0[...], dqkv_ref[0]) + tn(x1[...], dqkv_ref[1])
    acc = acc + tn(x2[...], dqkv_ref[2]) + tn(x3[...], dqkv_ref[3])
    all_ref[:, :wide] = acc.astype(all_ref.dtype)
    total = near_ref[:, :cols] + far_ref[:, :cols].astype(jnp.float32)
    total = total + far_x[...].astype(jnp.float32)
    all_ref[:, wide:] = total.astype(all_ref.dtype)
    products = acc * w_ref[:, :wide].astype(jnp.float32)
    low = products.astype(jnp.bfloat16)
    ones = jnp.ones((8, wide), jnp.bfloat16)
    sums = nt(ones, low) + nt(ones, (products - low.astype(jnp.float32)).astype(jnp.bfloat16))
    sums = sums[:1] / gain_ref[...]
    low = sums.astype(jnp.bfloat16)
    row = lax.broadcasted_iota(jnp.int32, small_ref.shape, 0)
    small = jnp.where(row == 0, low, small_ref[...])
    small = jnp.where(row == 8, (sums - low.astype(jnp.float32)).astype(jnp.bfloat16), small)
    count, full = out_ref.shape[:2]
    shard = all_ref.shape[0] // count
    for part in range(count):
        out_ref[part, :shard] = all_ref[part * shard : (part + 1) * shard]
        out_ref[part, shard:] = small


def qkv_grads(xs, dqkv, near, far, far_x, small, weights, gain, count):
    rows, dim = xs[0].shape
    wide = dqkv.shape[2]
    full = wide + wide // 3
    extra = small.shape[0]
    return call(
        qkv_grads_kernel,
        "qkv_grads",
        [low_shape(count, dim // count + extra, full)],
        [VMEM] * 11,
        [pltpu.VMEM((dim, full), jnp.bfloat16)],
        8 * rows * dim * wide,
        0,
        (*xs, dqkv, near, far, far_x, small, weights, gain),
    )[0]


def finish_kernel(tok_ref, grad_ref, b0, b1, b2, gain_ref, out_ref):

    def tile(span):
        normed, inv_std = norm_stats(tok_ref[span].astype(jnp.float32))
        back = b0[span].astype(jnp.float32) + b1[span].astype(jnp.float32)
        back = back + b2[span].astype(jnp.float32)
        scaled = back * gain_ref[...]
        inner = scaled - jnp.mean(scaled, axis=-1, keepdims=True)
        inner = inner - normed * jnp.mean(scaled * normed, axis=-1, keepdims=True)
        out_ref[span] = grad_ref[span] + inner * inv_std

    loop(tok_ref.shape[0], tile)


def finish(tokens, grad, backs, gain):
    rows, dim = tokens.shape
    return call(
        finish_kernel,
        "finish",
        [wide_shape(rows, dim)],
        [VMEM] * 6,
        [],
        rows * dim * 20,
        rows,
        (tokens, grad, *backs, gain),
    )[0]


def norm_kernel(t0, t1, gain_ref, o0, o1):
    for src, out in ((t0, o0), (t1, o1)):

        def tile(span, src=src, out=out):
            normed, _ = norm_stats(src[span].astype(jnp.float32))
            out[span] = (normed * gain_ref[...]).astype(out.dtype)

        loop(t0.shape[0], tile)


def norms(blocks, gain):
    rows, dim = blocks[0].shape
    return call(
        norm_kernel,
        "norms",
        [low_shape(rows, dim)] * 2,
        [VMEM] * 3,
        [],
        rows * dim * 20,
        rows,
        (*blocks, gain),
    )


def share_kernel(shard, parts_ref, *outs):
    cols = outs[0].shape[1]
    for at, out in enumerate(outs):
        if out.shape[0] != shard:
            break
        span = slice(at * cols, (at + 1) * cols)
        total = parts_ref[0, :shard, span].astype(jnp.float32)
        for part in range(1, parts_ref.shape[0]):
            total = total + parts_ref[part, :shard, span].astype(jnp.float32)
        out[...] = total
    if parts_ref.shape[1] > shard:
        total = parts_ref[0, shard:].astype(jnp.float32)
        for part in range(1, parts_ref.shape[0]):
            total = total + parts_ref[part, shard:].astype(jnp.float32)
        half = total.shape[0] // 2
        outs[-1][...] = total[:half] + total[half:]


def shares(parts, shard, cols, name):
    count, full, wide = parts.shape
    outs = [wide_shape(shard, cols)] * (wide // cols)
    if full > shard:
        outs.append(wide_shape((full - shard) // 2, wide))
    return call(
        functools.partial(share_kernel, shard),
        name,
        outs,
        [VMEM],
        [],
        count * full * wide,
        0,
        (parts,),
    )


def output_kernel(info_ref, resid_ref, b0, b1, b2, attn_sq, gain_two, out_ref, small_ref, *sums):
    rows, dim = resid_ref.shape
    final_sum, mlp_sum = sums
    final_sum[...] = jnp.zeros_like(final_sum)
    mlp_sum[...] = jnp.zeros_like(mlp_sum)

    def tile(span):
        valid = valid_rows(info_ref, rows, span.start, BLK)
        mlp_out = b0[span].astype(jnp.float32) + b1[span].astype(jnp.float32)
        mlp_out = mlp_out + b2[span].astype(jnp.float32)
        final = resid_ref[span] + mlp_out
        out_ref[span] = final.astype(out_ref.dtype)
        final_sum[...] += row_sum(final * final * valid)
        mlp_sum[...] += row_sum(mlp_out * mlp_out * valid)

    loop(rows, tile)
    count = jnp.clip(info_ref[1] - info_ref[0] * rows, 0, rows).astype(jnp.float32)
    lane = lax.broadcasted_iota(jnp.int32, (1, dim), 1)
    counts = jnp.where(lane == 0, count, 0.0)
    row = lax.broadcasted_iota(jnp.int32, (8, dim), 0)
    wide = jnp.zeros((8, dim), jnp.float32)
    values = (jnp.zeros_like(gain_two), gain_two[...], final_sum[...], attn_sq[...], mlp_sum[...], counts)
    for at, value in enumerate(values):
        wide = jnp.where(row == at, value, wide)
    low = wide.astype(jnp.bfloat16)
    small_ref[...] = jnp.concatenate([low, (wide - low.astype(jnp.float32)).astype(jnp.bfloat16)], axis=0)


def output(info, resid, parts, sums):
    rows, dim = resid.shape
    return call(
        output_kernel,
        "output",
        [low_shape(rows, dim), low_shape(16, dim)],
        [SMEM] + [VMEM] * 6,
        [pltpu.VMEM((1, dim), jnp.float32)] * 2,
        rows * dim * 10,
        0,
        (info, resid, *parts, *sums),
    )


def pack_early_kernel(info_ref, wq, wk, wv, wo, out_ref):
    cols = wq.shape[1]
    even = info_ref[0] % 2 == 0
    fresh = jnp.where(even, wv[:, :cols], wv[:, cols : 2 * cols])
    turned = wo[...].T
    for part in range(out_ref.shape[0]):
        for at, value in enumerate((wq[...], wk[...], fresh, turned)):
            out_ref[part, :, at * cols : (at + 1) * cols] = value


def pack_early(info, copies, wq, wk, wv, wo):
    shard, cols = wq.shape
    return call(
        pack_early_kernel, "pack_early", [low_shape(copies, shard, 4 * cols)],
        [SMEM] + [VMEM] * 4, [], shard * cols, 0, (info, wq, wk, wv, wo), 60,
    )[0]


X_SWAP = [(0, 2), (1, 3), (2, 0), (3, 1)]
CORE_SWAP = [(0, 1), (1, 0), (2, 3), (3, 2)]


def swap_x(v):
    return lax.ppermute(v, "tensor", X_SWAP)


def swap_core(v):
    return lax.ppermute(v, "tensor", CORE_SWAP)


def tied(value, *others):
    return lax.optimization_barrier((value, *others))[0]


def plus(a, b):
    return (a.astype(jnp.float32) + b.astype(jnp.float32)).astype(jnp.bfloat16)


def body(
    tokens,
    first_values,
    pieces,
    lengths,
    w_query,
    w_key,
    w_value,
    w_out,
    w_up,
    w_down,
    gain_attn,
    gain_mlp,
    cotangent,
):
    dp_size = lax.axis_size("dp")
    rank = lax.axis_index("tensor")
    core = rank % 2
    rows, dim = tokens.shape
    shard, cols = w_query.shape
    up_cols = w_up.shape[1]
    parity = lax.axis_index("dp") % 2
    info = jnp.concatenate(
        [rank[None].astype(jnp.int32), lengths, pieces[::BLK], parity[None].astype(jnp.int32)]
    )
    gain_one, gain_two = gain_attn[None], gain_mlp[None]
    pairs = [(i, i ^ 1) for i in range(dp_size)]
    lines = [list(range(first, dp_size, 2)) for first in range(2)]

    def gather_line(v):
        return lax.all_to_all(v, "dp", 0, 0, axis_index_groups=lines)

    def swap_pair(v):
        return lax.ppermute(v, "dp", pairs)

    def in_order(mine, other):
        lower = jnp.where(parity == 0, mine, other)
        upper = jnp.where(parity == 0, other, mine)
        return jnp.stack([lower, upper], axis=1).reshape(dim, -1)

    def pieces_of(mine, other):
        if shard % 16 == 0:
            return (mine, other)
        return (in_order(mine, other)[None],)

    early = pack_early(info, dp_size // 2, w_query, w_key, w_value, w_out)
    early_mine = gather_line(early)
    tok_x = swap_x(tokens)
    tok_core = swap_core(tokens)
    xs_near = norms((tokens, tok_core), gain_one)
    early_other = swap_pair(early_mine)
    tok_diag = swap_core(tok_x)
    late = tied(jnp.concatenate([w_up, w_down.T], axis=1), tok_diag)
    late_all = lax.all_gather(late, "dp", axis=0, tiled=True)
    first_x = lax.ppermute(first_values, "tensor", [(0, 2), (1, 3)])
    firsts = (first_values, swap_core(first_values), first_x, swap_core(first_x))
    xs = (*xs_near, *norms((tok_x, tok_diag), gain_one))
    early_all, out_own, *prepared, o_first, lse_first = attend_first(
        info, xs, pieces_of(early_mine, early_other), firsts, cols
    )

    out_x = swap_x(out_own)
    cot_x = swap_x(tied(cotangent, first_x))
    o_first = tied(o_first, cot_x)
    h_own, h_core, h_pair, lse = attend_rest(info, *prepared[:3], o_first, lse_first)
    h_pair, h_core = lax.optimization_barrier((h_pair, h_core, cot_x, out_x))[:2]
    cot_core = swap_core(cotangent)
    cot_diag = swap_core(cot_x)
    outs = (out_own, swap_core(out_own), out_x, swap_core(out_x))

    from_x = swap_x(h_pair)
    heads_mine = (h_own, swap_core(h_core), from_x, swap_core(from_x))
    resid, mlp_in, attn_sq = middle(
        info, tokens, heads_mine, outs, gain_two
    )
    in_x = swap_x(mlp_in)
    in_core = swap_core(mlp_in)
    hid_a, dup_a, back_own, back_core, out_0, out_1 = mlp_near(
        (mlp_in, in_core), (cotangent, cot_core), late_all
    )
    back_1 = swap_core(back_core)
    out_near = swap_core(out_1)
    in_far = tied(in_x, back_own)
    in_diag = swap_core(in_far)
    hid_b, dup_b, back_x, back_diag = mlp_far((in_far, in_diag), (cot_x, cot_diag), late_all)
    back_far = plus(back_x, swap_core(back_diag))
    back_2 = swap_x(back_far)
    grads_mlp, out_2, out_3 = mlp_grads(
        (mlp_in, in_core, in_x, in_diag),
        (cotangent, cot_core, cot_x, cot_diag),
        hid_a, tied(hid_b, back_far), dup_a, dup_b, late_all, up_cols,
    )
    mlp_share = lax.psum_scatter(grads_mlp, "dp", scatter_dimension=0, tiled=True)
    out_sum = plus(out_2, swap_core(out_3))

    resid_grad, resid_low, d_own, d_core, d_pair, gain_two_sum = turn(
        resid, cotangent, (back_own, back_1, back_2), gain_two, outs
    )
    d_x = swap_x(d_pair)
    grads_heads = (d_own, swap_core(d_core), d_x, swap_core(d_x))
    near, far = out_grads(resid_low, heads_mine)
    far = swap_core(far)
    dqkv, dv_own, dv_core, dv_pair = attend_back(
        info, prepared, grads_heads, (h_own, h_core, h_pair), lse
    )
    out_from_x = swap_x(tied(out_sum, d_x))
    near_x = swap_x(tied(slot_sum(near, far), d_x))
    dqkv, dv_pair = lax.optimization_barrier((dqkv, dv_pair, out_from_x, near_x))[:2]

    first_from_x = lax.ppermute(dv_pair, "tensor", [(2, 0), (3, 1)])
    final, small = output(info, resid, (out_0, out_near, out_from_x), (attn_sq, gain_two_sum))
    joined = shard % 16 == 0
    tail = qkv_grads(
        xs, tied(dqkv, small), near, far, near_x, small, early_all, gain_one, dp_size if joined else 1
    )
    if not joined:
        small = tail[0, dim:]
        tail = tail[0, :dim]
    tail_all = lax.all_to_all(tail.reshape(dp_size, -1, 4 * cols), "dp", 0, 0)
    b_0, b_1, b_2, b_3 = input_grads(tied(dqkv, tail, first_from_x), early_all)
    b_from_x = swap_x(plus(b_2, swap_core(b_3)))
    b_from_core = swap_core(b_1)

    first_a = jnp.where(rank < 2, first_from_x[:, :cols], dv_own)
    first_b = swap_core(jnp.where(rank < 2, first_from_x[:, cols:], dv_core))
    first_grad = jnp.where(
        core == 0,
        jnp.concatenate([first_a, first_b], axis=1),
        jnp.concatenate([first_b, first_a], axis=1),
    ).astype(jnp.float32)
    token_grad = finish(tokens, resid_grad, (b_0, b_from_core, b_from_x), gain_one)
    grad_up, grad_down_t = shares(mlp_share[None], shard, up_cols, "mlp_shares")
    tail_all = tied(tail_all, token_grad, grad_up, first_grad)
    grad_q, grad_k, value_own, grad_out_t, *rest = shares(tail_all, shard, cols, "tail_shares")
    if joined:
        total = rest[0]
    else:
        total = lax.psum(small[:8].astype(jnp.float32) + small[8:].astype(jnp.float32), "dp")
    total = total + swap_x(total)
    total = total + swap_core(total)
    value_x = lax.ppermute(value_own, "tensor", [(0, 2), (1, 3)])
    value_here = jnp.where(rank < 2, value_own, value_x)
    value_peer = swap_core(value_here)
    value_share = jnp.where(
        core == 0,
        jnp.concatenate([value_here, value_peer], axis=1),
        jnp.concatenate([value_peer, value_here], axis=1),
    )
    square_total = jnp.sum(total[2:6], axis=1)
    rms = jnp.sqrt(square_total[:3] / (square_total[3] * dim))
    return (
        final,
        token_grad,
        first_grad,
        grad_q,
        grad_k,
        value_share,
        grad_out_t.T,
        grad_up,
        grad_down_t.T,
        total[0],
        total[1],
        rms,
    )


def solution(mesh):
    in_specs = (
        P(("dp", "tensor"), None),
        P(("dp", "tensor"), None),
        P("dp"),
        P("dp"),
        P("dp", "tensor"),
        P("dp", "tensor"),
        P("dp", None),
        P("tensor", "dp"),
        P("dp", "tensor"),
        P("tensor", "dp"),
        P(),
        P(),
        P(("dp", "tensor"), None),
    )
    out_specs = (
        P(("dp", "tensor"), None),
        P(("dp", "tensor"), None),
        P(("dp", "tensor"), None),
        P("dp", "tensor"),
        P("dp", "tensor"),
        P("dp", None),
        P("tensor", "dp"),
        P("dp", "tensor"),
        P("tensor", "dp"),
        P(),
        P(),
        P(),
    )
    return jax.shard_map(body, mesh=mesh, in_specs=in_specs, out_specs=out_specs, check_vma=False)
```

```python
import functools
import math

import jax
import jax.numpy as jnp
from jax import lax
from jax.experimental import pallas as pl
from jax.experimental.pallas import tpu as pltpu
from jax.sharding import PartitionSpec as P

HD = 64
EPS = 1e-05
NEG = -1e30
BLK = 256
LANES = 128

SMEM = pl.BlockSpec(memory_space=pltpu.SMEM)
VMEM = pl.BlockSpec(memory_space=pltpu.VMEM)


def nt(a, b):
    return lax.dot_general(a, b, (((1,), (1,)), ((), ())), preferred_element_type=jnp.float32)


def nn(a, b):
    return jnp.dot(a, b, preferred_element_type=jnp.float32)


def tn(a, b):
    return lax.dot_general(a, b, (((0,), (0,)), ((), ())), preferred_element_type=jnp.float32)


WEIGHTS = {"attend_back": 1.45, "output": 0.01, "mlp_shares": 0.01, "tail_shares": 0.01, "finish": 0.01, "fold": 0.01}


def call(kernel, name, outs, specs, scratch, flops, exps, args, vmem=12):
    weight = WEIGHTS.get(name, 3.0)
    moved = sum(math.prod(v.shape) * v.dtype.itemsize for v in list(args) + list(outs))
    return pl.pallas_call(
        kernel,
        name=name,
        out_shape=tuple(outs),
        in_specs=specs,
        out_specs=tuple(VMEM for _ in outs),
        scratch_shapes=scratch,
        compiler_params=pltpu.CompilerParams(vmem_limit_bytes=vmem << 20),
        cost_estimate=pl.CostEstimate(
            flops=int(flops * weight),
            transcendentals=int(exps * weight),
            bytes_accessed=int(moved * weight),
        ),
    )(*args)


def low_shape(*shape):
    return jax.ShapeDtypeStruct(shape, jnp.bfloat16)


def wide_shape(*shape):
    return jax.ShapeDtypeStruct(shape, jnp.float32)


def loop(count, body):
    def step(tile, carry):
        body(pl.ds(pl.multiple_of(tile * BLK, BLK), BLK))
        return carry

    lax.fori_loop(0, count // BLK, step, 0)


def diag_allowed(picture, query_axis):
    query_pos = lax.broadcasted_iota(jnp.int32, (BLK, BLK), query_axis)
    key_pos = lax.broadcasted_iota(jnp.int32, (BLK, BLK), 1 - query_axis)
    return (key_pos <= query_pos) | (picture > 0)


def place(info_ref, rel, rows):
    return pl.multiple_of((info_ref[0] ^ rel) * rows, rows)


def assemble(dst_ref, parts, half):
    if len(parts) == 1:
        dst_ref[...] = parts[0][0]
        return
    mine, other = parts
    count, shard = mine.shape[:2]
    for part in range(count):
        dst_ref[pl.ds(pl.multiple_of((2 * part + half) * shard, shard), shard), :] = mine[part]
        dst_ref[pl.ds(pl.multiple_of((2 * part + 1 - half) * shard, shard), shard), :] = other[part]


def forward_head(head, slot, info_ref, q_aug, k_aug, v_aug, o_rows, lse_ref):
    seq = q_aug.shape[1]
    for block in range(seq // BLK):
        lo, hi = block * BLK, (block + 1) * BLK
        scores = nt(q_aug[head, lo:hi, :], k_aug[head, :hi, :])
        last = jnp.where(diag_allowed(info_ref[2 + block], 0), scores[:, lo:], NEG)
        row_max = jnp.max(last, axis=1, keepdims=True)
        if block:
            row_max = jnp.maximum(row_max, jnp.max(scores[:, :lo], axis=1, keepdims=True))
        acc = nn(jnp.exp(last - row_max).astype(jnp.bfloat16), v_aug[head, lo:hi, :])
        if block:
            front = jnp.exp(scores[:, :lo] - row_max).astype(jnp.bfloat16)
            acc = acc + nn(front, v_aug[head, :lo, :])
        total = acc[:, HD : HD + 1]
        o_rows[slot, lo:hi, :] = (acc[:, :HD] / total).astype(o_rows.dtype)
        lse = row_max + jnp.log(total)
        lse_ref[slot, :, lo:hi] = jnp.broadcast_to(lse, (BLK, LANES)).T[:1]


def first_kernel(info_ref, x0, x1, x2, x3, f0, f1, f2, f3, *refs):
    *parts, w_ref, out_w, q_aug, k_aug, v_aug, k_t, o_rows, lse_ref = refs
    inputs, firsts = (x0, x1, x2, x3), (f0, f1, f2, f3)
    rows = x0.shape[0]
    seq = 4 * rows
    heads = q_aug.shape[0]
    cols = heads * HD
    rank = info_ref[0]
    assemble(w_ref, parts, info_ref[2 + seq // BLK])
    out_w[...] = w_ref[:, 3 * cols :]
    lane = lax.broadcasted_iota(jnp.int32, (seq, HD), 1)
    pos = lax.broadcasted_iota(jnp.int32, (seq, HD), 0)
    bias = jnp.where((lane == 0) & (pos >= info_ref[1]), NEG, 0.0).astype(jnp.bfloat16)
    one = jnp.where(lane == 0, 1.0, 0.0).astype(jnp.bfloat16)
    ones = jnp.where(lane < 3, 1.0, 0.0).astype(jnp.bfloat16)
    for head in range(heads):
        q_aug[head, :, HD:] = one
        k_aug[head, :, HD:] = bias
        v_aug[head, :, HD:] = ones
    for rel in range(4):
        span = pl.ds(place(info_ref, rel, rows), rows)
        part = nn(inputs[rel][...], w_ref[:, : 3 * cols])
        for head in range(heads):
            at = head * HD
            q_aug[head, span, :HD] = part[:, at : at + HD].astype(jnp.bfloat16) * jnp.bfloat16(
                1.0 / math.sqrt(HD)
            )
            keys = part[:, cols + at : cols + at + HD].astype(jnp.bfloat16)
            k_aug[head, span, :HD] = keys
            k_t[head, :, span] = keys.T
            reused = jnp.where(
                rank % 2 == 0, firsts[rel][:, at : at + HD], firsts[rel][:, cols + at : cols + at + HD]
            )
            fresh = part[:, 2 * cols + at : 2 * cols + at + HD].astype(jnp.bfloat16)
            v_aug[head, span, :HD] = jnp.where(rank < 2, fresh, reused)
    forward_head(0, 0, info_ref, q_aug, k_aug, v_aug, o_rows, lse_ref)


def attend_first(info, inputs, parts, firsts, cols):
    rows, dim = inputs[0].shape
    wide = parts[0].shape[2]
    heads = cols // HD
    seq = 4 * rows
    work = seq * (seq + BLK) // 2
    return call(
        first_kernel,
        "attend_first",
        [
            low_shape(dim, wide),
            low_shape(dim, cols),
            low_shape(heads, seq, 2 * HD),
            low_shape(heads, seq, 2 * HD),
            low_shape(heads, seq, 2 * HD),
            low_shape(heads, HD, seq),
            low_shape(1, seq, HD),
            wide_shape(1, 1, seq),
        ],
        [SMEM] + [VMEM] * (8 + len(parts)),
        [],
        16 * work * HD + 2 * seq * dim * wide,
        work,
        (info, *inputs, *firsts, *parts),
    )


def rest_kernel(
    info_ref, q_aug, k_aug, v_aug, o_first, lse_first, own_ref, core_ref, pair_ref, lse_ref, o_rows, lse_part
):
    rows, cols = own_ref.shape
    heads = cols // HD

    def per_head(head, carry):
        forward_head(head + 1, head, info_ref, q_aug, k_aug, v_aug, o_rows, lse_part)
        return carry

    lax.fori_loop(0, heads - 1, per_head, 0)
    lse_ref[0] = lse_first[0]
    for head in range(1, heads):
        lse_ref[head] = lse_part[head - 1]
    for rel, (out, first) in enumerate(((own_ref, 0), (core_ref, 0), (pair_ref, 0), (pair_ref, cols))):
        span = pl.ds(place(info_ref, rel, rows), rows)
        out[:, first : first + HD] = o_first[0, span, :]
        for head in range(1, heads):
            at = first + head * HD
            out[:, at : at + HD] = o_rows[head - 1, span, :]


def attend_rest(info, q_aug, k_aug, v_aug, o_first, lse_first):
    heads, seq = q_aug.shape[:2]
    rows, cols = seq // 4, heads * HD
    work = (heads - 1) * seq * (seq + BLK) // 2
    return call(
        rest_kernel,
        "attend_rest",
        [
            low_shape(rows, cols),
            low_shape(rows, cols),
            low_shape(rows, 2 * cols),
            wide_shape(heads, 1, seq),
        ],
        [SMEM] + [VMEM] * 5,
        [pltpu.VMEM((heads - 1, seq, HD), jnp.bfloat16), pltpu.VMEM((heads - 1, 1, seq), jnp.float32)],
        16 * work * HD,
        work,
        (info, q_aug, k_aug, v_aug, o_first, lse_first),
    )


def backward_kernel(
    info_ref, q_aug, k_aug, v_aug, k_t, g0, g1, g2, g3, own_ref, core_ref, pair_ref, lse_ref,
    dqkv_ref, dv_own, dv_core, dv_pair, g_aug, dq_t, dk_acc, dv_acc,
):
    rows, cols = own_ref.shape
    grads = ((g0, 0), (g1, 0), (g2, 0), (g3, cols))
    outs = ((own_ref, 0), (core_ref, 0), (pair_ref, 0), (pair_ref, cols))
    dv_outs = ((dv_own, 0), (dv_core, 0), (dv_pair, 0), (dv_pair, cols))
    heads, seq = q_aug.shape[:2]
    lane = lax.broadcasted_iota(jnp.int32, (rows, HD), 1)
    for head in range(heads):
        at = head * HD
        for rel in range(4):
            span = pl.ds(place(info_ref, rel, rows), rows)
            src, first = grads[rel]
            grad = src[:, first + at : first + at + HD]
            g_aug[head, span, :HD] = grad
            src, first = outs[rel]
            products = grad.astype(jnp.float32) * src[:, first + at : first + at + HD].astype(jnp.float32)
            left = -jnp.sum(products, axis=1, keepdims=True)
            part = jnp.zeros((rows, HD), jnp.bfloat16)
            for piece in range(3):
                low = left.astype(jnp.bfloat16)
                part = jnp.where(lane == piece, low, part)
                left = left - low.astype(jnp.float32)
            g_aug[head, span, HD:] = part

    def per_head(head, carry):
        for block in range(seq // BLK):
            lo, hi = block * BLK, (block + 1) * BLK
            probs = jnp.exp(nt(k_aug[head, lo:hi, :], q_aug[head, lo:, :]) - lse_ref[head, :, lo:])
            first = jnp.where(diag_allowed(info_ref[2 + block], 1), probs[:, :BLK], 0.0)
            probs = first if hi == seq else jnp.concatenate([first, probs[:, BLK:]], axis=1)
            grad_probs = nt(v_aug[head, lo:hi, :], g_aug[head, lo:, :])
            grad_scores = (probs * grad_probs).astype(jnp.bfloat16)
            dv_acc[head, lo:hi, :] = nn(probs.astype(jnp.bfloat16), g_aug[head, lo:, :])[:, :HD].astype(
                jnp.bfloat16
            )
            dk_acc[head, lo:hi, :] = nn(grad_scores, q_aug[head, lo:, :])[:, :HD].astype(jnp.bfloat16)
            part = nn(k_t[head, :, lo:hi], grad_scores)
            if block:
                dq_t[head, :, lo:] += part
            else:
                dq_t[head, :, :] = part
        return carry

    lax.fori_loop(0, heads, per_head, 0)
    fresh = info_ref[0] < 2
    for rel in range(4):
        span = pl.ds(place(info_ref, rel, rows), rows)
        part = dq_t[:, :, span].reshape(cols, rows)
        dqkv_ref[rel, :, :cols] = (part.T * (1.0 / math.sqrt(HD))).astype(dqkv_ref.dtype)
        for head in range(heads):
            at = head * HD
            dqkv_ref[rel, :, cols + at : cols + at + HD] = dk_acc[head, span, :]
            value = dv_acc[head, span, :]
            out, first = dv_outs[rel]
            out[:, first + at : first + at + HD] = value
            kept = jnp.where(fresh, value, jnp.zeros_like(value))
            dqkv_ref[rel, :, 2 * cols + at : 2 * cols + at + HD] = kept


def attend_back(info, prepared, grads, outs, lse):
    heads, seq = prepared[0].shape[:2]
    rows, cols = seq // 4, heads * HD
    work = heads * seq * (seq + BLK) // 2
    return call(
        backward_kernel,
        "attend_back",
        [
            low_shape(4, rows, 3 * cols),
            low_shape(rows, cols),
            low_shape(rows, cols),
            low_shape(rows, 2 * cols),
        ],
        [SMEM] + [VMEM] * 12,
        [
            pltpu.VMEM((heads, seq, 2 * HD), jnp.bfloat16),
            pltpu.VMEM((heads, HD, seq), jnp.float32),
            pltpu.VMEM((heads, seq, HD), jnp.bfloat16),
            pltpu.VMEM((heads, seq, HD), jnp.bfloat16),
        ],
        40 * work * HD,
        work,
        (info, *prepared, *grads, *outs, lse),
        20,
    )


def norm_stats(wide):
    centred = wide - jnp.mean(wide, axis=-1, keepdims=True)
    inv_std = lax.rsqrt(jnp.mean(centred * centred, axis=-1, keepdims=True) + EPS)
    return centred * inv_std, inv_std


def valid_rows(info_ref, rows, start, count):
    pos = info_ref[0] * rows + start + lax.broadcasted_iota(jnp.int32, (count, 1), 0)
    return (pos < info_ref[1]).astype(jnp.float32)


def row_sum(v):
    return jnp.sum(v, axis=0, keepdims=True)


def middle_kernel(
    info_ref, tok_ref, h0, h1, h2, h3, w0, w1, w2, w3, gain_ref, resid_ref, input_ref, square_ref
):
    rows = tok_ref.shape[0]
    cols = h0.shape[1]
    square_ref[...] = jnp.zeros_like(square_ref)

    def tile(span):
        attn = nt(h0[span], w0[...]) + nt(h1[span], w1[...])
        attn = attn + nt(h2[span, :cols], w2[...]) + nt(h3[span, cols:], w3[...])
        resid = tok_ref[span].astype(jnp.float32) + attn
        resid_ref[span] = resid
        normed, _ = norm_stats(resid)
        input_ref[span] = (normed * gain_ref[...]).astype(input_ref.dtype)
        square_ref[...] += row_sum(attn * attn * valid_rows(info_ref, rows, span.start, BLK))

    loop(rows, tile)


def middle(info, tokens, heads, weights, gain):
    rows, dim = tokens.shape
    return call(
        middle_kernel,
        "middle",
        [wide_shape(rows, dim), low_shape(rows, dim), wide_shape(1, dim)],
        [SMEM] + [VMEM] * 10,
        [],
        2 * rows * dim * dim,
        rows,
        (info, tokens, *heads, *weights, gain),
    )


GELU_C = math.sqrt(2.0 / math.pi)
CUBE = 0.044715


def mlp_tiles(xs, cots, w_ref, hid_ref, dup_ref, backs, outs):
    rows = xs[0].shape[0]
    up_cols = w_ref.shape[1] // 2
    up_w, down_t = w_ref.at[:, :up_cols], w_ref.at[:, up_cols:]
    for block in range(len(xs)):

        def tile(span, block=block):
            up = nn(xs[block][span], up_w[...])
            up2 = up * up
            th = jnp.tanh(GELU_C * up * (1.0 + CUBE * up2))
            half = 0.5 * (1.0 + th)
            hidden = (up * half).astype(jnp.bfloat16)
            hid_ref[block, span] = hidden
            slope = half + 0.5 * up * (1.0 - th * th) * (GELU_C * (1.0 + 3.0 * CUBE * up2))
            dup = (nn(cots[block][span], down_t[...]) * slope).astype(jnp.bfloat16)
            dup_ref[block, span] = dup
            backs[block][span] = nt(dup, up_w[...]).astype(jnp.bfloat16)
            if outs:
                outs[block][span] = nt(hidden, down_t[...]).astype(jnp.bfloat16)

        loop(rows, tile)


def mlp_near_kernel(x0, x1, c0, c1, w_ref, hid_ref, dup_ref, b0, b1, o0, o1):
    mlp_tiles((x0, x1), (c0, c1), w_ref, hid_ref, dup_ref, (b0, b1), (o0, o1))


def mlp_far_kernel(x_ref, c_ref, w_ref, hid_ref, dup_ref, back_ref):
    mlp_tiles((x_ref,), (c_ref,), w_ref, hid_ref, dup_ref, (back_ref,), ())


def mlp_near(xs, cots, weights):
    rows, dim = xs[0].shape
    wide = weights.shape[1]
    return call(
        mlp_near_kernel,
        "mlp_near",
        [low_shape(2, rows, wide // 2)] * 2 + [low_shape(rows, dim)] * 4,
        [VMEM] * 5,
        [],
        8 * rows * dim * wide,
        rows * wide,
        (*xs, *cots, weights),
    )


def mlp_far(x, cot, weights):
    rows, dim = x.shape
    wide = weights.shape[1]
    return call(
        mlp_far_kernel,
        "mlp_far",
        [low_shape(1, rows, wide // 2)] * 2 + [low_shape(rows, dim)],
        [VMEM] * 3,
        [],
        3 * rows * dim * wide,
        rows * wide // 2,
        (x, cot, weights),
    )


def mlp_grads_kernel(
    up_cols, x0, x1, x2, x3, c0, c1, c2, c3, h_a, h_x, h_d, d_a, d_x, d_d, w_ref, g_ref, o0, o1
):
    down_t = w_ref.at[:, up_cols : 2 * up_cols]
    step = 2 * BLK
    for far, out in ((h_x, o0), (h_d, o1)):
        out[...] = nt(far[0], down_t[...]).astype(out.dtype)
    for start in range(0, up_cols, BLK):
        span = slice(start, start + BLK)
        acc = tn(x0[...], d_a[0, :, span]) + tn(x1[...], d_a[1, :, span])
        acc = acc + tn(x2[...], d_x[0, :, span]) + tn(x3[...], d_d[0, :, span])
        g_ref[:, span] = acc.astype(g_ref.dtype)
        acc = tn(c0[...], h_a[0, :, span]) + tn(c1[...], h_a[1, :, span])
        acc = acc + tn(c2[...], h_x[0, :, span]) + tn(c3[...], h_d[0, :, span])
        g_ref[:, up_cols + start : up_cols + start + BLK] = acc.astype(g_ref.dtype)


def mlp_grads(xs, cots, hids, dups, weights, up_cols):
    rows, dim = xs[0].shape
    return call(
        functools.partial(mlp_grads_kernel, up_cols),
        "mlp_grads",
        [low_shape(dim, 2 * up_cols), low_shape(rows, dim), low_shape(rows, dim)],
        [VMEM] * 15,
        [],
        20 * rows * dim * up_cols,
        0,
        (*xs, *cots, *hids, *dups, weights),
    )


def turn_kernel(
    resid_ref, cot_ref, b0, b1, b2, gain_ref, w0, w1, w2, w3,
    grad_ref, low_ref, d_own, d_core, d_pair, gain_out,
):
    rows = resid_ref.shape[0]
    cols = d_own.shape[1]
    gain_out[...] = jnp.zeros_like(gain_out)

    def tile(span):
        normed, inv_std = norm_stats(resid_ref[span])
        back = b0[span].astype(jnp.float32) + b1[span].astype(jnp.float32)
        back = back + b2[span].astype(jnp.float32)
        gain_out[...] += row_sum(back * normed)
        scaled = back * gain_ref[...]
        inner = scaled - jnp.mean(scaled, axis=-1, keepdims=True)
        inner = inner - normed * jnp.mean(scaled * normed, axis=-1, keepdims=True)
        grad = cot_ref[span].astype(jnp.float32) + inner * inv_std
        grad_ref[span] = grad
        low = grad.astype(jnp.bfloat16)
        low_ref[span] = low
        d_own[span] = nn(low, w0[...]).astype(jnp.bfloat16)
        d_core[span] = nn(low, w1[...]).astype(jnp.bfloat16)
        d_pair[span, :cols] = nn(low, w2[...]).astype(jnp.bfloat16)
        d_pair[span, cols:] = nn(low, w3[...]).astype(jnp.bfloat16)

    loop(rows, tile)


def turn(resid, cot, backs, gain, weights):
    rows, dim = cot.shape
    cols = weights[0].shape[1]
    return call(
        turn_kernel,
        "turn",
        [
            wide_shape(rows, dim),
            low_shape(rows, dim),
            low_shape(rows, cols),
            low_shape(rows, cols),
            low_shape(rows, 2 * cols),
            wide_shape(1, dim),
        ],
        [VMEM] * 10,
        [],
        2 * rows * dim * dim,
        rows,
        (resid, cot, *backs, gain, *weights),
    )


def out_grads_kernel(low_ref, h0, h1, h2, h3, o_near, o_far):
    cols = h0.shape[1]
    low = low_ref[...]
    o_near[:, :cols] = tn(low, h0[...])
    o_far[:, :cols] = tn(low, h1[...]).astype(jnp.bfloat16)
    o_near[:, cols:] = tn(low, h2[:, :cols])
    o_far[:, cols:] = tn(low, h3[:, cols:]).astype(jnp.bfloat16)


def out_grads(low, heads):
    rows, dim = low.shape
    cols = heads[0].shape[1]
    return call(
        out_grads_kernel,
        "out_grads",
        [wide_shape(dim, 2 * cols), low_shape(dim, 2 * cols)],
        [VMEM] * 5,
        [],
        2 * rows * dim * dim,
        0,
        (low, *heads),
    )


def slot_sum_kernel(near_ref, far_ref, out_ref):
    cols = out_ref.shape[1]
    out_ref[...] = (near_ref[:, cols:] + far_ref[:, cols:].astype(jnp.float32)).astype(out_ref.dtype)


def slot_sum(near, far):
    dim, wide = near.shape
    return call(
        slot_sum_kernel, "slot_sum", [low_shape(dim, wide // 2)], [VMEM] * 2, [], dim * wide, 0, (near, far)
    )[0]


def input_grads_kernel(dqkv_ref, w_ref, o0, o1, o2, o3):
    rows, wide = dqkv_ref.shape[1:]
    for rel, out in ((2, o2), (3, o3), (0, o0), (1, o1)):

        def tile(span, rel=rel, out=out):
            out[span] = nt(dqkv_ref[rel, span], w_ref[:, :wide]).astype(out.dtype)

        loop(rows, tile)


def input_grads(dqkv, weights):
    rows, cols = dqkv.shape[1:]
    dim = weights.shape[0]
    return call(
        input_grads_kernel,
        "input_grads",
        [low_shape(rows, dim)] * 4,
        [VMEM] * 2,
        [],
        8 * rows * dim * cols,
        0,
        (dqkv, weights),
    )


def qkv_grads_kernel(
    info_ref, x0, x1, x2, x3, dqkv_ref, near_ref, far_ref, far_x, small_ref, w_ref, gain_ref, *refs
):
    *outs, all_ref = refs
    wide = dqkv_ref.shape[2]
    cols = wide // 3
    acc = tn(x0[...], dqkv_ref[0]) + tn(x1[...], dqkv_ref[1])
    acc = acc + tn(x2[...], dqkv_ref[2]) + tn(x3[...], dqkv_ref[3])
    all_ref[:, :wide] = acc.astype(all_ref.dtype)
    total = near_ref[:, :cols] + far_ref[:, :cols].astype(jnp.float32)
    total = total + far_x[...].astype(jnp.float32)
    all_ref[:, wide:] = total.astype(all_ref.dtype)
    products = acc * w_ref[:, :wide].astype(jnp.float32)
    low = products.astype(jnp.bfloat16)
    ones = jnp.ones((8, wide), jnp.bfloat16)
    sums = nt(ones, low) + nt(ones, (products - low.astype(jnp.float32)).astype(jnp.bfloat16))
    sums = sums[:1] / gain_ref[...]
    low = sums.astype(jnp.bfloat16)
    row = lax.broadcasted_iota(jnp.int32, small_ref.shape, 0)
    small = jnp.where(row == 0, low, small_ref[...])
    small = jnp.where(row == 8, (sums - low.astype(jnp.float32)).astype(jnp.bfloat16), small)
    if len(outs) == 1:
        outs[0][0, : all_ref.shape[0]] = all_ref[...]
        outs[0][0, all_ref.shape[0] :] = small
        return
    half = info_ref[2 + 4 * x0.shape[0] // BLK]
    count, full = outs[0].shape[:2]
    shard = full - small.shape[0]
    for parity, out in ((half, outs[0]), (1 - half, outs[1])):
        for part in range(count):
            start = pl.multiple_of((2 * part + parity) * shard, shard)
            out[part, :shard] = all_ref[pl.ds(start, shard), :]
            out[part, shard:] = small


def qkv_grads(info, xs, dqkv, near, far, far_x, small, weights, gain, count):
    rows, dim = xs[0].shape
    wide = dqkv.shape[2]
    full = wide + wide // 3
    extra = small.shape[0]
    if count == 1:
        outs = [low_shape(1, dim + extra, full)]
    else:
        outs = [low_shape(count // 2, dim // count + extra, full)] * 2
    return call(
        qkv_grads_kernel,
        "qkv_grads",
        outs,
        [SMEM] + [VMEM] * 11,
        [pltpu.VMEM((dim, full), jnp.bfloat16)],
        8 * rows * dim * wide,
        0,
        (info, *xs, dqkv, near, far, far_x, small, weights, gain),
    )


def fold_kernel(shard, info_ref, a_ref, b_ref, *outs):
    line = info_ref[info_ref.shape[0] - 1]
    for step, out in enumerate(outs):
        part = line ^ step
        total = a_ref[part, :shard].astype(jnp.float32) + b_ref[part, :shard].astype(jnp.float32)
        out[:shard] = total.astype(out.dtype)
        total = a_ref[part, shard:].astype(jnp.float32) + b_ref[part, shard:].astype(jnp.float32)
        half = total.shape[0] // 2
        wide = total[:half] + total[half:]
        low = wide.astype(jnp.bfloat16)
        rest = (wide - low.astype(jnp.float32)).astype(jnp.bfloat16)
        out[shard:] = jnp.concatenate([low, rest], axis=0)


def fold(info, a, b, shard):
    count, full, wide = a.shape
    return call(
        functools.partial(fold_kernel, shard), "fold", [low_shape(full, wide)] * count,
        [SMEM] + [VMEM] * 2, [], a.size, 0, (info, a, b),
    )


def finish_kernel(tok_ref, grad_ref, b0, b1, b2, gain_ref, out_ref):

    def tile(span):
        normed, inv_std = norm_stats(tok_ref[span].astype(jnp.float32))
        back = b0[span].astype(jnp.float32) + b1[span].astype(jnp.float32)
        back = back + b2[span].astype(jnp.float32)
        scaled = back * gain_ref[...]
        inner = scaled - jnp.mean(scaled, axis=-1, keepdims=True)
        inner = inner - normed * jnp.mean(scaled * normed, axis=-1, keepdims=True)
        out_ref[span] = grad_ref[span] + inner * inv_std

    loop(tok_ref.shape[0], tile)


def finish(tokens, grad, backs, gain):
    rows, dim = tokens.shape
    return call(
        finish_kernel,
        "finish",
        [wide_shape(rows, dim)],
        [VMEM] * 6,
        [],
        rows * dim * 20,
        rows,
        (tokens, grad, *backs, gain),
    )[0]


def norm_kernel(t0, t1, gain_ref, o0, o1):
    for src, out in ((t0, o0), (t1, o1)):

        def tile(span, src=src, out=out):
            normed, _ = norm_stats(src[span].astype(jnp.float32))
            out[span] = (normed * gain_ref[...]).astype(out.dtype)

        loop(t0.shape[0], tile)


def norms(blocks, gain):
    rows, dim = blocks[0].shape
    return call(
        norm_kernel,
        "norms",
        [low_shape(rows, dim)] * 2,
        [VMEM] * 3,
        [],
        rows * dim * 20,
        rows,
        (*blocks, gain),
    )


def share_kernel(shard, parts_ref, *outs):
    cols = outs[0].shape[1]
    for at, out in enumerate(outs):
        if out.shape[0] != shard:
            break
        span = slice(at * cols, (at + 1) * cols)
        total = parts_ref[0, :shard, span].astype(jnp.float32)
        for part in range(1, parts_ref.shape[0]):
            total = total + parts_ref[part, :shard, span].astype(jnp.float32)
        out[...] = total
    if parts_ref.shape[1] > shard:
        total = parts_ref[0, shard:].astype(jnp.float32)
        for part in range(1, parts_ref.shape[0]):
            total = total + parts_ref[part, shard:].astype(jnp.float32)
        half = total.shape[0] // 2
        outs[-1][...] = total[:half] + total[half:]


def shares(parts, shard, cols, name):
    count, full, wide = parts.shape
    outs = [wide_shape(shard, cols)] * (wide // cols)
    if full > shard:
        outs.append(wide_shape((full - shard) // 2, wide))
    return call(
        functools.partial(share_kernel, shard),
        name,
        outs,
        [VMEM],
        [],
        count * full * wide,
        0,
        (parts,),
    )


def tail_kernel(count, *refs):
    parts, (q_out, k_out, o_out, mix_ref) = refs[:count], refs[count:]
    shard, cols = q_out.shape
    wide = mix_ref.shape[1]

    def total(rows, span):
        acc = parts[0][rows, span].astype(jnp.float32)
        for part in parts[1:]:
            acc = acc + part[rows, span].astype(jnp.float32)
        return acc

    first = slice(0, shard)
    q_out[...] = total(first, slice(0, cols))
    k_out[...] = total(first, slice(cols, 2 * cols))
    o_out[...] = total(first, slice(3 * cols, 4 * cols)).T
    small = total(slice(shard, shard + 16), slice(0, wide))
    mix_ref[:8] = small[:8] + small[8:]
    value = total(first, slice(2 * cols, 3 * cols))
    height = shard // 4
    for at in range(4):
        mix_ref[8:, at * cols : (at + 1) * cols] = value[at * height : (at + 1) * height]


def tail_shares(parts, shard, cols):
    full, wide = parts[0].shape
    return call(
        functools.partial(tail_kernel, len(parts)),
        "tail_shares",
        [
            wide_shape(shard, cols),
            wide_shape(shard, cols),
            wide_shape(cols, shard),
            wide_shape(8 + shard // 4, wide),
        ],
        [VMEM] * len(parts),
        [],
        len(parts) * full * wide,
        0,
        tuple(parts),
    )


def meet_kernel(info_ref, own_ref, peer_ref, out_ref):
    out_ref[:8] = own_ref[:8] + peer_ref[:8]
    out_ref[8:] = jnp.where(info_ref[0] < 2, own_ref[8:], peer_ref[8:])


def meet(info, own, peer):
    return call(
        meet_kernel, "meet", [wide_shape(*own.shape)], [SMEM] + [VMEM] * 2, [], own.size, 0, (info, own, peer)
    )[0]


def last_kernel(info_ref, own_ref, peer_ref, value_ref, gain_one, gain_two, rms_ref):
    dim = own_ref.shape[1]
    cols = dim // 4
    total = own_ref[:8] + peer_ref[:8]
    gain_one[...] = total[0:1]
    gain_two[...] = total[1:2]
    sums = jnp.sum(total, axis=1, keepdims=True)
    roots = jnp.sqrt(sums / (sums[5:6] * dim))
    lane = lax.broadcasted_iota(jnp.int32, rms_ref.shape, 1)
    rms_ref[...] = jnp.where(lane == 0, roots[2:3], jnp.where(lane == 1, roots[3:4], roots[4:5]))
    even = info_ref[0] % 2 == 0
    own, peer = own_ref[8:], peer_ref[8:]
    lower, upper = jnp.where(even, own, peer), jnp.where(even, peer, own)
    height = own.shape[0]
    for at in range(4):
        rows, span = slice(at * height, (at + 1) * height), slice(at * cols, (at + 1) * cols)
        value_ref[rows, :cols] = lower[:, span]
        value_ref[rows, cols:] = upper[:, span]


def last(info, own, peer):
    dim = own.shape[1]
    return call(
        last_kernel,
        "last",
        [wide_shape(4 * (own.shape[0] - 8), dim // 2), wide_shape(1, dim), wide_shape(1, dim), wide_shape(1, LANES)],
        [SMEM] + [VMEM] * 2,
        [],
        own.size,
        0,
        (info, own, peer),
    )


def output_kernel(info_ref, resid_ref, b0, b1, b2, attn_sq, gain_two, out_ref, small_ref, *sums):
    rows, dim = resid_ref.shape
    final_sum, mlp_sum = sums
    final_sum[...] = jnp.zeros_like(final_sum)
    mlp_sum[...] = jnp.zeros_like(mlp_sum)

    def tile(span):
        valid = valid_rows(info_ref, rows, span.start, BLK)
        mlp_out = b0[span].astype(jnp.float32) + b1[span].astype(jnp.float32)
        mlp_out = mlp_out + b2[span].astype(jnp.float32)
        final = resid_ref[span] + mlp_out
        out_ref[span] = final.astype(out_ref.dtype)
        final_sum[...] += row_sum(final * final * valid)
        mlp_sum[...] += row_sum(mlp_out * mlp_out * valid)

    loop(rows, tile)
    count = jnp.clip(info_ref[1] - info_ref[0] * rows, 0, rows).astype(jnp.float32)
    lane = lax.broadcasted_iota(jnp.int32, (1, dim), 1)
    counts = jnp.where(lane == 0, count, 0.0)
    row = lax.broadcasted_iota(jnp.int32, (8, dim), 0)
    wide = jnp.zeros((8, dim), jnp.float32)
    values = (jnp.zeros_like(gain_two), gain_two[...], final_sum[...], attn_sq[...], mlp_sum[...], counts)
    for at, value in enumerate(values):
        wide = jnp.where(row == at, value, wide)
    low = wide.astype(jnp.bfloat16)
    small_ref[...] = jnp.concatenate([low, (wide - low.astype(jnp.float32)).astype(jnp.bfloat16)], axis=0)


def output(info, resid, parts, sums):
    rows, dim = resid.shape
    return call(
        output_kernel,
        "output",
        [low_shape(rows, dim), low_shape(16, dim)],
        [SMEM] + [VMEM] * 6,
        [pltpu.VMEM((1, dim), jnp.float32)] * 2,
        rows * dim * 10,
        0,
        (info, resid, *parts, *sums),
    )


def pack_early_kernel(info_ref, wq, wk, wv, wo, out_ref):
    cols = wq.shape[1]
    even = info_ref[0] % 2 == 0
    fresh = jnp.where(even, wv[:, :cols], wv[:, cols : 2 * cols])
    turned = wo[...].T
    for part in range(out_ref.shape[0]):
        for at, value in enumerate((wq[...], wk[...], fresh, turned)):
            out_ref[part, :, at * cols : (at + 1) * cols] = value


def pack_early(info, copies, wq, wk, wv, wo):
    shard, cols = wq.shape
    return call(
        pack_early_kernel, "pack_early", [low_shape(copies, shard, 4 * cols)],
        [SMEM] + [VMEM] * 4, [], shard * cols, 0, (info, wq, wk, wv, wo), 60,
    )[0]


X_SWAP = [(0, 2), (1, 3), (2, 0), (3, 1)]
CORE_SWAP = [(0, 1), (1, 0), (2, 3), (3, 2)]


def swap_x(v):
    return lax.ppermute(v, "tensor", X_SWAP)


def swap_core(v):
    return lax.ppermute(v, "tensor", CORE_SWAP)


def tied(value, *others):
    return lax.optimization_barrier((value, *others))[0]


def plus(a, b):
    return (a.astype(jnp.float32) + b.astype(jnp.float32)).astype(jnp.bfloat16)


def body(
    tokens,
    first_values,
    pieces,
    lengths,
    w_query,
    w_key,
    w_value,
    w_out,
    w_up,
    w_down,
    gain_attn,
    gain_mlp,
    cotangent,
):
    dp_size = lax.axis_size("dp")
    rank = lax.axis_index("tensor")
    core = rank % 2
    rows, dim = tokens.shape
    shard, cols = w_query.shape
    up_cols = w_up.shape[1]
    parity = lax.axis_index("dp") % 2
    info = jnp.concatenate(
        [
            rank[None].astype(jnp.int32),
            lengths,
            pieces[::BLK],
            parity[None].astype(jnp.int32),
            (lax.axis_index("dp") // 2)[None].astype(jnp.int32),
        ]
    )
    gain_one, gain_two = gain_attn[None], gain_mlp[None]
    pairs = [(i, i ^ 1) for i in range(dp_size)]
    lines = [list(range(first, dp_size, 2)) for first in range(2)]

    def gather_line(v):
        return lax.all_to_all(v, "dp", 0, 0, axis_index_groups=lines)

    def swap_pair(v):
        return lax.ppermute(v, "dp", pairs)

    def in_order(mine, other):
        lower = jnp.where(parity == 0, mine, other)
        upper = jnp.where(parity == 0, other, mine)
        return jnp.stack([lower, upper], axis=1).reshape(dim, -1)

    def pieces_of(mine, other):
        if shard % 16 == 0:
            return (mine, other)
        return (in_order(mine, other)[None],)

    early = pack_early(rank[None].astype(jnp.int32), dp_size // 2, w_query, w_key, w_value, w_out)
    early_mine = gather_line(early)
    tok_x = swap_x(tokens)
    tok_core = swap_core(tokens)
    xs_near = norms((tokens, tok_core), gain_one)
    early_other = swap_pair(early_mine)
    tok_diag = swap_core(tok_x)
    late = tied(jnp.concatenate([w_up, w_down.T], axis=1), tok_core)
    late_all = lax.all_gather(late, "dp", axis=0, tiled=True)
    first_x = lax.ppermute(first_values, "tensor", [(0, 2), (1, 3)])
    firsts = (first_values, swap_core(first_values), first_x, swap_core(first_x))
    xs = (*xs_near, *norms((tok_x, tok_diag), gain_one))
    early_all, out_own, *prepared, o_first, lse_first = attend_first(
        info, xs, pieces_of(early_mine, early_other), firsts, cols
    )

    out_x = swap_x(out_own)
    cot_x = swap_x(tied(cotangent, first_x))
    h_own, h_core, h_pair, lse = attend_rest(info, *prepared[:3], o_first, lse_first)
    h_pair, h_core = lax.optimization_barrier((h_pair, h_core, cot_x, out_x))[:2]
    cot_core = swap_core(cotangent)
    cot_diag = swap_core(cot_x)
    outs = (out_own, swap_core(out_own), out_x, swap_core(out_x))

    from_x = swap_x(h_pair)
    heads_mine = (h_own, swap_core(h_core), from_x, swap_core(from_x))
    resid, mlp_in, attn_sq = middle(
        info, tokens, heads_mine, outs, gain_two
    )
    in_x = swap_x(mlp_in)
    in_core = swap_core(mlp_in)
    hid_a, dup_a, back_own, back_core, out_0, out_1 = mlp_near(
        (mlp_in, in_core), (cotangent, cot_core), late_all
    )
    back_1 = swap_core(back_core)
    out_near = swap_core(out_1)
    in_far = tied(in_x, back_own)
    in_diag = swap_core(in_far)
    hid_x, dup_x, back_x = mlp_far(in_far, cot_x, late_all)
    hid_d, dup_d, back_diag = mlp_far(tied(in_diag, back_x), cot_diag, late_all)
    back_far = plus(back_x, swap_core(back_diag))
    back_2 = swap_x(back_far)
    grads_mlp, out_2, out_3 = mlp_grads(
        (mlp_in, in_core, in_x, in_diag),
        (cotangent, cot_core, cot_x, cot_diag),
        (hid_a, hid_x, tied(hid_d, back_far)), (dup_a, dup_x, dup_d), late_all, up_cols,
    )
    mlp_share = lax.psum_scatter(grads_mlp, "dp", scatter_dimension=0, tiled=True)
    out_sum = plus(out_2, swap_core(out_3))

    resid_grad, resid_low, d_own, d_core, d_pair, gain_two_sum = turn(
        resid, cotangent, (back_own, back_1, back_2), gain_two, outs
    )
    d_x = swap_x(d_pair)
    grads_heads = (d_own, swap_core(d_core), d_x, swap_core(d_x))
    near, far = out_grads(tied(resid_low, out_sum), heads_mine)
    far = swap_core(far)
    dqkv, dv_own, dv_core, dv_pair = attend_back(
        info, prepared, grads_heads, (h_own, h_core, h_pair), lse
    )
    out_from_x = swap_x(tied(out_sum, d_x))
    near_x = swap_x(tied(slot_sum(near, far), d_x))
    dqkv, dv_pair = lax.optimization_barrier((dqkv, dv_pair, out_from_x, near_x))[:2]

    first_from_x = lax.ppermute(dv_pair, "tensor", [(2, 0), (3, 1)])
    final, small = output(info, resid, (out_0, out_near, out_from_x), (attn_sq, gain_two_sum))
    b_0, b_1, b_2, b_3 = input_grads(tied(dqkv, small), early_all)
    joined = shard % 16 == 0 and dp_size <= 8
    tail = qkv_grads(
        info, xs, tied(dqkv, b_3), near, far, near_x, small, early_all, gain_one, dp_size if joined else 1
    )
    if joined:
        tail_pair = swap_pair(tail[1])
    tail_first = tail[0]
    plus_far = plus(b_2, swap_core(b_3))
    b_from_x = swap_x(plus_far)
    b_from_core = swap_core(b_1)

    first_a = jnp.where(rank < 2, first_from_x[:, :cols], dv_own)
    first_b = swap_core(jnp.where(rank < 2, first_from_x[:, cols:], dv_core))
    first_grad = jnp.where(
        core == 0,
        jnp.concatenate([first_a, first_b], axis=1),
        jnp.concatenate([first_b, first_a], axis=1),
    ).astype(jnp.float32)
    token_grad = finish(tokens, resid_grad, (b_0, b_from_core, b_from_x), gain_one)
    grad_up, grad_down_t = shares(mlp_share[None], shard, up_cols, "mlp_shares")
    if joined:
        folded = fold(info, tied(tail_first, plus_far, first_from_x), tail_pair, shard)
        tail_parts = [folded[0]] + [
            lax.ppermute(folded[step], "dp", [(i, i ^ (2 * step)) for i in range(dp_size)])
            for step in range(1, dp_size // 2)
        ]
        tail_parts[0] = tied(tail_parts[0], token_grad, grad_up, first_grad)
        grad_q, grad_k, grad_out, mix = tail_shares(tail_parts, shard, cols)
        mix = meet(info, mix, swap_x(mix))
        value_share, gain_one_sum, gain_two_total, rms = last(info, mix, swap_core(mix))
        gain_one_sum, gain_two_total = gain_one_sum.reshape(dim), gain_two_total.reshape(dim)
        rms = rms[0, :3]
    else:
        small = tail_first[0, dim:].astype(jnp.float32)
        total = lax.psum(small[:8] + small[8:], ("dp", "tensor"))
        tail_all = lax.all_to_all(tail_first[0, :dim].reshape(dp_size, shard, 4 * cols), "dp", 0, 0)
        total_grads = jnp.sum(tail_all.astype(jnp.float32), axis=0)
        grad_q, grad_k = total_grads[:, :cols], total_grads[:, cols : 2 * cols]
        grad_out = total_grads[:, 3 * cols :].T
        value_own = total_grads[:, 2 * cols : 3 * cols]
        value_here = jnp.where(rank < 2, value_own, swap_x(value_own))
        value_peer = swap_core(value_here)
        value_share = jnp.where(
            core == 0,
            jnp.concatenate([value_here, value_peer], axis=1),
            jnp.concatenate([value_peer, value_here], axis=1),
        )
        sums = jnp.sum(total, axis=1)
        rms = jnp.sqrt(sums[2:5] / (sums[5] * dim))
        gain_one_sum, gain_two_total = total[0], total[1]
    return (
        final,
        token_grad,
        first_grad,
        grad_q,
        grad_k,
        value_share,
        grad_out,
        grad_up,
        grad_down_t.T,
        gain_one_sum,
        gain_two_total,
        rms,
    )


def solution(mesh):
    in_specs = (
        P(("dp", "tensor"), None),
        P(("dp", "tensor"), None),
        P("dp"),
        P("dp"),
        P("dp", "tensor"),
        P("dp", "tensor"),
        P("dp", None),
        P("tensor", "dp"),
        P("dp", "tensor"),
        P("tensor", "dp"),
        P(),
        P(),
        P(("dp", "tensor"), None),
    )
    out_specs = (
        P(("dp", "tensor"), None),
        P(("dp", "tensor"), None),
        P(("dp", "tensor"), None),
        P("dp", "tensor"),
        P("dp", "tensor"),
        P("dp", None),
        P("tensor", "dp"),
        P("dp", "tensor"),
        P("tensor", "dp"),
        P(),
        P(),
        P(),
    )
    return jax.shard_map(body, mesh=mesh, in_specs=in_specs, out_specs=out_specs, check_vma=False)
```

```python
import functools
import math

import jax
import jax.numpy as jnp
from jax import lax
from jax.experimental import pallas as pl
from jax.experimental.pallas import tpu as pltpu
from jax.sharding import PartitionSpec as P

HD = 64
EPS = 1e-05
NEG = -1e30
BLK = 256
LANES = 128

SMEM = pl.BlockSpec(memory_space=pltpu.SMEM)
VMEM = pl.BlockSpec(memory_space=pltpu.VMEM)


def nt(a, b):
    return lax.dot_general(a, b, (((1,), (1,)), ((), ())), preferred_element_type=jnp.float32)


def nn(a, b):
    return jnp.dot(a, b, preferred_element_type=jnp.float32)


def tn(a, b):
    return lax.dot_general(a, b, (((0,), (0,)), ((), ())), preferred_element_type=jnp.float32)


WEIGHTS = {"attend_back": 0.6, "input_grads": 0.01, "output": 0.01, "mlp_shares": 0.01, "tail_shares": 0.01, "finish": 0.01, "fold": 0.01}


def call(kernel, name, outs, specs, scratch, flops, exps, args, vmem=12):
    weight = WEIGHTS.get(name, 3.0)
    moved = sum(math.prod(v.shape) * v.dtype.itemsize for v in list(args) + list(outs))
    return pl.pallas_call(
        kernel,
        name=name,
        out_shape=tuple(outs),
        in_specs=specs,
        out_specs=tuple(VMEM for _ in outs),
        scratch_shapes=scratch,
        compiler_params=pltpu.CompilerParams(vmem_limit_bytes=vmem << 20),
        cost_estimate=pl.CostEstimate(
            flops=int(flops * weight),
            transcendentals=int(exps * weight),
            bytes_accessed=int(moved * weight),
        ),
    )(*args)


def low_shape(*shape):
    return jax.ShapeDtypeStruct(shape, jnp.bfloat16)


def wide_shape(*shape):
    return jax.ShapeDtypeStruct(shape, jnp.float32)


def loop(count, body):
    def step(tile, carry):
        body(pl.ds(pl.multiple_of(tile * BLK, BLK), BLK))
        return carry

    lax.fori_loop(0, count // BLK, step, 0)


def diag_allowed(picture, query_axis):
    query_pos = lax.broadcasted_iota(jnp.int32, (BLK, BLK), query_axis)
    key_pos = lax.broadcasted_iota(jnp.int32, (BLK, BLK), 1 - query_axis)
    return (key_pos <= query_pos) | (picture > 0)


def place(info_ref, rel, rows):
    return pl.multiple_of((info_ref[0] ^ rel) * rows, rows)


def assemble(dst_ref, parts, half):
    if len(parts) == 1:
        dst_ref[...] = parts[0][0]
        return
    mine, other = parts
    count, shard = mine.shape[:2]
    for part in range(count):
        dst_ref[pl.ds(pl.multiple_of((2 * part + half) * shard, shard), shard), :] = mine[part]
        dst_ref[pl.ds(pl.multiple_of((2 * part + 1 - half) * shard, shard), shard), :] = other[part]


def forward_head(head, slot, info_ref, q_aug, k_aug, v_aug, o_rows, lse_ref):
    seq = q_aug.shape[1]
    for block in range(seq // BLK):
        lo, hi = block * BLK, (block + 1) * BLK
        scores = nt(q_aug[head, lo:hi, :], k_aug[head, :hi, :])
        last = jnp.where(diag_allowed(info_ref[2 + block], 0), scores[:, lo:], NEG)
        row_max = jnp.max(last, axis=1, keepdims=True)
        if block:
            row_max = jnp.maximum(row_max, jnp.max(scores[:, :lo], axis=1, keepdims=True))
        acc = nn(jnp.exp(last - row_max).astype(jnp.bfloat16), v_aug[head, lo:hi, :])
        if block:
            front = jnp.exp(scores[:, :lo] - row_max).astype(jnp.bfloat16)
            acc = acc + nn(front, v_aug[head, :lo, :])
        total = acc[:, HD : HD + 1]
        o_rows[slot, lo:hi, :] = (acc[:, :HD] / total).astype(o_rows.dtype)
        lse = row_max + jnp.log(total)
        lse_ref[slot, :, lo:hi] = jnp.broadcast_to(lse, (BLK, LANES)).T[:1]


def first_kernel(info_ref, x0, x1, x2, x3, f0, f1, f2, f3, *refs):
    *parts, w_ref, out_w, q_aug, k_aug, v_aug, k_t, o_rows, lse_ref = refs
    inputs, firsts = (x0, x1, x2, x3), (f0, f1, f2, f3)
    rows = x0.shape[0]
    seq = 4 * rows
    heads = q_aug.shape[0]
    cols = heads * HD
    rank = info_ref[0]
    assemble(w_ref, parts, info_ref[2 + seq // BLK])
    out_w[...] = w_ref[:, 3 * cols :]
    lane = lax.broadcasted_iota(jnp.int32, (seq, HD), 1)
    pos = lax.broadcasted_iota(jnp.int32, (seq, HD), 0)
    bias = jnp.where((lane == 0) & (pos >= info_ref[1]), NEG, 0.0).astype(jnp.bfloat16)
    one = jnp.where(lane == 0, 1.0, 0.0).astype(jnp.bfloat16)
    ones = jnp.where(lane < 3, 1.0, 0.0).astype(jnp.bfloat16)
    for head in range(heads):
        q_aug[head, :, HD:] = one
        k_aug[head, :, HD:] = bias
        v_aug[head, :, HD:] = ones
    for rel in range(4):
        span = pl.ds(place(info_ref, rel, rows), rows)
        part = nn(inputs[rel][...], w_ref[:, : 3 * cols])
        for head in range(heads):
            at = head * HD
            q_aug[head, span, :HD] = part[:, at : at + HD].astype(jnp.bfloat16) * jnp.bfloat16(
                1.0 / math.sqrt(HD)
            )
            keys = part[:, cols + at : cols + at + HD].astype(jnp.bfloat16)
            k_aug[head, span, :HD] = keys
            k_t[head, :, span] = keys.T
            reused = jnp.where(
                rank % 2 == 0, firsts[rel][:, at : at + HD], firsts[rel][:, cols + at : cols + at + HD]
            )
            fresh = part[:, 2 * cols + at : 2 * cols + at + HD].astype(jnp.bfloat16)
            v_aug[head, span, :HD] = jnp.where(rank < 2, fresh, reused)
    forward_head(0, 0, info_ref, q_aug, k_aug, v_aug, o_rows, lse_ref)


def attend_first(info, inputs, parts, firsts, cols):
    rows, dim = inputs[0].shape
    wide = parts[0].shape[2]
    heads = cols // HD
    seq = 4 * rows
    work = seq * (seq + BLK) // 2
    return call(
        first_kernel,
        "attend_first",
        [
            low_shape(dim, wide),
            low_shape(dim, cols),
            low_shape(heads, seq, 2 * HD),
            low_shape(heads, seq, 2 * HD),
            low_shape(heads, seq, 2 * HD),
            low_shape(heads, HD, seq),
            low_shape(1, seq, HD),
            wide_shape(1, 1, seq),
        ],
        [SMEM] + [VMEM] * (8 + len(parts)),
        [],
        16 * work * HD + 2 * seq * dim * wide,
        work,
        (info, *inputs, *firsts, *parts),
    )


def rest_kernel(
    info_ref, q_aug, k_aug, v_aug, o_first, lse_first, own_ref, core_ref, pair_ref, lse_ref, o_rows, lse_part
):
    rows, cols = own_ref.shape
    heads = cols // HD

    def per_head(head, carry):
        forward_head(head + 1, head, info_ref, q_aug, k_aug, v_aug, o_rows, lse_part)
        return carry

    lax.fori_loop(0, heads - 1, per_head, 0)
    lse_ref[0] = lse_first[0]
    for head in range(1, heads):
        lse_ref[head] = lse_part[head - 1]
    for rel, (out, first) in enumerate(((own_ref, 0), (core_ref, 0), (pair_ref, 0), (pair_ref, cols))):
        span = pl.ds(place(info_ref, rel, rows), rows)
        out[:, first : first + HD] = o_first[0, span, :]
        for head in range(1, heads):
            at = first + head * HD
            out[:, at : at + HD] = o_rows[head - 1, span, :]


def attend_rest(info, q_aug, k_aug, v_aug, o_first, lse_first):
    heads, seq = q_aug.shape[:2]
    rows, cols = seq // 4, heads * HD
    work = (heads - 1) * seq * (seq + BLK) // 2
    return call(
        rest_kernel,
        "attend_rest",
        [
            low_shape(rows, cols),
            low_shape(rows, cols),
            low_shape(rows, 2 * cols),
            wide_shape(heads, 1, seq),
        ],
        [SMEM] + [VMEM] * 5,
        [pltpu.VMEM((heads - 1, seq, HD), jnp.bfloat16), pltpu.VMEM((heads - 1, 1, seq), jnp.float32)],
        16 * work * HD,
        work,
        (info, q_aug, k_aug, v_aug, o_first, lse_first),
    )


def backward_kernel(
    info_ref, q_aug, k_aug, v_aug, k_t, g0, g1, g2, g3, own_ref, core_ref, pair_ref, lse_ref,
    dqkv_ref, dv_own, dv_core, dv_pair, g_aug, dq_t, dk_acc, dv_acc,
):
    rows, cols = own_ref.shape
    grads = ((g0, 0), (g1, 0), (g2, 0), (g3, cols))
    outs = ((own_ref, 0), (core_ref, 0), (pair_ref, 0), (pair_ref, cols))
    dv_outs = ((dv_own, 0), (dv_core, 0), (dv_pair, 0), (dv_pair, cols))
    heads, seq = q_aug.shape[:2]
    lane = lax.broadcasted_iota(jnp.int32, (rows, HD), 1)
    for head in range(heads):
        at = head * HD
        for rel in range(4):
            span = pl.ds(place(info_ref, rel, rows), rows)
            src, first = grads[rel]
            grad = src[:, first + at : first + at + HD]
            g_aug[head, span, :HD] = grad
            src, first = outs[rel]
            products = grad.astype(jnp.float32) * src[:, first + at : first + at + HD].astype(jnp.float32)
            left = -jnp.sum(products, axis=1, keepdims=True)
            part = jnp.zeros((rows, HD), jnp.bfloat16)
            for piece in range(3):
                low = left.astype(jnp.bfloat16)
                part = jnp.where(lane == piece, low, part)
                left = left - low.astype(jnp.float32)
            g_aug[head, span, HD:] = part

    def per_head(head, carry):
        for block in range(seq // BLK):
            lo, hi = block * BLK, (block + 1) * BLK
            probs = jnp.exp(nt(k_aug[head, lo:hi, :], q_aug[head, lo:, :]) - lse_ref[head, :, lo:])
            first = jnp.where(diag_allowed(info_ref[2 + block], 1), probs[:, :BLK], 0.0)
            probs = first if hi == seq else jnp.concatenate([first, probs[:, BLK:]], axis=1)
            grad_probs = nt(v_aug[head, lo:hi, :], g_aug[head, lo:, :])
            grad_scores = (probs * grad_probs).astype(jnp.bfloat16)
            dv_acc[head, lo:hi, :] = nn(probs.astype(jnp.bfloat16), g_aug[head, lo:, :])[:, :HD].astype(
                jnp.bfloat16
            )
            dk_acc[head, lo:hi, :] = nn(grad_scores, q_aug[head, lo:, :])[:, :HD].astype(jnp.bfloat16)
            part = nn(k_t[head, :, lo:hi], grad_scores)
            if block:
                dq_t[head, :, lo:] += part
            else:
                dq_t[head, :, :] = part
        return carry

    lax.fori_loop(0, heads, per_head, 0)
    fresh = info_ref[0] < 2
    for rel in range(4):
        span = pl.ds(place(info_ref, rel, rows), rows)
        part = dq_t[:, :, span].reshape(cols, rows)
        dqkv_ref[rel, :, :cols] = (part.T * (1.0 / math.sqrt(HD))).astype(dqkv_ref.dtype)
        for head in range(heads):
            at = head * HD
            dqkv_ref[rel, :, cols + at : cols + at + HD] = dk_acc[head, span, :]
            value = dv_acc[head, span, :]
            out, first = dv_outs[rel]
            out[:, first + at : first + at + HD] = value
            kept = jnp.where(fresh, value, jnp.zeros_like(value))
            dqkv_ref[rel, :, 2 * cols + at : 2 * cols + at + HD] = kept


def attend_back(info, prepared, grads, outs, lse):
    heads, seq = prepared[0].shape[:2]
    rows, cols = seq // 4, heads * HD
    work = heads * seq * (seq + BLK) // 2
    return call(
        backward_kernel,
        "attend_back",
        [
            low_shape(4, rows, 3 * cols),
            low_shape(rows, cols),
            low_shape(rows, cols),
            low_shape(rows, 2 * cols),
        ],
        [SMEM] + [VMEM] * 12,
        [
            pltpu.VMEM((heads, seq, 2 * HD), jnp.bfloat16),
            pltpu.VMEM((heads, HD, seq), jnp.float32),
            pltpu.VMEM((heads, seq, HD), jnp.bfloat16),
            pltpu.VMEM((heads, seq, HD), jnp.bfloat16),
        ],
        40 * work * HD,
        work,
        (info, *prepared, *grads, *outs, lse),
        20,
    )


def norm_stats(wide):
    centred = wide - jnp.mean(wide, axis=-1, keepdims=True)
    inv_std = lax.rsqrt(jnp.mean(centred * centred, axis=-1, keepdims=True) + EPS)
    return centred * inv_std, inv_std


def valid_rows(info_ref, rows, start, count):
    pos = info_ref[0] * rows + start + lax.broadcasted_iota(jnp.int32, (count, 1), 0)
    return (pos < info_ref[1]).astype(jnp.float32)


def row_sum(v):
    return jnp.sum(v, axis=0, keepdims=True)


def middle_kernel(
    info_ref, tok_ref, h0, h1, h2, h3, w0, w1, w2, w3, gain_ref, resid_ref, input_ref, square_ref
):
    rows = tok_ref.shape[0]
    cols = h0.shape[1]
    square_ref[...] = jnp.zeros_like(square_ref)

    def tile(span):
        attn = nt(h0[span], w0[...]) + nt(h1[span], w1[...])
        attn = attn + nt(h2[span, :cols], w2[...]) + nt(h3[span, cols:], w3[...])
        resid = tok_ref[span].astype(jnp.float32) + attn
        resid_ref[span] = resid
        normed, _ = norm_stats(resid)
        input_ref[span] = (normed * gain_ref[...]).astype(input_ref.dtype)
        square_ref[...] += row_sum(attn * attn * valid_rows(info_ref, rows, span.start, BLK))

    loop(rows, tile)


def middle(info, tokens, heads, weights, gain):
    rows, dim = tokens.shape
    return call(
        middle_kernel,
        "middle",
        [wide_shape(rows, dim), low_shape(rows, dim), wide_shape(1, dim)],
        [SMEM] + [VMEM] * 10,
        [],
        2 * rows * dim * dim,
        rows,
        (info, tokens, *heads, *weights, gain),
    )


GELU_C = math.sqrt(2.0 / math.pi)
CUBE = 0.044715


def mlp_tiles(xs, cots, w_ref, hid_ref, dup_ref, backs, outs):
    rows = xs[0].shape[0]
    up_cols = w_ref.shape[1] // 2
    up_w, down_t = w_ref.at[:, :up_cols], w_ref.at[:, up_cols:]
    for block in range(len(xs)):

        def tile(span, block=block):
            up = nn(xs[block][span], up_w[...])
            up2 = up * up
            th = jnp.tanh(GELU_C * up * (1.0 + CUBE * up2))
            half = 0.5 * (1.0 + th)
            hidden = (up * half).astype(jnp.bfloat16)
            hid_ref[block, span] = hidden
            slope = half + 0.5 * up * (1.0 - th * th) * (GELU_C * (1.0 + 3.0 * CUBE * up2))
            dup = (nn(cots[block][span], down_t[...]) * slope).astype(jnp.bfloat16)
            dup_ref[block, span] = dup
            backs[block][span] = nt(dup, up_w[...]).astype(jnp.bfloat16)
            if outs:
                outs[block][span] = nt(hidden, down_t[...]).astype(jnp.bfloat16)

        loop(rows, tile)


def mlp_near_kernel(x0, x1, c0, c1, w_ref, hid_ref, dup_ref, b0, b1, o0, o1):
    mlp_tiles((x0, x1), (c0, c1), w_ref, hid_ref, dup_ref, (b0, b1), (o0, o1))


def mlp_far_kernel(x_ref, c_ref, w_ref, hid_ref, dup_ref, back_ref):
    mlp_tiles((x_ref,), (c_ref,), w_ref, hid_ref, dup_ref, (back_ref,), ())


def mlp_near(xs, cots, weights):
    rows, dim = xs[0].shape
    wide = weights.shape[1]
    return call(
        mlp_near_kernel,
        "mlp_near",
        [low_shape(2, rows, wide // 2)] * 2 + [low_shape(rows, dim)] * 4,
        [VMEM] * 5,
        [],
        8 * rows * dim * wide,
        rows * wide,
        (*xs, *cots, weights),
    )


def mlp_far(x, cot, weights):
    rows, dim = x.shape
    wide = weights.shape[1]
    return call(
        mlp_far_kernel,
        "mlp_far",
        [low_shape(1, rows, wide // 2)] * 2 + [low_shape(rows, dim)],
        [VMEM] * 3,
        [],
        3 * rows * dim * wide,
        rows * wide // 2,
        (x, cot, weights),
    )


def mlp_grads_kernel(
    up_cols, x0, x1, x2, x3, c0, c1, c2, c3, h_a, h_x, h_d, d_a, d_x, d_d, w_ref, g_ref, o0, o1
):
    down_t = w_ref.at[:, up_cols : 2 * up_cols]
    step = 2 * BLK
    for far, out in ((h_x, o0), (h_d, o1)):
        out[...] = nt(far[0], down_t[...]).astype(out.dtype)
    for start in range(0, up_cols, BLK):
        span = slice(start, start + BLK)
        acc = tn(x0[...], d_a[0, :, span]) + tn(x1[...], d_a[1, :, span])
        acc = acc + tn(x2[...], d_x[0, :, span]) + tn(x3[...], d_d[0, :, span])
        g_ref[:, span] = acc.astype(g_ref.dtype)
        acc = tn(c0[...], h_a[0, :, span]) + tn(c1[...], h_a[1, :, span])
        acc = acc + tn(c2[...], h_x[0, :, span]) + tn(c3[...], h_d[0, :, span])
        g_ref[:, up_cols + start : up_cols + start + BLK] = acc.astype(g_ref.dtype)


def mlp_grads(xs, cots, hids, dups, weights, up_cols):
    rows, dim = xs[0].shape
    return call(
        functools.partial(mlp_grads_kernel, up_cols),
        "mlp_grads",
        [low_shape(dim, 2 * up_cols), low_shape(rows, dim), low_shape(rows, dim)],
        [VMEM] * 15,
        [],
        20 * rows * dim * up_cols,
        0,
        (*xs, *cots, *hids, *dups, weights),
    )


def turn_kernel(
    resid_ref, cot_ref, b0, b1, b2, gain_ref, w0, w1, w2, w3,
    grad_ref, low_ref, d_own, d_core, d_pair, gain_out,
):
    rows = resid_ref.shape[0]
    cols = d_own.shape[1]
    gain_out[...] = jnp.zeros_like(gain_out)

    def tile(span):
        normed, inv_std = norm_stats(resid_ref[span])
        back = b0[span].astype(jnp.float32) + b1[span].astype(jnp.float32)
        back = back + b2[span].astype(jnp.float32)
        gain_out[...] += row_sum(back * normed)
        scaled = back * gain_ref[...]
        inner = scaled - jnp.mean(scaled, axis=-1, keepdims=True)
        inner = inner - normed * jnp.mean(scaled * normed, axis=-1, keepdims=True)
        grad = cot_ref[span].astype(jnp.float32) + inner * inv_std
        grad_ref[span] = grad
        low = grad.astype(jnp.bfloat16)
        low_ref[span] = low
        d_own[span] = nn(low, w0[...]).astype(jnp.bfloat16)
        d_core[span] = nn(low, w1[...]).astype(jnp.bfloat16)
        d_pair[span, :cols] = nn(low, w2[...]).astype(jnp.bfloat16)
        d_pair[span, cols:] = nn(low, w3[...]).astype(jnp.bfloat16)

    loop(rows, tile)


def turn(resid, cot, backs, gain, weights):
    rows, dim = cot.shape
    cols = weights[0].shape[1]
    return call(
        turn_kernel,
        "turn",
        [
            wide_shape(rows, dim),
            low_shape(rows, dim),
            low_shape(rows, cols),
            low_shape(rows, cols),
            low_shape(rows, 2 * cols),
            wide_shape(1, dim),
        ],
        [VMEM] * 10,
        [],
        2 * rows * dim * dim,
        rows,
        (resid, cot, *backs, gain, *weights),
    )


def out_grads_kernel(low_ref, h0, h1, h2, h3, o_near, o_far):
    cols = h0.shape[1]
    low = low_ref[...]
    o_near[:, :cols] = tn(low, h0[...])
    o_far[:, :cols] = tn(low, h1[...]).astype(jnp.bfloat16)
    o_near[:, cols:] = tn(low, h2[:, :cols])
    o_far[:, cols:] = tn(low, h3[:, cols:]).astype(jnp.bfloat16)


def out_grads(low, heads):
    rows, dim = low.shape
    cols = heads[0].shape[1]
    return call(
        out_grads_kernel,
        "out_grads",
        [wide_shape(dim, 2 * cols), low_shape(dim, 2 * cols)],
        [VMEM] * 5,
        [],
        2 * rows * dim * dim,
        0,
        (low, *heads),
    )


def slot_sum_kernel(near_ref, far_ref, out_ref):
    cols = out_ref.shape[1]
    out_ref[...] = (near_ref[:, cols:] + far_ref[:, cols:].astype(jnp.float32)).astype(out_ref.dtype)


def slot_sum(near, far):
    dim, wide = near.shape
    return call(
        slot_sum_kernel, "slot_sum", [low_shape(dim, wide // 2)], [VMEM] * 2, [], dim * wide, 0, (near, far)
    )[0]


def input_grads_kernel(first, dqkv_ref, w_ref, o0, o1):
    rows, wide = dqkv_ref.shape[1:]
    for rel, out in ((first, o0), (first + 1, o1)):

        def tile(span, rel=rel, out=out):
            out[span] = nt(dqkv_ref[rel, span], w_ref[:, :wide]).astype(out.dtype)

        loop(rows, tile)


def input_grads(dqkv, weights, first):
    rows, cols = dqkv.shape[1:]
    dim = weights.shape[0]
    return call(
        functools.partial(input_grads_kernel, first),
        "input_grads",
        [low_shape(rows, dim)] * 2,
        [VMEM] * 2,
        [],
        4 * rows * dim * cols,
        0,
        (dqkv, weights),
    )


def qkv_grads_kernel(
    info_ref, x0, x1, x2, x3, dqkv_ref, near_ref, far_ref, far_x, small_ref, w_ref, gain_ref, *refs
):
    *outs, all_ref = refs
    wide = dqkv_ref.shape[2]
    cols = wide // 3
    acc = tn(x0[...], dqkv_ref[0]) + tn(x1[...], dqkv_ref[1])
    acc = acc + tn(x2[...], dqkv_ref[2]) + tn(x3[...], dqkv_ref[3])
    all_ref[:, :wide] = acc.astype(all_ref.dtype)
    total = near_ref[:, :cols] + far_ref[:, :cols].astype(jnp.float32)
    total = total + far_x[...].astype(jnp.float32)
    all_ref[:, wide:] = total.astype(all_ref.dtype)
    products = acc * w_ref[:, :wide].astype(jnp.float32)
    low = products.astype(jnp.bfloat16)
    ones = jnp.ones((8, wide), jnp.bfloat16)
    sums = nt(ones, low) + nt(ones, (products - low.astype(jnp.float32)).astype(jnp.bfloat16))
    sums = sums[:1] / gain_ref[...]
    low = sums.astype(jnp.bfloat16)
    row = lax.broadcasted_iota(jnp.int32, small_ref.shape, 0)
    small = jnp.where(row == 0, low, small_ref[...])
    small = jnp.where(row == 8, (sums - low.astype(jnp.float32)).astype(jnp.bfloat16), small)
    if len(outs) == 1:
        outs[0][0, : all_ref.shape[0]] = all_ref[...]
        outs[0][0, all_ref.shape[0] :] = small
        return
    half = info_ref[2 + 4 * x0.shape[0] // BLK]
    count, full = outs[0].shape[:2]
    shard = full - small.shape[0]
    for parity, out in ((half, outs[0]), (1 - half, outs[1])):
        for part in range(count):
            start = pl.multiple_of((2 * part + parity) * shard, shard)
            out[part, :shard] = all_ref[pl.ds(start, shard), :]
            out[part, shard:] = small


def qkv_grads(info, xs, dqkv, near, far, far_x, small, weights, gain, count):
    rows, dim = xs[0].shape
    wide = dqkv.shape[2]
    full = wide + wide // 3
    extra = small.shape[0]
    if count == 1:
        outs = [low_shape(1, dim + extra, full)]
    else:
        outs = [low_shape(count // 2, dim // count + extra, full)] * 2
    return call(
        qkv_grads_kernel,
        "qkv_grads",
        outs,
        [SMEM] + [VMEM] * 11,
        [pltpu.VMEM((dim, full), jnp.bfloat16)],
        8 * rows * dim * wide,
        0,
        (info, *xs, dqkv, near, far, far_x, small, weights, gain),
    )


def fold_kernel(shard, info_ref, a_ref, b_ref, *outs):
    line = info_ref[info_ref.shape[0] - 1]
    for step, out in enumerate(outs):
        part = line ^ step
        total = a_ref[part, :shard].astype(jnp.float32) + b_ref[part, :shard].astype(jnp.float32)
        out[:shard] = total.astype(out.dtype)
        total = a_ref[part, shard:].astype(jnp.float32) + b_ref[part, shard:].astype(jnp.float32)
        half = total.shape[0] // 2
        wide = total[:half] + total[half:]
        low = wide.astype(jnp.bfloat16)
        rest = (wide - low.astype(jnp.float32)).astype(jnp.bfloat16)
        out[shard:] = jnp.concatenate([low, rest], axis=0)


def fold(info, a, b, shard):
    count, full, wide = a.shape
    return call(
        functools.partial(fold_kernel, shard), "fold", [low_shape(full, wide)] * count,
        [SMEM] + [VMEM] * 2, [], a.size, 0, (info, a, b),
    )


def finish_kernel(tok_ref, grad_ref, b0, b1, b2, gain_ref, out_ref):

    def tile(span):
        normed, inv_std = norm_stats(tok_ref[span].astype(jnp.float32))
        back = b0[span].astype(jnp.float32) + b1[span].astype(jnp.float32)
        back = back + b2[span].astype(jnp.float32)
        scaled = back * gain_ref[...]
        inner = scaled - jnp.mean(scaled, axis=-1, keepdims=True)
        inner = inner - normed * jnp.mean(scaled * normed, axis=-1, keepdims=True)
        out_ref[span] = grad_ref[span] + inner * inv_std

    loop(tok_ref.shape[0], tile)


def finish(tokens, grad, backs, gain):
    rows, dim = tokens.shape
    return call(
        finish_kernel,
        "finish",
        [wide_shape(rows, dim)],
        [VMEM] * 6,
        [],
        rows * dim * 20,
        rows,
        (tokens, grad, *backs, gain),
    )[0]


def norm_kernel(t0, t1, gain_ref, o0, o1):
    for src, out in ((t0, o0), (t1, o1)):

        def tile(span, src=src, out=out):
            normed, _ = norm_stats(src[span].astype(jnp.float32))
            out[span] = (normed * gain_ref[...]).astype(out.dtype)

        loop(t0.shape[0], tile)


def norms(blocks, gain):
    rows, dim = blocks[0].shape
    return call(
        norm_kernel,
        "norms",
        [low_shape(rows, dim)] * 2,
        [VMEM] * 3,
        [],
        rows * dim * 20,
        rows,
        (*blocks, gain),
    )


def share_kernel(shard, parts_ref, *outs):
    cols = outs[0].shape[1]
    for at, out in enumerate(outs):
        if out.shape[0] != shard:
            break
        span = slice(at * cols, (at + 1) * cols)
        total = parts_ref[0, :shard, span].astype(jnp.float32)
        for part in range(1, parts_ref.shape[0]):
            total = total + parts_ref[part, :shard, span].astype(jnp.float32)
        out[...] = total
    if parts_ref.shape[1] > shard:
        total = parts_ref[0, shard:].astype(jnp.float32)
        for part in range(1, parts_ref.shape[0]):
            total = total + parts_ref[part, shard:].astype(jnp.float32)
        half = total.shape[0] // 2
        outs[-1][...] = total[:half] + total[half:]


def shares(parts, shard, cols, name):
    count, full, wide = parts.shape
    outs = [wide_shape(shard, cols)] * (wide // cols)
    if full > shard:
        outs.append(wide_shape((full - shard) // 2, wide))
    return call(
        functools.partial(share_kernel, shard),
        name,
        outs,
        [VMEM],
        [],
        count * full * wide,
        0,
        (parts,),
    )


def tail_kernel(count, *refs):
    parts, (q_out, k_out, o_out, mix_ref) = refs[:count], refs[count:]
    shard, cols = q_out.shape
    wide = mix_ref.shape[1]

    def total(rows, span):
        acc = parts[0][rows, span].astype(jnp.float32)
        for part in parts[1:]:
            acc = acc + part[rows, span].astype(jnp.float32)
        return acc

    first = slice(0, shard)
    q_out[...] = total(first, slice(0, cols))
    k_out[...] = total(first, slice(cols, 2 * cols))
    o_out[...] = total(first, slice(3 * cols, 4 * cols)).T
    small = total(slice(shard, shard + 16), slice(0, wide))
    mix_ref[:8] = small[:8] + small[8:]
    value = total(first, slice(2 * cols, 3 * cols))
    height = shard // 4
    for at in range(4):
        mix_ref[8:, at * cols : (at + 1) * cols] = value[at * height : (at + 1) * height]


def tail_shares(parts, shard, cols):
    full, wide = parts[0].shape
    return call(
        functools.partial(tail_kernel, len(parts)),
        "tail_shares",
        [
            wide_shape(shard, cols),
            wide_shape(shard, cols),
            wide_shape(cols, shard),
            wide_shape(8 + shard // 4, wide),
        ],
        [VMEM] * len(parts),
        [],
        len(parts) * full * wide,
        0,
        tuple(parts),
    )


def meet_kernel(info_ref, own_ref, peer_ref, out_ref):
    out_ref[:8] = own_ref[:8] + peer_ref[:8]
    out_ref[8:] = jnp.where(info_ref[0] < 2, own_ref[8:], peer_ref[8:])


def meet(info, own, peer):
    return call(
        meet_kernel, "meet", [wide_shape(*own.shape)], [SMEM] + [VMEM] * 2, [], own.size, 0, (info, own, peer)
    )[0]


def last_kernel(info_ref, own_ref, peer_ref, value_ref, gain_one, gain_two, rms_ref):
    dim = own_ref.shape[1]
    cols = dim // 4
    total = own_ref[:8] + peer_ref[:8]
    gain_one[...] = total[0:1]
    gain_two[...] = total[1:2]
    sums = jnp.sum(total, axis=1, keepdims=True)
    roots = jnp.sqrt(sums / (sums[5:6] * dim))
    lane = lax.broadcasted_iota(jnp.int32, rms_ref.shape, 1)
    rms_ref[...] = jnp.where(lane == 0, roots[2:3], jnp.where(lane == 1, roots[3:4], roots[4:5]))
    even = info_ref[0] % 2 == 0
    own, peer = own_ref[8:], peer_ref[8:]
    lower, upper = jnp.where(even, own, peer), jnp.where(even, peer, own)
    height = own.shape[0]
    for at in range(4):
        rows, span = slice(at * height, (at + 1) * height), slice(at * cols, (at + 1) * cols)
        value_ref[rows, :cols] = lower[:, span]
        value_ref[rows, cols:] = upper[:, span]


def last(info, own, peer):
    dim = own.shape[1]
    return call(
        last_kernel,
        "last",
        [wide_shape(4 * (own.shape[0] - 8), dim // 2), wide_shape(1, dim), wide_shape(1, dim), wide_shape(1, LANES)],
        [SMEM] + [VMEM] * 2,
        [],
        own.size,
        0,
        (info, own, peer),
    )


def output_kernel(info_ref, resid_ref, b0, b1, b2, attn_sq, gain_two, out_ref, small_ref, *sums):
    rows, dim = resid_ref.shape
    final_sum, mlp_sum = sums
    final_sum[...] = jnp.zeros_like(final_sum)
    mlp_sum[...] = jnp.zeros_like(mlp_sum)

    def tile(span):
        valid = valid_rows(info_ref, rows, span.start, BLK)
        mlp_out = b0[span].astype(jnp.float32) + b1[span].astype(jnp.float32)
        mlp_out = mlp_out + b2[span].astype(jnp.float32)
        final = resid_ref[span] + mlp_out
        out_ref[span] = final.astype(out_ref.dtype)
        final_sum[...] += row_sum(final * final * valid)
        mlp_sum[...] += row_sum(mlp_out * mlp_out * valid)

    loop(rows, tile)
    count = jnp.clip(info_ref[1] - info_ref[0] * rows, 0, rows).astype(jnp.float32)
    lane = lax.broadcasted_iota(jnp.int32, (1, dim), 1)
    counts = jnp.where(lane == 0, count, 0.0)
    row = lax.broadcasted_iota(jnp.int32, (8, dim), 0)
    wide = jnp.zeros((8, dim), jnp.float32)
    values = (jnp.zeros_like(gain_two), gain_two[...], final_sum[...], attn_sq[...], mlp_sum[...], counts)
    for at, value in enumerate(values):
        wide = jnp.where(row == at, value, wide)
    low = wide.astype(jnp.bfloat16)
    small_ref[...] = jnp.concatenate([low, (wide - low.astype(jnp.float32)).astype(jnp.bfloat16)], axis=0)


def output(info, resid, parts, sums):
    rows, dim = resid.shape
    return call(
        output_kernel,
        "output",
        [low_shape(rows, dim), low_shape(16, dim)],
        [SMEM] + [VMEM] * 6,
        [pltpu.VMEM((1, dim), jnp.float32)] * 2,
        rows * dim * 10,
        0,
        (info, resid, *parts, *sums),
    )


def pack_early_kernel(info_ref, wq, wk, wv, wo, out_ref):
    cols = wq.shape[1]
    even = info_ref[0] % 2 == 0
    fresh = jnp.where(even, wv[:, :cols], wv[:, cols : 2 * cols])
    turned = wo[...].T
    for part in range(out_ref.shape[0]):
        for at, value in enumerate((wq[...], wk[...], fresh, turned)):
            out_ref[part, :, at * cols : (at + 1) * cols] = value


def pack_early(info, copies, wq, wk, wv, wo):
    shard, cols = wq.shape
    return call(
        pack_early_kernel, "pack_early", [low_shape(copies, shard, 4 * cols)],
        [SMEM] + [VMEM] * 4, [], shard * cols, 0, (info, wq, wk, wv, wo), 60,
    )[0]


X_SWAP = [(0, 2), (1, 3), (2, 0), (3, 1)]
CORE_SWAP = [(0, 1), (1, 0), (2, 3), (3, 2)]


def swap_x(v):
    return lax.ppermute(v, "tensor", X_SWAP)


def swap_core(v):
    return lax.ppermute(v, "tensor", CORE_SWAP)


def tied(value, *others):
    return lax.optimization_barrier((value, *others))[0]


def plus(a, b):
    return (a.astype(jnp.float32) + b.astype(jnp.float32)).astype(jnp.bfloat16)


def body(
    tokens,
    first_values,
    pieces,
    lengths,
    w_query,
    w_key,
    w_value,
    w_out,
    w_up,
    w_down,
    gain_attn,
    gain_mlp,
    cotangent,
):
    dp_size = lax.axis_size("dp")
    rank = lax.axis_index("tensor")
    core = rank % 2
    rows, dim = tokens.shape
    shard, cols = w_query.shape
    up_cols = w_up.shape[1]
    parity = lax.axis_index("dp") % 2
    info = jnp.concatenate(
        [
            rank[None].astype(jnp.int32),
            lengths,
            pieces[::BLK],
            parity[None].astype(jnp.int32),
            (lax.axis_index("dp") // 2)[None].astype(jnp.int32),
        ]
    )
    gain_one, gain_two = gain_attn[None], gain_mlp[None]
    pairs = [(i, i ^ 1) for i in range(dp_size)]
    lines = [list(range(first, dp_size, 2)) for first in range(2)]

    def gather_line(v):
        return lax.all_to_all(v, "dp", 0, 0, axis_index_groups=lines)

    def swap_pair(v):
        return lax.ppermute(v, "dp", pairs)

    def in_order(mine, other):
        lower = jnp.where(parity == 0, mine, other)
        upper = jnp.where(parity == 0, other, mine)
        return jnp.stack([lower, upper], axis=1).reshape(dim, -1)

    def pieces_of(mine, other):
        if shard % 16 == 0:
            return (mine, other)
        return (in_order(mine, other)[None],)

    early = pack_early(rank[None].astype(jnp.int32), dp_size // 2, w_query, w_key, w_value, w_out)
    early_mine = gather_line(early)
    tok_x = swap_x(tokens)
    tok_core = swap_core(tokens)
    xs_near = norms((tokens, tok_core), gain_one)
    early_other = swap_pair(early_mine)
    tok_diag = swap_core(tok_x)
    late = tied(jnp.concatenate([w_up, w_down.T], axis=1), tok_core)
    late_all = lax.all_gather(late, "dp", axis=0, tiled=True)
    first_x = lax.ppermute(first_values, "tensor", [(0, 2), (1, 3)])
    firsts = (first_values, swap_core(first_values), first_x, swap_core(first_x))
    xs = (*xs_near, *norms((tok_x, tok_diag), gain_one))
    early_all, out_own, *prepared, o_first, lse_first = attend_first(
        info, xs, pieces_of(early_mine, early_other), firsts, cols
    )

    out_x = swap_x(out_own)
    cot_x = swap_x(tied(cotangent, first_x))
    h_own, h_core, h_pair, lse = attend_rest(info, *prepared[:3], o_first, lse_first)
    h_pair, h_core = lax.optimization_barrier((h_pair, h_core, cot_x, out_x))[:2]
    cot_core = swap_core(cotangent)
    cot_diag = swap_core(cot_x)
    outs = (out_own, swap_core(out_own), out_x, swap_core(out_x))

    from_x = swap_x(h_pair)
    heads_mine = (h_own, swap_core(h_core), from_x, swap_core(from_x))
    resid, mlp_in, attn_sq = middle(
        info, tokens, heads_mine, outs, gain_two
    )
    in_x = swap_x(mlp_in)
    in_core = swap_core(mlp_in)
    hid_a, dup_a, back_own, back_core, out_0, out_1 = mlp_near(
        (mlp_in, in_core), (cotangent, cot_core), late_all
    )
    back_1 = swap_core(back_core)
    out_near = swap_core(out_1)
    in_far = tied(in_x, back_own)
    in_diag = swap_core(in_far)
    hid_x, dup_x, back_x = mlp_far(in_far, cot_x, late_all)
    hid_d, dup_d, back_diag = mlp_far(tied(in_diag, back_x), cot_diag, late_all)
    back_far = plus(back_x, swap_core(back_diag))
    back_2 = swap_x(back_far)
    grads_mlp, out_2, out_3 = mlp_grads(
        (mlp_in, in_core, in_x, in_diag),
        (cotangent, cot_core, cot_x, cot_diag),
        (hid_a, hid_x, tied(hid_d, back_far)), (dup_a, dup_x, dup_d), late_all, up_cols,
    )
    mlp_share = lax.psum_scatter(grads_mlp, "dp", scatter_dimension=0, tiled=True)
    out_sum = plus(out_2, swap_core(out_3))

    resid_grad, resid_low, d_own, d_core, d_pair, gain_two_sum = turn(
        resid, cotangent, (back_own, back_1, back_2), gain_two, outs
    )
    d_x = swap_x(d_pair)
    grads_heads = (d_own, swap_core(d_core), d_x, swap_core(d_x))
    near, far = out_grads(tied(resid_low, out_sum), heads_mine)
    far = swap_core(far)
    dqkv, dv_own, dv_core, dv_pair = attend_back(
        info, prepared, grads_heads, (h_own, h_core, h_pair), lse
    )
    out_from_x = swap_x(tied(out_sum, d_x))
    near_x = swap_x(tied(slot_sum(near, far), d_x))
    dqkv, dv_pair = lax.optimization_barrier((dqkv, dv_pair, out_from_x, near_x))[:2]

    first_from_x = lax.ppermute(dv_pair, "tensor", [(2, 0), (3, 1)])
    final, small = output(info, resid, (out_0, out_near, out_from_x), (attn_sq, gain_two_sum))
    b_2, b_3 = input_grads(tied(dqkv, small), early_all, 2)
    joined = shard % 16 == 0 and dp_size <= 8
    tail = qkv_grads(
        info, xs, tied(dqkv, b_3), near, far, near_x, small, early_all, gain_one, dp_size if joined else 1
    )
    if joined:
        tail_pair = swap_pair(tail[1])
    tail_first = tail[0]
    plus_far = plus(b_2, swap_core(b_3))
    b_from_x = swap_x(plus_far)

    b_0, b_1 = input_grads(tied(dqkv, plus_far), early_all, 0)
    b_from_core = swap_core(b_1)
    if joined:
        folded = fold(info, tied(tail_first, plus_far, b_0), tail_pair, shard)
    first_a = jnp.where(rank < 2, first_from_x[:, :cols], dv_own)
    first_b = swap_core(jnp.where(rank < 2, first_from_x[:, cols:], dv_core))
    first_grad = jnp.where(
        core == 0,
        jnp.concatenate([first_a, first_b], axis=1),
        jnp.concatenate([first_b, first_a], axis=1),
    ).astype(jnp.float32)
    token_grad = finish(tokens, resid_grad, (b_0, b_from_core, b_from_x), gain_one)
    grad_up, grad_down_t = shares(mlp_share[None], shard, up_cols, "mlp_shares")
    if joined:
        tail_parts = [folded[0]] + [
            lax.ppermute(folded[step], "dp", [(i, i ^ (2 * step)) for i in range(dp_size)])
            for step in range(1, dp_size // 2)
        ]
        tail_parts[0] = tied(tail_parts[0], token_grad, grad_up, first_grad)
        grad_q, grad_k, grad_out, mix = tail_shares(tail_parts, shard, cols)
        mix = meet(info, mix, swap_x(mix))
        value_share, gain_one_sum, gain_two_total, rms = last(info, mix, swap_core(mix))
        gain_one_sum, gain_two_total = gain_one_sum.reshape(dim), gain_two_total.reshape(dim)
        rms = rms[0, :3]
    else:
        small = tail_first[0, dim:].astype(jnp.float32)
        total = lax.psum(small[:8] + small[8:], ("dp", "tensor"))
        tail_all = lax.all_to_all(tail_first[0, :dim].reshape(dp_size, shard, 4 * cols), "dp", 0, 0)
        total_grads = jnp.sum(tail_all.astype(jnp.float32), axis=0)
        grad_q, grad_k = total_grads[:, :cols], total_grads[:, cols : 2 * cols]
        grad_out = total_grads[:, 3 * cols :].T
        value_own = total_grads[:, 2 * cols : 3 * cols]
        value_here = jnp.where(rank < 2, value_own, swap_x(value_own))
        value_peer = swap_core(value_here)
        value_share = jnp.where(
            core == 0,
            jnp.concatenate([value_here, value_peer], axis=1),
            jnp.concatenate([value_peer, value_here], axis=1),
        )
        sums = jnp.sum(total, axis=1)
        rms = jnp.sqrt(sums[2:5] / (sums[5] * dim))
        gain_one_sum, gain_two_total = total[0], total[1]
    return (
        final,
        token_grad,
        first_grad,
        grad_q,
        grad_k,
        value_share,
        grad_out,
        grad_up,
        grad_down_t.T,
        gain_one_sum,
        gain_two_total,
        rms,
    )


def solution(mesh):
    in_specs = (
        P(("dp", "tensor"), None),
        P(("dp", "tensor"), None),
        P("dp"),
        P("dp"),
        P("dp", "tensor"),
        P("dp", "tensor"),
        P("dp", None),
        P("tensor", "dp"),
        P("dp", "tensor"),
        P("tensor", "dp"),
        P(),
        P(),
        P(("dp", "tensor"), None),
    )
    out_specs = (
        P(("dp", "tensor"), None),
        P(("dp", "tensor"), None),
        P(("dp", "tensor"), None),
        P("dp", "tensor"),
        P("dp", "tensor"),
        P("dp", None),
        P("tensor", "dp"),
        P("dp", "tensor"),
        P("tensor", "dp"),
        P(),
        P(),
        P(),
    )
    return jax.shard_map(body, mesh=mesh, in_specs=in_specs, out_specs=out_specs, check_vma=False)
```

```python
import functools
import math

import jax
import jax.numpy as jnp
from jax import lax
from jax.experimental import pallas as pl
from jax.experimental.pallas import tpu as pltpu
from jax.sharding import PartitionSpec as P

HD = 64
EPS = 1e-05
NEG = -1e30
BLK = 256
LANES = 128

SMEM = pl.BlockSpec(memory_space=pltpu.SMEM)
VMEM = pl.BlockSpec(memory_space=pltpu.VMEM)


def nt(a, b):
    return lax.dot_general(a, b, (((1,), (1,)), ((), ())), preferred_element_type=jnp.float32)


def nn(a, b):
    return jnp.dot(a, b, preferred_element_type=jnp.float32)


def tn(a, b):
    return lax.dot_general(a, b, (((0,), (0,)), ((), ())), preferred_element_type=jnp.float32)


WEIGHTS = {"attend_back": 0.6, "input_grads": 0.01, "output": 0.01, "mlp_shares": 0.01, "tail_shares": 0.01, "finish": 0.01, "fold": 0.01}


def call(kernel, name, outs, specs, scratch, flops, exps, args, vmem=12):
    weight = WEIGHTS.get(name, 3.0)
    moved = sum(math.prod(v.shape) * v.dtype.itemsize for v in list(args) + list(outs))
    return pl.pallas_call(
        kernel,
        name=name,
        out_shape=tuple(outs),
        in_specs=specs,
        out_specs=tuple(VMEM for _ in outs),
        scratch_shapes=scratch,
        compiler_params=pltpu.CompilerParams(vmem_limit_bytes=vmem << 20),
        cost_estimate=pl.CostEstimate(
            flops=int(flops * weight),
            transcendentals=int(exps * weight),
            bytes_accessed=int(moved * weight),
        ),
    )(*args)


def low_shape(*shape):
    return jax.ShapeDtypeStruct(shape, jnp.bfloat16)


def wide_shape(*shape):
    return jax.ShapeDtypeStruct(shape, jnp.float32)


def loop(count, body):
    def step(tile, carry):
        body(pl.ds(pl.multiple_of(tile * BLK, BLK), BLK))
        return carry

    lax.fori_loop(0, count // BLK, step, 0)


def diag_allowed(picture, query_axis):
    query_pos = lax.broadcasted_iota(jnp.int32, (BLK, BLK), query_axis)
    key_pos = lax.broadcasted_iota(jnp.int32, (BLK, BLK), 1 - query_axis)
    return (key_pos <= query_pos) | (picture > 0)


def place(info_ref, rel, rows):
    return pl.multiple_of((info_ref[0] ^ rel) * rows, rows)


def assemble(dst_ref, parts, half):
    if len(parts) == 1:
        dst_ref[...] = parts[0][0]
        return
    mine, other = parts
    count, shard = mine.shape[:2]
    for part in range(count):
        dst_ref[pl.ds(pl.multiple_of((2 * part + half) * shard, shard), shard), :] = mine[part]
        dst_ref[pl.ds(pl.multiple_of((2 * part + 1 - half) * shard, shard), shard), :] = other[part]


def forward_head(head, slot, info_ref, q_aug, k_aug, v_aug, o_rows, lse_ref):
    seq = q_aug.shape[1]
    for block in range(seq // BLK):
        lo, hi = block * BLK, (block + 1) * BLK
        scores = nt(q_aug[head, lo:hi, :], k_aug[head, :hi, :])
        last = jnp.where(diag_allowed(info_ref[2 + block], 0), scores[:, lo:], NEG)
        row_max = jnp.max(last, axis=1, keepdims=True)
        if block:
            row_max = jnp.maximum(row_max, jnp.max(scores[:, :lo], axis=1, keepdims=True))
        acc = nn(jnp.exp(last - row_max).astype(jnp.bfloat16), v_aug[head, lo:hi, :])
        if block:
            front = jnp.exp(scores[:, :lo] - row_max).astype(jnp.bfloat16)
            acc = acc + nn(front, v_aug[head, :lo, :])
        total = acc[:, HD : HD + 1]
        o_rows[slot, lo:hi, :] = (acc[:, :HD] / total).astype(o_rows.dtype)
        lse = row_max + jnp.log(total)
        lse_ref[slot, :, lo:hi] = jnp.broadcast_to(lse, (BLK, LANES)).T[:1]


def first_kernel(info_ref, x0, x1, x2, x3, f0, f1, f2, f3, *refs):
    *parts, w_ref, out_w, q_aug, k_aug, v_aug, k_t, o_rows, lse_ref = refs
    inputs, firsts = (x0, x1, x2, x3), (f0, f1, f2, f3)
    rows = x0.shape[0]
    seq = 4 * rows
    heads = q_aug.shape[0]
    cols = heads * HD
    rank = info_ref[0]
    assemble(w_ref, parts, info_ref[2 + seq // BLK])
    out_w[...] = w_ref[:, 3 * cols :]
    lane = lax.broadcasted_iota(jnp.int32, (seq, HD), 1)
    pos = lax.broadcasted_iota(jnp.int32, (seq, HD), 0)
    bias = jnp.where((lane == 0) & (pos >= info_ref[1]), NEG, 0.0).astype(jnp.bfloat16)
    one = jnp.where(lane == 0, 1.0, 0.0).astype(jnp.bfloat16)
    ones = jnp.where(lane < 3, 1.0, 0.0).astype(jnp.bfloat16)
    for head in range(heads):
        q_aug[head, :, HD:] = one
        k_aug[head, :, HD:] = bias
        v_aug[head, :, HD:] = ones
    for rel in range(4):
        span = pl.ds(place(info_ref, rel, rows), rows)
        part = nn(inputs[rel][...], w_ref[:, : 3 * cols])
        for head in range(heads):
            at = head * HD
            q_aug[head, span, :HD] = part[:, at : at + HD].astype(jnp.bfloat16) * jnp.bfloat16(
                1.0 / math.sqrt(HD)
            )
            keys = part[:, cols + at : cols + at + HD].astype(jnp.bfloat16)
            k_aug[head, span, :HD] = keys
            k_t[head, :, span] = keys.T
            reused = jnp.where(
                rank % 2 == 0, firsts[rel][:, at : at + HD], firsts[rel][:, cols + at : cols + at + HD]
            )
            fresh = part[:, 2 * cols + at : 2 * cols + at + HD].astype(jnp.bfloat16)
            v_aug[head, span, :HD] = jnp.where(rank < 2, fresh, reused)
    forward_head(0, 0, info_ref, q_aug, k_aug, v_aug, o_rows, lse_ref)


def attend_first(info, inputs, parts, firsts, cols):
    rows, dim = inputs[0].shape
    wide = parts[0].shape[2]
    heads = cols // HD
    seq = 4 * rows
    work = seq * (seq + BLK) // 2
    return call(
        first_kernel,
        "attend_first",
        [
            low_shape(dim, wide),
            low_shape(dim, cols),
            low_shape(heads, seq, 2 * HD),
            low_shape(heads, seq, 2 * HD),
            low_shape(heads, seq, 2 * HD),
            low_shape(heads, HD, seq),
            low_shape(1, seq, HD),
            wide_shape(1, 1, seq),
        ],
        [SMEM] + [VMEM] * (8 + len(parts)),
        [],
        16 * work * HD + 2 * seq * dim * wide,
        work,
        (info, *inputs, *firsts, *parts),
    )


def rest_kernel(
    info_ref, q_aug, k_aug, v_aug, o_first, lse_first, own_ref, core_ref, pair_ref, lse_ref, o_rows, lse_part
):
    rows, cols = own_ref.shape
    heads = cols // HD

    def per_head(head, carry):
        forward_head(head + 1, head, info_ref, q_aug, k_aug, v_aug, o_rows, lse_part)
        return carry

    lax.fori_loop(0, heads - 1, per_head, 0)
    lse_ref[0] = lse_first[0]
    for head in range(1, heads):
        lse_ref[head] = lse_part[head - 1]
    for rel, (out, first) in enumerate(((own_ref, 0), (core_ref, 0), (pair_ref, 0), (pair_ref, cols))):
        span = pl.ds(place(info_ref, rel, rows), rows)
        out[:, first : first + HD] = o_first[0, span, :]
        for head in range(1, heads):
            at = first + head * HD
            out[:, at : at + HD] = o_rows[head - 1, span, :]


def attend_rest(info, q_aug, k_aug, v_aug, o_first, lse_first):
    heads, seq = q_aug.shape[:2]
    rows, cols = seq // 4, heads * HD
    work = (heads - 1) * seq * (seq + BLK) // 2
    return call(
        rest_kernel,
        "attend_rest",
        [
            low_shape(rows, cols),
            low_shape(rows, cols),
            low_shape(rows, 2 * cols),
            wide_shape(heads, 1, seq),
        ],
        [SMEM] + [VMEM] * 5,
        [pltpu.VMEM((heads - 1, seq, HD), jnp.bfloat16), pltpu.VMEM((heads - 1, 1, seq), jnp.float32)],
        16 * work * HD,
        work,
        (info, q_aug, k_aug, v_aug, o_first, lse_first),
    )


def backward_kernel(
    info_ref, q_aug, k_aug, v_aug, k_t, g0, g1, g2, g3, own_ref, core_ref, pair_ref, lse_ref,
    dqkv_ref, dv_own, dv_core, dv_pair, g_aug, dq_t, dk_acc, dv_acc,
):
    rows, cols = own_ref.shape
    grads = ((g0, 0), (g1, 0), (g2, 0), (g3, cols))
    outs = ((own_ref, 0), (core_ref, 0), (pair_ref, 0), (pair_ref, cols))
    dv_outs = ((dv_own, 0), (dv_core, 0), (dv_pair, 0), (dv_pair, cols))
    heads, seq = q_aug.shape[:2]
    lane = lax.broadcasted_iota(jnp.int32, (rows, HD), 1)
    for head in range(heads):
        at = head * HD
        for rel in range(4):
            span = pl.ds(place(info_ref, rel, rows), rows)
            src, first = grads[rel]
            grad = src[:, first + at : first + at + HD]
            g_aug[head, span, :HD] = grad
            src, first = outs[rel]
            products = grad.astype(jnp.float32) * src[:, first + at : first + at + HD].astype(jnp.float32)
            left = -jnp.sum(products, axis=1, keepdims=True)
            part = jnp.zeros((rows, HD), jnp.bfloat16)
            for piece in range(3):
                low = left.astype(jnp.bfloat16)
                part = jnp.where(lane == piece, low, part)
                left = left - low.astype(jnp.float32)
            g_aug[head, span, HD:] = part

    def per_head(head, carry):
        for block in range(seq // BLK):
            lo, hi = block * BLK, (block + 1) * BLK
            probs = jnp.exp(nt(k_aug[head, lo:hi, :], q_aug[head, lo:, :]) - lse_ref[head, :, lo:])
            first = jnp.where(diag_allowed(info_ref[2 + block], 1), probs[:, :BLK], 0.0)
            probs = first if hi == seq else jnp.concatenate([first, probs[:, BLK:]], axis=1)
            grad_probs = nt(v_aug[head, lo:hi, :], g_aug[head, lo:, :])
            grad_scores = (probs * grad_probs).astype(jnp.bfloat16)
            dv_acc[head, lo:hi, :] = nn(probs.astype(jnp.bfloat16), g_aug[head, lo:, :])[:, :HD].astype(
                jnp.bfloat16
            )
            dk_acc[head, lo:hi, :] = nn(grad_scores, q_aug[head, lo:, :])[:, :HD].astype(jnp.bfloat16)
            part = nn(k_t[head, :, lo:hi], grad_scores)
            if block:
                dq_t[head, :, lo:] += part
            else:
                dq_t[head, :, :] = part
        return carry

    lax.fori_loop(0, heads, per_head, 0)
    fresh = info_ref[0] < 2
    for rel in range(4):
        span = pl.ds(place(info_ref, rel, rows), rows)
        part = dq_t[:, :, span].reshape(cols, rows)
        dqkv_ref[rel, :, :cols] = (part.T * (1.0 / math.sqrt(HD))).astype(dqkv_ref.dtype)
        for head in range(heads):
            at = head * HD
            dqkv_ref[rel, :, cols + at : cols + at + HD] = dk_acc[head, span, :]
            value = dv_acc[head, span, :]
            out, first = dv_outs[rel]
            out[:, first + at : first + at + HD] = value
            kept = jnp.where(fresh, value, jnp.zeros_like(value))
            dqkv_ref[rel, :, 2 * cols + at : 2 * cols + at + HD] = kept


def attend_back(info, prepared, grads, outs, lse):
    heads, seq = prepared[0].shape[:2]
    rows, cols = seq // 4, heads * HD
    work = heads * seq * (seq + BLK) // 2
    return call(
        backward_kernel,
        "attend_back",
        [
            low_shape(4, rows, 3 * cols),
            low_shape(rows, cols),
            low_shape(rows, cols),
            low_shape(rows, 2 * cols),
        ],
        [SMEM] + [VMEM] * 12,
        [
            pltpu.VMEM((heads, seq, 2 * HD), jnp.bfloat16),
            pltpu.VMEM((heads, HD, seq), jnp.float32),
            pltpu.VMEM((heads, seq, HD), jnp.bfloat16),
            pltpu.VMEM((heads, seq, HD), jnp.bfloat16),
        ],
        40 * work * HD,
        work,
        (info, *prepared, *grads, *outs, lse),
        20,
    )


def norm_stats(wide):
    centred = wide - jnp.mean(wide, axis=-1, keepdims=True)
    inv_std = lax.rsqrt(jnp.mean(centred * centred, axis=-1, keepdims=True) + EPS)
    return centred * inv_std, inv_std


def valid_rows(info_ref, rows, start, count):
    pos = info_ref[0] * rows + start + lax.broadcasted_iota(jnp.int32, (count, 1), 0)
    return (pos < info_ref[1]).astype(jnp.float32)


def row_sum(v):
    return jnp.sum(v, axis=0, keepdims=True)


def middle_kernel(
    info_ref, tok_ref, h0, h1, h2, h3, w0, w1, w2, w3, gain_ref, resid_ref, input_ref, square_ref
):
    rows = tok_ref.shape[0]
    cols = h0.shape[1]
    square_ref[...] = jnp.zeros_like(square_ref)

    def tile(span):
        attn = nt(h0[span], w0[...]) + nt(h1[span], w1[...])
        attn = attn + nt(h2[span, :cols], w2[...]) + nt(h3[span, cols:], w3[...])
        resid = tok_ref[span].astype(jnp.float32) + attn
        resid_ref[span] = resid
        normed, _ = norm_stats(resid)
        input_ref[span] = (normed * gain_ref[...]).astype(input_ref.dtype)
        square_ref[...] += row_sum(attn * attn * valid_rows(info_ref, rows, span.start, BLK))

    loop(rows, tile)


def middle(info, tokens, heads, weights, gain):
    rows, dim = tokens.shape
    return call(
        middle_kernel,
        "middle",
        [wide_shape(rows, dim), low_shape(rows, dim), wide_shape(1, dim)],
        [SMEM] + [VMEM] * 10,
        [],
        2 * rows * dim * dim,
        rows,
        (info, tokens, *heads, *weights, gain),
    )


GELU_C = math.sqrt(2.0 / math.pi)
CUBE = 0.044715


def mlp_tiles(xs, cots, w_ref, hid_ref, dup_ref, backs, outs):
    rows = xs[0].shape[0]
    up_cols = w_ref.shape[1] // 2
    up_w, down_t = w_ref.at[:, :up_cols], w_ref.at[:, up_cols:]
    for block in range(len(xs)):

        def tile(span, block=block):
            up = nn(xs[block][span], up_w[...])
            up2 = up * up
            th = jnp.tanh(GELU_C * up * (1.0 + CUBE * up2))
            half = 0.5 * (1.0 + th)
            hidden = (up * half).astype(jnp.bfloat16)
            hid_ref[block, span] = hidden
            slope = half + 0.5 * up * (1.0 - th * th) * (GELU_C * (1.0 + 3.0 * CUBE * up2))
            dup = (nn(cots[block][span], down_t[...]) * slope).astype(jnp.bfloat16)
            dup_ref[block, span] = dup
            backs[block][span] = nt(dup, up_w[...]).astype(jnp.bfloat16)
            if outs:
                outs[block][span] = nt(hidden, down_t[...]).astype(jnp.bfloat16)

        loop(rows, tile)


def mlp_near_kernel(x0, x1, c0, c1, w_ref, hid_ref, dup_ref, b0, b1, o0, o1):
    mlp_tiles((x0, x1), (c0, c1), w_ref, hid_ref, dup_ref, (b0, b1), (o0, o1))


def mlp_far_kernel(x_ref, c_ref, w_ref, hid_ref, dup_ref, back_ref):
    mlp_tiles((x_ref,), (c_ref,), w_ref, hid_ref, dup_ref, (back_ref,), ())


def mlp_near(xs, cots, weights):
    rows, dim = xs[0].shape
    wide = weights.shape[1]
    return call(
        mlp_near_kernel,
        "mlp_near",
        [low_shape(2, rows, wide // 2)] * 2 + [low_shape(rows, dim)] * 4,
        [VMEM] * 5,
        [],
        8 * rows * dim * wide,
        rows * wide,
        (*xs, *cots, weights),
    )


def mlp_far(x, cot, weights):
    rows, dim = x.shape
    wide = weights.shape[1]
    return call(
        mlp_far_kernel,
        "mlp_far",
        [low_shape(1, rows, wide // 2)] * 2 + [low_shape(rows, dim)],
        [VMEM] * 3,
        [],
        3 * rows * dim * wide,
        rows * wide // 2,
        (x, cot, weights),
    )


def mlp_grads_kernel(
    up_cols, x0, x1, x2, x3, c0, c1, c2, c3, h_a, h_x, h_d, d_a, d_x, d_d, w_ref, g_ref, o0, o1
):
    down_t = w_ref.at[:, up_cols : 2 * up_cols]
    step = 2 * BLK
    for far, out in ((h_x, o0), (h_d, o1)):
        out[...] = nt(far[0], down_t[...]).astype(out.dtype)
    for start in range(0, up_cols, BLK):
        span = slice(start, start + BLK)
        acc = tn(x0[...], d_a[0, :, span]) + tn(x1[...], d_a[1, :, span])
        acc = acc + tn(x2[...], d_x[0, :, span]) + tn(x3[...], d_d[0, :, span])
        g_ref[:, span] = acc.astype(g_ref.dtype)
        acc = tn(c0[...], h_a[0, :, span]) + tn(c1[...], h_a[1, :, span])
        acc = acc + tn(c2[...], h_x[0, :, span]) + tn(c3[...], h_d[0, :, span])
        g_ref[:, up_cols + start : up_cols + start + BLK] = acc.astype(g_ref.dtype)


def mlp_grads(xs, cots, hids, dups, weights, up_cols):
    rows, dim = xs[0].shape
    return call(
        functools.partial(mlp_grads_kernel, up_cols),
        "mlp_grads",
        [low_shape(dim, 2 * up_cols), low_shape(rows, dim), low_shape(rows, dim)],
        [VMEM] * 15,
        [],
        20 * rows * dim * up_cols,
        0,
        (*xs, *cots, *hids, *dups, weights),
    )


def turn_kernel(
    resid_ref, cot_ref, b0, b1, b2, gain_ref, w0, w1, w2, w3,
    grad_ref, low_ref, d_own, d_core, d_pair, gain_out,
):
    rows = resid_ref.shape[0]
    cols = d_own.shape[1]
    gain_out[...] = jnp.zeros_like(gain_out)

    def tile(span):
        normed, inv_std = norm_stats(resid_ref[span])
        back = b0[span].astype(jnp.float32) + b1[span].astype(jnp.float32)
        back = back + b2[span].astype(jnp.float32)
        gain_out[...] += row_sum(back * normed)
        scaled = back * gain_ref[...]
        inner = scaled - jnp.mean(scaled, axis=-1, keepdims=True)
        inner = inner - normed * jnp.mean(scaled * normed, axis=-1, keepdims=True)
        grad = cot_ref[span].astype(jnp.float32) + inner * inv_std
        grad_ref[span] = grad
        low = grad.astype(jnp.bfloat16)
        low_ref[span] = low
        d_own[span] = nn(low, w0[...]).astype(jnp.bfloat16)
        d_core[span] = nn(low, w1[...]).astype(jnp.bfloat16)
        d_pair[span, :cols] = nn(low, w2[...]).astype(jnp.bfloat16)
        d_pair[span, cols:] = nn(low, w3[...]).astype(jnp.bfloat16)

    loop(rows, tile)


def turn(resid, cot, backs, gain, weights):
    rows, dim = cot.shape
    cols = weights[0].shape[1]
    return call(
        turn_kernel,
        "turn",
        [
            wide_shape(rows, dim),
            low_shape(rows, dim),
            low_shape(rows, cols),
            low_shape(rows, cols),
            low_shape(rows, 2 * cols),
            wide_shape(1, dim),
        ],
        [VMEM] * 10,
        [],
        2 * rows * dim * dim,
        rows,
        (resid, cot, *backs, gain, *weights),
    )


def out_grads_kernel(low_ref, h0, h1, h2, h3, o_near, o_far):
    cols = h0.shape[1]
    low = low_ref[...]
    o_near[:, :cols] = tn(low, h0[...])
    o_far[:, :cols] = tn(low, h1[...]).astype(jnp.bfloat16)
    o_near[:, cols:] = tn(low, h2[:, :cols])
    o_far[:, cols:] = tn(low, h3[:, cols:]).astype(jnp.bfloat16)


def out_grads(low, heads):
    rows, dim = low.shape
    cols = heads[0].shape[1]
    return call(
        out_grads_kernel,
        "out_grads",
        [wide_shape(dim, 2 * cols), low_shape(dim, 2 * cols)],
        [VMEM] * 5,
        [],
        2 * rows * dim * dim,
        0,
        (low, *heads),
    )


def slot_sum_kernel(near_ref, far_ref, out_ref):
    cols = out_ref.shape[1]
    out_ref[...] = (near_ref[:, cols:] + far_ref[:, cols:].astype(jnp.float32)).astype(out_ref.dtype)


def slot_sum(near, far):
    dim, wide = near.shape
    return call(
        slot_sum_kernel, "slot_sum", [low_shape(dim, wide // 2)], [VMEM] * 2, [], dim * wide, 0, (near, far)
    )[0]


def input_grads_kernel(first, dqkv_ref, w_ref, o0, o1):
    rows, wide = dqkv_ref.shape[1:]
    for rel, out in ((first, o0), (first + 1, o1)):

        def tile(span, rel=rel, out=out):
            out[span] = nt(dqkv_ref[rel, span], w_ref[:, :wide]).astype(out.dtype)

        loop(rows, tile)


def input_grads(dqkv, weights, first):
    rows, cols = dqkv.shape[1:]
    dim = weights.shape[0]
    return call(
        functools.partial(input_grads_kernel, first),
        "input_grads",
        [low_shape(rows, dim)] * 2,
        [VMEM] * 2,
        [],
        4 * rows * dim * cols,
        0,
        (dqkv, weights),
    )


def qkv_grads_kernel(
    info_ref, x0, x1, x2, x3, dqkv_ref, near_ref, far_ref, far_x, small_ref, w_ref, gain_ref, *refs
):
    *outs, all_ref = refs
    wide = dqkv_ref.shape[2]
    cols = wide // 3
    acc = tn(x0[...], dqkv_ref[0]) + tn(x1[...], dqkv_ref[1])
    acc = acc + tn(x2[...], dqkv_ref[2]) + tn(x3[...], dqkv_ref[3])
    all_ref[:, :wide] = acc.astype(all_ref.dtype)
    total = near_ref[:, :cols] + far_ref[:, :cols].astype(jnp.float32)
    total = total + far_x[...].astype(jnp.float32)
    all_ref[:, wide:] = total.astype(all_ref.dtype)
    products = acc * w_ref[:, :wide].astype(jnp.float32)
    low = products.astype(jnp.bfloat16)
    ones = jnp.ones((8, wide), jnp.bfloat16)
    sums = nt(ones, low) + nt(ones, (products - low.astype(jnp.float32)).astype(jnp.bfloat16))
    sums = sums[:1] / gain_ref[...]
    low = sums.astype(jnp.bfloat16)
    row = lax.broadcasted_iota(jnp.int32, small_ref.shape, 0)
    small = jnp.where(row == 0, low, small_ref[...])
    small = jnp.where(row == 8, (sums - low.astype(jnp.float32)).astype(jnp.bfloat16), small)
    if len(outs) == 1:
        outs[0][0, : all_ref.shape[0]] = all_ref[...]
        outs[0][0, all_ref.shape[0] :] = small
        return
    half = info_ref[2 + 4 * x0.shape[0] // BLK]
    count, full = outs[0].shape[:2]
    shard = full - small.shape[0]
    for parity, out in ((half, outs[0]), (1 - half, outs[1])):
        for part in range(count):
            start = pl.multiple_of((2 * part + parity) * shard, shard)
            out[part, :shard] = all_ref[pl.ds(start, shard), :]
            out[part, shard:] = small


def qkv_grads(info, xs, dqkv, near, far, far_x, small, weights, gain, count):
    rows, dim = xs[0].shape
    wide = dqkv.shape[2]
    full = wide + wide // 3
    extra = small.shape[0]
    if count == 1:
        outs = [low_shape(1, dim + extra, full)]
    else:
        outs = [low_shape(count // 2, dim // count + extra, full)] * 2
    return call(
        qkv_grads_kernel,
        "qkv_grads",
        outs,
        [SMEM] + [VMEM] * 11,
        [pltpu.VMEM((dim, full), jnp.bfloat16)],
        8 * rows * dim * wide,
        0,
        (info, *xs, dqkv, near, far, far_x, small, weights, gain),
    )


def fold_kernel(shard, info_ref, a_ref, b_ref, *outs):
    line = info_ref[info_ref.shape[0] - 1]
    for step, out in enumerate(outs):
        part = line ^ step
        total = a_ref[part, :shard].astype(jnp.float32) + b_ref[part, :shard].astype(jnp.float32)
        out[:shard] = total.astype(out.dtype)
        total = a_ref[part, shard:].astype(jnp.float32) + b_ref[part, shard:].astype(jnp.float32)
        half = total.shape[0] // 2
        wide = total[:half] + total[half:]
        low = wide.astype(jnp.bfloat16)
        rest = (wide - low.astype(jnp.float32)).astype(jnp.bfloat16)
        out[shard:] = jnp.concatenate([low, rest], axis=0)


def fold(info, a, b, shard):
    count, full, wide = a.shape
    return call(
        functools.partial(fold_kernel, shard), "fold", [low_shape(full, wide)] * count,
        [SMEM] + [VMEM] * 2, [], a.size, 0, (info, a, b),
    )


def finish_kernel(tok_ref, grad_ref, b0, b1, b2, gain_ref, out_ref):

    def tile(span):
        normed, inv_std = norm_stats(tok_ref[span].astype(jnp.float32))
        back = b0[span].astype(jnp.float32) + b1[span].astype(jnp.float32)
        back = back + b2[span].astype(jnp.float32)
        scaled = back * gain_ref[...]
        inner = scaled - jnp.mean(scaled, axis=-1, keepdims=True)
        inner = inner - normed * jnp.mean(scaled * normed, axis=-1, keepdims=True)
        out_ref[span] = grad_ref[span] + inner * inv_std

    loop(tok_ref.shape[0], tile)


def finish(tokens, grad, backs, gain):
    rows, dim = tokens.shape
    return call(
        finish_kernel,
        "finish",
        [wide_shape(rows, dim)],
        [VMEM] * 6,
        [],
        rows * dim * 20,
        rows,
        (tokens, grad, *backs, gain),
    )[0]


def norm_kernel(t0, t1, gain_ref, o0, o1):
    for src, out in ((t0, o0), (t1, o1)):

        def tile(span, src=src, out=out):
            normed, _ = norm_stats(src[span].astype(jnp.float32))
            out[span] = (normed * gain_ref[...]).astype(out.dtype)

        loop(t0.shape[0], tile)


def norms(blocks, gain):
    rows, dim = blocks[0].shape
    return call(
        norm_kernel,
        "norms",
        [low_shape(rows, dim)] * 2,
        [VMEM] * 3,
        [],
        rows * dim * 20,
        rows,
        (*blocks, gain),
    )


def share_kernel(shard, parts_ref, *outs):
    cols = outs[0].shape[1]
    for at, out in enumerate(outs):
        if out.shape[0] != shard:
            break
        span = slice(at * cols, (at + 1) * cols)
        total = parts_ref[0, :shard, span].astype(jnp.float32)
        for part in range(1, parts_ref.shape[0]):
            total = total + parts_ref[part, :shard, span].astype(jnp.float32)
        out[...] = total
    if parts_ref.shape[1] > shard:
        total = parts_ref[0, shard:].astype(jnp.float32)
        for part in range(1, parts_ref.shape[0]):
            total = total + parts_ref[part, shard:].astype(jnp.float32)
        half = total.shape[0] // 2
        outs[-1][...] = total[:half] + total[half:]


def shares(parts, shard, cols, name):
    count, full, wide = parts.shape
    outs = [wide_shape(shard, cols)] * (wide // cols)
    if full > shard:
        outs.append(wide_shape((full - shard) // 2, wide))
    return call(
        functools.partial(share_kernel, shard),
        name,
        outs,
        [VMEM],
        [],
        count * full * wide,
        0,
        (parts,),
    )


def tail_kernel(count, *refs):
    parts, (q_out, k_out, o_out, mix_ref) = refs[:count], refs[count:]
    shard, cols = q_out.shape
    wide = mix_ref.shape[1]

    def total(rows, span):
        acc = parts[0][rows, span].astype(jnp.float32)
        for part in parts[1:]:
            acc = acc + part[rows, span].astype(jnp.float32)
        return acc

    first = slice(0, shard)
    q_out[...] = total(first, slice(0, cols))
    k_out[...] = total(first, slice(cols, 2 * cols))
    o_out[...] = total(first, slice(3 * cols, 4 * cols)).T
    small = total(slice(shard, shard + 16), slice(0, wide))
    mix_ref[:8] = small[:8] + small[8:]
    value = total(first, slice(2 * cols, 3 * cols))
    height = shard // 4
    for at in range(4):
        mix_ref[8:, at * cols : (at + 1) * cols] = value[at * height : (at + 1) * height]


def tail_shares(parts, shard, cols):
    full, wide = parts[0].shape
    return call(
        functools.partial(tail_kernel, len(parts)),
        "tail_shares",
        [
            wide_shape(shard, cols),
            wide_shape(shard, cols),
            wide_shape(cols, shard),
            wide_shape(8 + shard // 4, wide),
        ],
        [VMEM] * len(parts),
        [],
        len(parts) * full * wide,
        0,
        tuple(parts),
    )


def meet_kernel(info_ref, own_ref, peer_ref, out_ref):
    out_ref[:8] = own_ref[:8] + peer_ref[:8]
    out_ref[8:] = jnp.where(info_ref[0] < 2, own_ref[8:], peer_ref[8:])


def meet(info, own, peer):
    return call(
        meet_kernel, "meet", [wide_shape(*own.shape)], [SMEM] + [VMEM] * 2, [], own.size, 0, (info, own, peer)
    )[0]


def last_kernel(info_ref, own_ref, peer_ref, value_ref, gain_one, gain_two, rms_ref):
    dim = own_ref.shape[1]
    cols = dim // 4
    total = own_ref[:8] + peer_ref[:8]
    gain_one[...] = total[0:1]
    gain_two[...] = total[1:2]
    sums = jnp.sum(total, axis=1, keepdims=True)
    roots = jnp.sqrt(sums / (sums[5:6] * dim))
    lane = lax.broadcasted_iota(jnp.int32, rms_ref.shape, 1)
    rms_ref[...] = jnp.where(lane == 0, roots[2:3], jnp.where(lane == 1, roots[3:4], roots[4:5]))
    even = info_ref[0] % 2 == 0
    own, peer = own_ref[8:], peer_ref[8:]
    lower, upper = jnp.where(even, own, peer), jnp.where(even, peer, own)
    height = own.shape[0]
    for at in range(4):
        rows, span = slice(at * height, (at + 1) * height), slice(at * cols, (at + 1) * cols)
        value_ref[rows, :cols] = lower[:, span]
        value_ref[rows, cols:] = upper[:, span]


def last(info, own, peer):
    dim = own.shape[1]
    return call(
        last_kernel,
        "last",
        [wide_shape(4 * (own.shape[0] - 8), dim // 2), wide_shape(1, dim), wide_shape(1, dim), wide_shape(1, LANES)],
        [SMEM] + [VMEM] * 2,
        [],
        own.size,
        0,
        (info, own, peer),
    )


def output_kernel(info_ref, resid_ref, b0, b1, b2, attn_sq, gain_two, out_ref, small_ref, *sums):
    rows, dim = resid_ref.shape
    final_sum, mlp_sum = sums
    final_sum[...] = jnp.zeros_like(final_sum)
    mlp_sum[...] = jnp.zeros_like(mlp_sum)

    def tile(span):
        valid = valid_rows(info_ref, rows, span.start, BLK)
        mlp_out = b0[span].astype(jnp.float32) + b1[span].astype(jnp.float32)
        mlp_out = mlp_out + b2[span].astype(jnp.float32)
        final = resid_ref[span] + mlp_out
        out_ref[span] = final.astype(out_ref.dtype)
        final_sum[...] += row_sum(final * final * valid)
        mlp_sum[...] += row_sum(mlp_out * mlp_out * valid)

    loop(rows, tile)
    count = jnp.clip(info_ref[1] - info_ref[0] * rows, 0, rows).astype(jnp.float32)
    lane = lax.broadcasted_iota(jnp.int32, (1, dim), 1)
    counts = jnp.where(lane == 0, count, 0.0)
    row = lax.broadcasted_iota(jnp.int32, (8, dim), 0)
    wide = jnp.zeros((8, dim), jnp.float32)
    values = (jnp.zeros_like(gain_two), gain_two[...], final_sum[...], attn_sq[...], mlp_sum[...], counts)
    for at, value in enumerate(values):
        wide = jnp.where(row == at, value, wide)
    low = wide.astype(jnp.bfloat16)
    small_ref[...] = jnp.concatenate([low, (wide - low.astype(jnp.float32)).astype(jnp.bfloat16)], axis=0)


def output(info, resid, parts, sums):
    rows, dim = resid.shape
    return call(
        output_kernel,
        "output",
        [low_shape(rows, dim), low_shape(16, dim)],
        [SMEM] + [VMEM] * 6,
        [pltpu.VMEM((1, dim), jnp.float32)] * 2,
        rows * dim * 10,
        0,
        (info, resid, *parts, *sums),
    )


def pack_early_kernel(info_ref, wq, wk, wv, wo, out_ref):
    cols = wq.shape[1]
    even = info_ref[0] % 2 == 0
    fresh = jnp.where(even, wv[:, :cols], wv[:, cols : 2 * cols])
    turned = wo[...].T
    for part in range(out_ref.shape[0]):
        for at, value in enumerate((wq[...], wk[...], fresh, turned)):
            out_ref[part, :, at * cols : (at + 1) * cols] = value


def pack_early(info, copies, wq, wk, wv, wo):
    shard, cols = wq.shape
    return call(
        pack_early_kernel, "pack_early", [low_shape(copies, shard, 4 * cols)],
        [SMEM] + [VMEM] * 4, [], shard * cols, 0, (info, wq, wk, wv, wo), 60,
    )[0]


X_SWAP = [(0, 2), (1, 3), (2, 0), (3, 1)]
CORE_SWAP = [(0, 1), (1, 0), (2, 3), (3, 2)]


def swap_x(v):
    return lax.ppermute(v, "tensor", X_SWAP)


def swap_core(v):
    return lax.ppermute(v, "tensor", CORE_SWAP)


def tied(value, *others):
    return lax.optimization_barrier((value, *others))[0]


def plus(a, b):
    return (a.astype(jnp.float32) + b.astype(jnp.float32)).astype(jnp.bfloat16)


def body(
    tokens,
    first_values,
    pieces,
    lengths,
    w_query,
    w_key,
    w_value,
    w_out,
    w_up,
    w_down,
    gain_attn,
    gain_mlp,
    cotangent,
):
    dp_size = lax.axis_size("dp")
    rank = lax.axis_index("tensor")
    core = rank % 2
    rows, dim = tokens.shape
    shard, cols = w_query.shape
    up_cols = w_up.shape[1]
    parity = lax.axis_index("dp") % 2
    info = jnp.concatenate(
        [
            rank[None].astype(jnp.int32),
            lengths,
            pieces[::BLK],
            parity[None].astype(jnp.int32),
            (lax.axis_index("dp") // 2)[None].astype(jnp.int32),
        ]
    )
    gain_one, gain_two = gain_attn[None], gain_mlp[None]
    pairs = [(i, i ^ 1) for i in range(dp_size)]
    lines = [list(range(first, dp_size, 2)) for first in range(2)]

    def gather_line(v):
        return lax.all_to_all(v, "dp", 0, 0, axis_index_groups=lines)

    def swap_pair(v):
        return lax.ppermute(v, "dp", pairs)

    def in_order(mine, other):
        lower = jnp.where(parity == 0, mine, other)
        upper = jnp.where(parity == 0, other, mine)
        return jnp.stack([lower, upper], axis=1).reshape(dim, -1)

    def pieces_of(mine, other):
        if shard % 16 == 0:
            return (mine, other)
        return (in_order(mine, other)[None],)

    early = pack_early(rank[None].astype(jnp.int32), dp_size // 2, w_query, w_key, w_value, w_out)
    early_mine = gather_line(early)
    tok_x = swap_x(tokens)
    tok_core = swap_core(tokens)
    xs_near = norms((tokens, tok_core), gain_one)
    early_other = swap_pair(early_mine)
    tok_diag = swap_core(tok_x)
    late = tied(jnp.concatenate([w_up, w_down.T], axis=1), tok_core)
    late_all = lax.all_gather(late, "dp", axis=0, tiled=True)
    first_x = lax.ppermute(first_values, "tensor", [(0, 2), (1, 3)])
    firsts = (first_values, swap_core(first_values), first_x, swap_core(first_x))
    xs = (*xs_near, *norms((tok_x, tok_diag), gain_one))
    early_all, out_own, *prepared, o_first, lse_first = attend_first(
        info, xs, pieces_of(early_mine, early_other), firsts, cols
    )

    out_x = swap_x(out_own)
    cot_x = swap_x(tied(cotangent, first_x))
    h_own, h_core, h_pair, lse = attend_rest(info, *prepared[:3], o_first, lse_first)
    h_pair, h_core = lax.optimization_barrier((h_pair, h_core, cot_x, out_x))[:2]
    cot_core = swap_core(cotangent)
    cot_diag = swap_core(cot_x)
    outs = (out_own, swap_core(out_own), out_x, swap_core(out_x))

    from_x = swap_x(h_pair)
    heads_mine = (h_own, swap_core(h_core), from_x, swap_core(from_x))
    resid, mlp_in, attn_sq = middle(
        info, tokens, heads_mine, outs, gain_two
    )
    in_x = swap_x(mlp_in)
    in_core = swap_core(mlp_in)
    hid_a, dup_a, back_own, back_core, out_0, out_1 = mlp_near(
        (mlp_in, in_core), (cotangent, cot_core), late_all
    )
    back_1 = swap_core(back_core)
    out_near = swap_core(out_1)
    in_far = tied(in_x, back_own)
    in_diag = swap_core(in_far)
    hid_x, dup_x, back_x = mlp_far(in_far, cot_x, late_all)
    hid_d, dup_d, back_diag = mlp_far(tied(in_diag, back_x), cot_diag, late_all)
    back_far = plus(back_x, swap_core(back_diag))
    back_2 = swap_x(back_far)
    grads_mlp, out_2, out_3 = mlp_grads(
        (mlp_in, in_core, in_x, in_diag),
        (cotangent, cot_core, cot_x, cot_diag),
        (hid_a, hid_x, tied(hid_d, back_far)), (dup_a, dup_x, dup_d), late_all, up_cols,
    )
    out_sum = plus(out_2, swap_core(out_3))

    resid_grad, resid_low, d_own, d_core, d_pair, gain_two_sum = turn(
        resid, cotangent, (back_own, back_1, back_2), gain_two, outs
    )
    d_x = swap_x(d_pair)
    mlp_share = lax.psum_scatter(tied(grads_mlp, resid_low), "dp", scatter_dimension=0, tiled=True)
    grads_heads = (d_own, swap_core(d_core), d_x, swap_core(d_x))
    near, far = out_grads(tied(resid_low, out_sum), heads_mine)
    far = swap_core(far)
    dqkv, dv_own, dv_core, dv_pair = attend_back(
        info, prepared, grads_heads, (h_own, h_core, h_pair), lse
    )
    out_from_x = swap_x(tied(out_sum, d_x))
    near_x = swap_x(tied(slot_sum(near, far), d_x))
    dqkv, dv_pair = lax.optimization_barrier((dqkv, dv_pair, out_from_x, near_x))[:2]

    first_from_x = lax.ppermute(dv_pair, "tensor", [(2, 0), (3, 1)])
    final, small = output(info, resid, (out_0, out_near, out_from_x), (attn_sq, gain_two_sum))
    b_2, b_3 = input_grads(tied(dqkv, small), early_all, 2)
    joined = shard % 16 == 0 and dp_size <= 8
    tail = qkv_grads(
        info, xs, tied(dqkv, b_3), near, far, near_x, small, early_all, gain_one, dp_size if joined else 1
    )
    if joined:
        tail_pair = swap_pair(tail[1])
    tail_first = tail[0]
    plus_far = plus(b_2, swap_core(b_3))
    b_from_x = swap_x(plus_far)

    b_0, b_1 = input_grads(tied(dqkv, plus_far), early_all, 0)
    b_from_core = swap_core(b_1)
    if joined:
        folded = fold(info, tied(tail_first, plus_far, b_0), tail_pair, shard)
    first_a = jnp.where(rank < 2, first_from_x[:, :cols], dv_own)
    first_b = swap_core(jnp.where(rank < 2, first_from_x[:, cols:], dv_core))
    first_grad = jnp.where(
        core == 0,
        jnp.concatenate([first_a, first_b], axis=1),
        jnp.concatenate([first_b, first_a], axis=1),
    ).astype(jnp.float32)
    token_grad = finish(tokens, resid_grad, (b_0, b_from_core, b_from_x), gain_one)
    grad_up, grad_down_t = shares(mlp_share[None], shard, up_cols, "mlp_shares")
    if joined:
        tail_parts = [folded[0]] + [
            lax.ppermute(folded[step], "dp", [(i, i ^ (2 * step)) for i in range(dp_size)])
            for step in range(1, dp_size // 2)
        ]
        tail_parts[0] = tied(tail_parts[0], token_grad, grad_up, first_grad)
        grad_q, grad_k, grad_out, mix = tail_shares(tail_parts, shard, cols)
        mix = meet(info, mix, swap_x(mix))
        value_share, gain_one_sum, gain_two_total, rms = last(info, mix, swap_core(mix))
        gain_one_sum, gain_two_total = gain_one_sum.reshape(dim), gain_two_total.reshape(dim)
        rms = rms[0, :3]
    else:
        small = tail_first[0, dim:].astype(jnp.float32)
        total = lax.psum(small[:8] + small[8:], ("dp", "tensor"))
        tail_all = lax.all_to_all(tail_first[0, :dim].reshape(dp_size, shard, 4 * cols), "dp", 0, 0)
        total_grads = jnp.sum(tail_all.astype(jnp.float32), axis=0)
        grad_q, grad_k = total_grads[:, :cols], total_grads[:, cols : 2 * cols]
        grad_out = total_grads[:, 3 * cols :].T
        value_own = total_grads[:, 2 * cols : 3 * cols]
        value_here = jnp.where(rank < 2, value_own, swap_x(value_own))
        value_peer = swap_core(value_here)
        value_share = jnp.where(
            core == 0,
            jnp.concatenate([value_here, value_peer], axis=1),
            jnp.concatenate([value_peer, value_here], axis=1),
        )
        sums = jnp.sum(total, axis=1)
        rms = jnp.sqrt(sums[2:5] / (sums[5] * dim))
        gain_one_sum, gain_two_total = total[0], total[1]
    return (
        final,
        token_grad,
        first_grad,
        grad_q,
        grad_k,
        value_share,
        grad_out,
        grad_up,
        grad_down_t.T,
        gain_one_sum,
        gain_two_total,
        rms,
    )


def solution(mesh):
    in_specs = (
        P(("dp", "tensor"), None),
        P(("dp", "tensor"), None),
        P("dp"),
        P("dp"),
        P("dp", "tensor"),
        P("dp", "tensor"),
        P("dp", None),
        P("tensor", "dp"),
        P("dp", "tensor"),
        P("tensor", "dp"),
        P(),
        P(),
        P(("dp", "tensor"), None),
    )
    out_specs = (
        P(("dp", "tensor"), None),
        P(("dp", "tensor"), None),
        P(("dp", "tensor"), None),
        P("dp", "tensor"),
        P("dp", "tensor"),
        P("dp", None),
        P("tensor", "dp"),
        P("dp", "tensor"),
        P("tensor", "dp"),
        P(),
        P(),
        P(),
    )
    return jax.shard_map(body, mesh=mesh, in_specs=in_specs, out_specs=out_specs, check_vma=False)
```
